128 devices in a mesh: seg: 8 (over x, core), seq: 16 (over z, y).
Axes of the slice: x: 4, y: 4, z: 4, core: 2. Of those that a mesh axis runs over, the one named last changes fastest.
Arguments:
- queries: bfloat16 [16384, 4096], P(('seg', 'seq')), may hold values from -6 to 6
- keys: bfloat16 [16384, 4096], P(('seg', 'seq')), may hold values from -6 to 6
- values: bfloat16 [16384, 4096], P(('seg', 'seq')), may hold values from -6 to 6
- prior_keys: bfloat16 [2048, 4096], P('seq'), may hold values from -6 to 6
- prior_values: bfloat16 [2048, 4096], P('seq'), may hold values from -6 to 6
- conv_keys: bfloat16 [32, 512, 128], P('seq'), may hold values from -0.5 to 0.5
- conv_values: bfloat16 [32, 512, 128], P('seq'), may hold values from -0.5 to 0.5
- doc_starts: int32 [8], replicated, may hold values from 0 to 4095, as said below
Outputs:
- attended: bfloat16 [16384, 4096], P(('seg', 'seq'))
- compressed_keys: bfloat16 [4096, 4096], P('seg', 'seq')
- compressed_values: bfloat16 [4096, 4096], P('seg', 'seq')
- recon_loss: float32 [], replicated
- grad_conv_keys: float32 [32, 512, 128], P('seq')
- grad_conv_values: float32 [32, 512, 128], P('seq')
The draws below stay inside these ranges and needn't reach their ends.
Inputs may be any that keep to these rules, and one draw needn't show every extreme that they name: `doc_starts`: entry g is the offset within segment g at which a document starts; an entry of 2048 or more means segment g continues the document before it. Entry 0 is 4095, entries 1 and 6 are 2048 or more, entry 7 lies from 1024 to 2047.
All inputs are finite; a program needn't handle non-finite values.
Results may differ from the reference program's by a relative error of at most 0.015.
Values may be sent and summed in bfloat16 or wider, within the bound.
A program may use at most 64 MiB of HBM per device.

```python
import math
import jax
import jax.numpy as jnp
from jax import lax

H = 32
DH = 128
RATE = 4
SEG_LEN = 2048
COMP_ROWS = 512
TOKENS = 16384
N_SEG = 8


def paired_rows(key):
    seeds = jax.random.split(jax.random.fold_in(key, 101), 2)
    shape = (TOKENS, H * DH)
    base_query = jnp.clip(jax.random.normal(seeds[0], shape, jnp.float32), -6.0, 6.0)
    base_key = jnp.clip(jax.random.normal(seeds[1], shape, jnp.float32), -6.0, 6.0)
    return (base_query, base_key)


def draw_queries(key, part):
    return paired_rows(key)[0].astype(jnp.bfloat16)


def draw_keys(key, part):
    return paired_rows(key)[1].astype(jnp.bfloat16)


def conv_draw(key, salt):
    inner_key = jax.random.fold_in(key, salt)
    shape = (H, RATE * DH, DH)
    spread = 0.5 / math.sqrt(RATE * DH)
    noise = jnp.clip(jax.random.normal(inner_key, shape, jnp.float32), -6.0, 6.0) * spread
    diagonal = (jnp.arange(RATE * DH)[:, None] % DH == jnp.arange(DH)[None, :]).astype(jnp.float32)
    return (0.25 * diagonal[None, :, :] + noise).astype(jnp.bfloat16)


def draw_conv_keys(key, part):
    return conv_draw(key, 211)


def draw_conv_values(key, part):
    return conv_draw(key, 307)


def draw_doc_starts(key, part):
    seeds = jax.random.split(jax.random.fold_in(key, 401), 4)
    segment_count = TOKENS // SEG_LEN
    general = jax.random.randint(seeds[0], (segment_count,), 0, 2 * SEG_LEN)
    continuing = jax.random.randint(seeds[1], (segment_count,), SEG_LEN, 2 * SEG_LEN)
    middle = jax.random.randint(seeds[2], (segment_count,), SEG_LEN // 2, SEG_LEN)
    early = jax.random.randint(seeds[3], (segment_count,), 0, SEG_LEN // 4)
    place = jnp.arange(segment_count)
    result = jnp.where(place == segment_count - 3, early, general)
    result = jnp.where(place == segment_count - 1, middle, result)
    result = jnp.where((place < 2) | (place == segment_count - 2), continuing, result)
    result = jnp.where(place == 0, 2 * SEG_LEN - 1, result)
    return result.astype(jnp.int32)


def steps_of(own_key, dims, cuts, low, largest):
    factor_of = 1.0
    for position, blocks in cuts:
        draws = jax.random.uniform(jax.random.fold_in(jax.random.fold_in(own_key, 6), position), (blocks,), jnp.float32, low / len(cuts), largest / len(cuts))
        factor_of = factor_of * jnp.repeat(jnp.exp(draws), dims[position] // blocks).reshape((-1,) + (1,) * (len(dims) - 1 - position))
    return factor_of


def normal_values(rng, extent, scale, limit, cuts=(), kind=jnp.bfloat16):
    factor_of = steps_of(rng, extent, cuts, -0.22, 0.18) if cuts else 1.0
    values = jax.random.normal(rng, extent, jnp.float32) * scale * factor_of
    return jnp.minimum(jnp.maximum(values, -limit), limit).astype(kind)


def setup_inputs(seed: int = 0) -> dict:
    streams_of = jax.random.split(jax.random.key(seed), 9)
    queries = draw_queries(jax.random.fold_in(streams_of[8], 71), 0)
    keys = draw_keys(jax.random.fold_in(streams_of[8], 71), 0)
    values = normal_values(streams_of[2], (TOKENS, H * DH), 1.0, 6.0, ((0, 128),))
    prior_keys = normal_values(streams_of[3], (SEG_LEN, H * DH), 1.0, 6.0, ((0, 16),))
    prior_values = normal_values(streams_of[4], (SEG_LEN, H * DH), 1.0, 6.0, ((0, 16),))
    conv_keys = draw_conv_keys(jax.random.fold_in(streams_of[8], 71), 0)
    conv_values = draw_conv_values(jax.random.fold_in(streams_of[8], 71), 0)
    doc_starts = draw_doc_starts(jax.random.fold_in(streams_of[8], 71), 0)
    return dict(queries=queries, keys=keys, values=values, prior_keys=prior_keys, prior_values=prior_values, conv_keys=conv_keys, conv_values=conv_values, doc_starts=doc_starts)


def visible_mask(group_index, doc_starts, query_place, column):
    comp_part = column < COMP_ROWS
    fine_part = (column >= COMP_ROWS) & (column < COMP_ROWS + SEG_LEN)
    own_part = column >= COMP_ROWS + SEG_LEN
    key_place = jnp.where(comp_part, RATE * column, jnp.where(fine_part, column - COMP_ROWS, column - COMP_ROWS - SEG_LEN))
    start_now = doc_starts[group_index]
    start_prev = jnp.where(group_index >= 1, doc_starts[jnp.maximum(group_index - 1, 0)], SEG_LEN)
    start_back = jnp.where(group_index >= 2, doc_starts[jnp.maximum(group_index - 2, 0)], SEG_LEN)
    lead_prev = jnp.where(start_prev < SEG_LEN, start_prev, 0)
    lead_back = jnp.where(start_back < SEG_LEN, start_back, 0)
    comp_open = (group_index >= 1) & (start_prev >= SEG_LEN)
    before_doc = query_place < start_now
    seen_comp = comp_part & comp_open & before_doc & (key_place >= lead_back)
    seen_fine = fine_part & before_doc & (key_place >= lead_prev)
    seen_own = own_part & (key_place <= query_place) & ((key_place >= start_now) | before_doc)
    return seen_comp | seen_fine | seen_own

def reference(queries, keys, values, prior_keys, prior_values, conv_keys, conv_values, doc_starts):
    score_scale = 1.0 / math.sqrt(DH)

    def by_head(flat_array):
        return flat_array.reshape(-1, SEG_LEN, H, DH).transpose(0, 2, 1, 3)
    query_heads = by_head(queries)
    key_heads = by_head(keys)
    value_heads = by_head(values)
    fine_keys = jnp.concatenate((by_head(prior_keys), key_heads[:-1]), axis=0)
    fine_values = jnp.concatenate((by_head(prior_values), value_heads[:-1]), axis=0)

    def compress(source_rows, weight):
        windows = source_rows.reshape(N_SEG, H, COMP_ROWS, RATE * DH).astype(jnp.float32)
        return jnp.einsum('ghcw,hwd->ghcd', windows, weight.astype(jnp.float32)).astype(jnp.bfloat16)
    comp_keys = compress(fine_keys, conv_keys)
    comp_values = compress(fine_values, conv_values)
    blank_rows = jnp.zeros((1, H, COMP_ROWS, DH), jnp.bfloat16)
    memory_keys = jnp.concatenate((blank_rows, comp_keys[:-1]), axis=0)
    memory_values = jnp.concatenate((blank_rows, comp_values[:-1]), axis=0)
    column = jnp.arange(COMP_ROWS + 2 * SEG_LEN, dtype=jnp.int32)[None, :]
    query_place = jnp.arange(SEG_LEN, dtype=jnp.int32)[:, None]

    def main_item(flat_index):
        group_index = flat_index // H
        head_index = flat_index % H
        query_rows = query_heads[group_index, head_index]
        key_rows = jnp.concatenate((memory_keys[group_index, head_index], fine_keys[group_index, head_index], key_heads[group_index, head_index]), axis=0)
        value_rows = jnp.concatenate((memory_values[group_index, head_index], fine_values[group_index, head_index], value_heads[group_index, head_index]), axis=0)
        visible = visible_mask(group_index, doc_starts, query_place, column)
        scores = jnp.dot(query_rows, key_rows.T, preferred_element_type=jnp.float32) * score_scale
        row_top = lax.optimization_barrier(jnp.max(jnp.where(visible, scores, -jnp.inf), axis=1, keepdims=True))
        weights = jnp.exp(jnp.where(visible, scores - row_top, -jnp.inf))
        row_total = lax.optimization_barrier(jnp.sum(weights, axis=1, keepdims=True))
        mixed_rows = jnp.dot(weights.astype(jnp.bfloat16), value_rows, preferred_element_type=jnp.float32) / row_total
        return mixed_rows.astype(jnp.bfloat16)
    attended = lax.map(main_item, jnp.arange(N_SEG * H, dtype=jnp.int32))
    attended = attended.reshape(N_SEG, H, SEG_LEN, DH).transpose(0, 2, 1, 3).reshape(TOKENS, H * DH)

    def recon_item(flat_index):
        group_index = flat_index // H
        head_index = flat_index % H
        query_rows = query_heads[group_index, head_index]
        fine_k = fine_keys[group_index, head_index]
        fine_v = fine_values[group_index, head_index]
        comp_k = comp_keys[group_index, head_index]
        comp_v = comp_values[group_index, head_index]
        fine_scores = jnp.dot(query_rows, fine_k.T, preferred_element_type=jnp.float32) * score_scale
        fine_exp = jnp.exp(fine_scores - lax.optimization_barrier(jnp.max(fine_scores, axis=1, keepdims=True)))
        fine_total = lax.optimization_barrier(jnp.sum(fine_exp, axis=1, keepdims=True))
        recon_fine = jnp.dot(fine_exp.astype(jnp.bfloat16), fine_v, preferred_element_type=jnp.float32) / fine_total
        comp_scores = jnp.dot(query_rows, comp_k.T, preferred_element_type=jnp.float32) * score_scale
        comp_exp = jnp.exp(comp_scores - lax.optimization_barrier(jnp.max(comp_scores, axis=1, keepdims=True)))
        comp_total = lax.optimization_barrier(jnp.sum(comp_exp, axis=1, keepdims=True))
        comp_weights = comp_exp.astype(jnp.bfloat16)
        recon_comp = jnp.dot(comp_weights, comp_v, preferred_element_type=jnp.float32) / comp_total
        differ = recon_fine - recon_comp
        out_grad = (-2.0 * differ / comp_total).astype(jnp.bfloat16)
        value_grad = jnp.dot(comp_weights.T, out_grad, preferred_element_type=jnp.float32).astype(jnp.bfloat16)
        inner_grad = jnp.dot(out_grad, comp_v.T, preferred_element_type=jnp.float32)
        row_offset = lax.optimization_barrier(jnp.sum(out_grad.astype(jnp.float32) * recon_comp, axis=1, keepdims=True))
        score_grad = (comp_exp * (inner_grad - row_offset)).astype(jnp.bfloat16)
        key_grad = (jnp.dot(score_grad.T, query_rows, preferred_element_type=jnp.float32) * score_scale).astype(jnp.bfloat16)
        windows_k = fine_k.reshape(COMP_ROWS, RATE * DH)
        windows_v = fine_v.reshape(COMP_ROWS, RATE * DH)
        grad_k = jnp.dot(windows_k.T, key_grad, preferred_element_type=jnp.float32)
        grad_v = jnp.dot(windows_v.T, value_grad, preferred_element_type=jnp.float32)
        return (jnp.sum(differ * differ), grad_k, grad_v)
    losses, grad_k, grad_v = lax.map(recon_item, jnp.arange(N_SEG * H, dtype=jnp.int32))
    grad_conv_keys = lax.optimization_barrier(jnp.sum(grad_k.reshape(N_SEG, H, RATE * DH, DH), axis=0))
    grad_conv_values = lax.optimization_barrier(jnp.sum(grad_v.reshape(N_SEG, H, RATE * DH, DH), axis=0))
    recon_loss = jnp.sum(losses) / (N_SEG * SEG_LEN)
    compressed_keys = comp_keys.transpose(0, 2, 1, 3).reshape(N_SEG * COMP_ROWS, H * DH)
    compressed_values = comp_values.transpose(0, 2, 1, 3).reshape(N_SEG * COMP_ROWS, H * DH)
    return (attended, compressed_keys, compressed_values, recon_loss, grad_conv_keys, grad_conv_values)
```

```python
import functools
import math

import jax
import jax.numpy as jnp
from jax import lax
from jax.experimental import pallas as pl
from jax.experimental.pallas import tpu as pltpu
from jax.sharding import Mesh
from jax.sharding import PartitionSpec as P

RATE = 4
SEQ = ("seq_0", "seq_1")
SEG = ("seg_0", "seg_1")
SEG_SEQ = ("seg_0", "seg_1", "seq_0", "seq_1")
NEG = -1e30
F32 = jnp.float32
BF16 = jnp.bfloat16
BQ = 256
DH = 128
NT = (((1,), (1,)), ((), ()))
NN = (((1,), (0,)), ((), ()))
TN = (((0,), (0,)), ((), ()))


def mm(a, b, dims):
    return lax.dot_general(a, b, dims, preferred_element_type=F32)


def recon_kernel(sc, q, fk, fv, wk, wv, ck, cv, gk, gv, loss, acc_b, m_b, l_b,
                 wink, winv, vab, vg, kg, cvt, lacc):
    rows = q.shape[0]
    heads = q.shape[1] // DH
    crows = rows // RATE
    s1 = sc[1]
    scale = 1.0 / math.sqrt(DH)
    c2 = scale * math.log2(math.e)
    r_i = lax.broadcasted_iota(jnp.int32, (128, 128), 0)
    c_i = lax.broadcasted_iota(jnp.int32, (128, 128), 1)
    perm = (c_i == RATE * (r_i % 32) + r_i // 32).astype(BF16)

    def window(b, carry):
        at = pl.ds(pl.multiple_of(b * 128, 128), 128)
        to = pl.ds(pl.multiple_of(b * 32, 32), 32)
        wa = mm(perm, fk[at, :], NN).astype(BF16)
        wb = mm(perm, fv[at, :], NN).astype(BF16)
        for r in range(RATE):
            wink[r, to, :] = wa[32 * r:32 * r + 32]
            winv[r, to, :] = wb[32 * r:32 * r + 32]
        return carry

    lax.fori_loop(0, rows // 128, window, 0)
    for h in range(heads):
        cols = slice(h * DH, (h + 1) * DH)
        for win, w, out in ((wink, wk, ck), (winv, wv, cv)):
            total = mm(win[0, :, cols], w[h, 0:DH, :], NN)
            for r in range(1, RATE):
                total += mm(win[r, :, cols], w[h, r * DH:(r + 1) * DH, :], NN)
            out[:, cols] = total.astype(BF16)
        cvt[h] = cv[:, cols].astype(F32).T.astype(BF16)
        row = lax.broadcasted_iota(jnp.int32, (rows, DH), 0)
        val = fv[:, cols]
        zero = jnp.zeros_like(val)
        vab[h, :, 0:DH] = jnp.where(row < s1, val, zero)
        vab[h, :, DH:] = jnp.where(row < s1, zero, val)
    vg[...] = jnp.zeros_like(vg)
    kg[...] = jnp.zeros_like(kg)
    lacc[...] = jnp.zeros_like(lacc)

    def block(i, carry):
        at = pl.ds(pl.multiple_of(i * BQ, BQ), BQ)
        tops = []
        for h in range(heads):
            cols = slice(h * DH, (h + 1) * DH)
            qb = q[at, cols]
            is_b = lax.broadcasted_iota(jnp.int32, (1, rows), 1) >= s1
            s = mm(qb, fk[:, cols], NT)
            m_all = jnp.max(s, axis=1, keepdims=True)
            m_tail = jnp.max(jnp.where(is_b, s, NEG), axis=1, keepdims=True)
            p = jnp.exp2((s - jnp.where(is_b, m_tail, m_all)) * c2)
            l_all = jnp.sum(p, axis=1, keepdims=True)
            l_tail = jnp.sum(jnp.where(is_b, p, 0.0), axis=1, keepdims=True)
            u = mm(p.astype(BF16), vab[h], NN)
            u_tail = u[:, DH:]
            w_tail = jnp.exp2((m_tail - m_all) * c2)
            fine = (u[:, :DH] + w_tail * u_tail) / ((l_all - l_tail) + w_tail * l_tail)
            acc_b[at, cols] = u_tail
            tops.append((m_tail, l_tail))
            st = mm(ck[:, cols], qb, NT)
            mc = jnp.max(st, axis=0, keepdims=True)
            pt = jnp.exp2((st - mc) * c2)
            lc = jnp.sum(pt, axis=0, keepdims=True)
            ptb = pt.astype(BF16)
            rc = mm(cvt[h], ptb, NN) / lc
            differ = fine.T - rc
            lacc[...] += differ * differ
            og = (-2.0 * differ / lc).astype(BF16)
            vg[h] += mm(ptb, og, NT)
            inner = mm(cv[:, cols], og, NN)
            offset = jnp.sum(og.astype(F32) * rc, axis=0, keepdims=True)
            sg = (pt * (inner - offset)).astype(BF16)
            kg[h] += mm(sg, qb, NN)
        half = lax.broadcasted_iota(jnp.int32, (BQ, DH), 1) < DH // 2
        m_b[at, :] = jnp.where(half, tops[0][0], tops[1][0])
        l_b[at, :] = jnp.where(half, tops[0][1], tops[1][1])
        return carry

    lax.fori_loop(0, rows // BQ, block, 0)
    loss[...] = jnp.full(loss.shape, jnp.sum(lacc[...]), F32)
    for h in range(heads):
        cols = slice(h * DH, (h + 1) * DH)
        kgb = (kg[h] * scale).astype(BF16)
        vgb = vg[h].astype(BF16)
        for r in range(RATE):
            gk[h, r * DH:(r + 1) * DH, :] = mm(wink[r, :, cols], kgb, TN).astype(BF16)
            gv[h, r * DH:(r + 1) * DH, :] = mm(winv[r, :, cols], vgb, TN).astype(BF16)


def attend_kernel(sc, q, k, v, mk, mv, acc_b, m_b, l_b, out):
    rows = q.shape[0]
    heads = q.shape[1] // DH
    crows = rows // RATE
    b0 = sc[0]
    lead = sc[2]
    c2 = math.log2(math.e) / math.sqrt(DH)
    for i in range(rows // BQ):
        lo, hi = i * BQ, (i + 1) * BQ
        for h in range(heads):
            cols = slice(h * DH, (h + 1) * DH)
            qb = q[lo:hi, cols]
            place = lax.broadcasted_iota(jnp.int32, (BQ, 1), 0) + lo
            before = place < b0
            first = jnp.where(before, 0, b0)
            s = mm(qb, k[0:hi, cols], NT)
            at = lax.broadcasted_iota(jnp.int32, (BQ, hi), 1)
            s = jnp.where(at >= first, s, NEG)
            tail = s[:, lo:hi]
            tri = (lax.broadcasted_iota(jnp.int32, (BQ, BQ), 1)
                   <= lax.broadcasted_iota(jnp.int32, (BQ, BQ), 0))
            tail = jnp.where(tri, tail, NEG)
            if i:
                s = jnp.concatenate((s[:, :lo], tail), axis=1)
            else:
                s = tail
            sm = mm(qb, mk[:, cols], NT)
            jm = lax.broadcasted_iota(jnp.int32, (BQ, crows), 1)
            sm = jnp.where(RATE * jm >= jnp.where(before, lead, RATE * crows), sm, NEG)
            spot = h * (DH // 2)
            m_f = jnp.where(before, m_b[lo:hi, spot:spot + 1], NEG)
            top = jnp.maximum(jnp.max(s, axis=1, keepdims=True), jnp.max(sm, axis=1, keepdims=True))
            top = jnp.maximum(top, m_f)
            p = jnp.exp2((s - top) * c2)
            pm = jnp.exp2((sm - top) * c2)
            wf = jnp.exp2((m_f - top) * c2)
            total = (jnp.sum(p, axis=1, keepdims=True) + jnp.sum(pm, axis=1, keepdims=True)
                     + wf * l_b[lo:hi, spot:spot + 1])
            acc = mm(p.astype(BF16), v[0:hi, cols], NN) + mm(pm.astype(BF16), mv[:, cols], NN)
            acc += wf * acc_b[lo:hi, cols]
            out[lo:hi, cols] = (acc / total).astype(BF16)


def shifted(block, axis, distance):
    count = lax.axis_size(axis)
    return lax.ppermute(block, axis, [(i, i + distance) for i in range(count - distance)])


def pick_entry(small_table, wanted):
    return jnp.sum(jnp.where(jnp.arange(small_table.shape[0]) == wanted, small_table, 0))


def vmem(n):
    return [pl.BlockSpec(memory_space=pltpu.VMEM)] * n


SMEM = pl.BlockSpec(memory_space=pltpu.SMEM)


def on_device(queries, keys, values, prior_keys, prior_values, conv_keys, conv_values, doc_starts):
    seq_count = lax.axis_size(SEQ)
    group = lax.axis_index(SEG)
    rows = queries.shape[0] * seq_count
    heads = conv_keys.shape[0]
    width = heads * DH
    crows = rows // RATE
    q, k, v, pk, pv = (
        lax.all_to_all(a, SEQ, split_axis=1, concat_axis=0, tiled=True)
        for a in (queries, keys, values, prior_keys, prior_values)
    )
    fk = jnp.where(group == 0, pk, shifted(k, SEG, 1))
    fv = jnp.where(group == 0, pv, shifted(v, SEG, 1))
    b0 = pick_entry(doc_starts, group)
    b1 = jnp.where(group >= 1, pick_entry(doc_starts, group - 1), rows)
    b2 = jnp.where(group >= 2, pick_entry(doc_starts, group - 2), rows)
    s1 = jnp.where(b1 < rows, b1, 0)
    s2 = jnp.where(b2 < rows, b2, 0)
    lead = jnp.where((group >= 1) & (b1 >= rows), s2, rows)
    sc = jnp.stack((b0, s1, lead, lead)).astype(jnp.int32)
    shape = jax.ShapeDtypeStruct
    limit = 60 << 20
    ck, cv, gk, gv, loss, acc_b, m_b, l_b = pl.pallas_call(
        recon_kernel,
        out_shape=(
            shape((crows, width), BF16), shape((crows, width), BF16),
            shape((heads, RATE * DH, DH), BF16), shape((heads, RATE * DH, DH), BF16),
            shape((8, 128), F32),
            shape((rows, width), F32), shape((rows, DH), F32), shape((rows, DH), F32),
        ),
        in_specs=[SMEM] + vmem(5),
        out_specs=tuple(vmem(8)),
        scratch_shapes=[
            pltpu.VMEM((RATE, crows, width), BF16), pltpu.VMEM((RATE, crows, width), BF16),
            pltpu.VMEM((heads, rows, 2 * DH), BF16),
            pltpu.VMEM((heads, crows, DH), F32), pltpu.VMEM((heads, crows, DH), F32),
            pltpu.VMEM((heads, DH, crows), BF16), pltpu.VMEM((DH, BQ), F32),
        ],
        compiler_params=pltpu.CompilerParams(vmem_limit_bytes=limit),
        name="recon",
    )(sc, q, fk, fv, conv_keys, conv_values)
    mk = shifted(ck, SEG, 1)
    mv = shifted(cv, SEG, 1)
    grads = lax.psum(jnp.concatenate((gk, gv)), SEG)
    total = loss[0, 0]
    for axis in SEG_SEQ:
        total = lax.psum(total, axis)
    attended = pl.pallas_call(
        attend_kernel,
        out_shape=shape((rows, width), BF16),
        in_specs=[SMEM] + vmem(8),
        out_specs=vmem(1)[0],
        compiler_params=pltpu.CompilerParams(vmem_limit_bytes=limit),
        name="attend",
    )(sc, q, k, v, mk, mv, acc_b, m_b, l_b)
    attended = lax.all_to_all(attended, SEQ, split_axis=0, concat_axis=1, tiled=True)
    recon_loss = total / (lax.axis_size(SEG) * rows)
    grads = grads.astype(F32)
    return (attended, ck, cv, recon_loss, grads[:heads], grads[heads:])


def solution(mesh):
    finer = Mesh(mesh.devices.reshape(4, 2, 4, 4), ("seg_0", "seg_1", "seq_0", "seq_1"))
    return jax.shard_map(
        on_device,
        mesh=finer,
        in_specs=(
            P(SEG_SEQ, None), P(SEG_SEQ, None), P(SEG_SEQ, None),
            P(SEQ, None), P(SEQ, None),
            P(SEQ, None, None), P(SEQ, None, None),
            P(),
        ),
        out_specs=(
            P(SEG_SEQ, None), P(SEG, SEQ), P(SEG, SEQ), P(),
            P(SEQ, None, None), P(SEQ, None, None),
        ),
        check_vma=False,
    )
```

```python
import functools
import math

import jax
import jax.numpy as jnp
from jax import lax
from jax.experimental import pallas as pl
from jax.experimental.pallas import tpu as pltpu
from jax.sharding import Mesh
from jax.sharding import PartitionSpec as P

RATE = 4
SEQ = ("seq_0", "seq_1")
SEG = ("seg_0", "seg_1")
SEG_SEQ = ("seg_0", "seg_1", "seq_0", "seq_1")
NEG = -1e30
MESH = pl.DeviceIdType.MESH
F32 = jnp.float32
BF16 = jnp.bfloat16
BQ = 256
DH = 128
NT = (((1,), (1,)), ((), ()))
NN = (((1,), (0,)), ((), ()))
TN = (((0,), (0,)), ((), ()))


def mm(a, b, dims):
    return lax.dot_general(a, b, dims, preferred_element_type=F32)


def recon_kernel(sc, q, fk, fv, wk, wv, ck, cv, gk, gv, loss, acc_b, m_b, l_b,
                 wink, winv, vab, vg, kg, cvt, lacc):
    rows = q.shape[0]
    heads = q.shape[1] // DH
    crows = rows // RATE
    s1 = sc[1]
    scale = 1.0 / math.sqrt(DH)
    c2 = scale * math.log2(math.e)
    r_i = lax.broadcasted_iota(jnp.int32, (128, 128), 0)
    c_i = lax.broadcasted_iota(jnp.int32, (128, 128), 1)
    perm = (c_i == RATE * (r_i % 32) + r_i // 32).astype(BF16)

    def window(b, carry):
        at = pl.ds(pl.multiple_of(b * 128, 128), 128)
        to = pl.ds(pl.multiple_of(b * 32, 32), 32)
        wa = mm(perm, fk[at, :], NN).astype(BF16)
        wb = mm(perm, fv[at, :], NN).astype(BF16)
        for r in range(RATE):
            wink[r, to, :] = wa[32 * r:32 * r + 32]
            winv[r, to, :] = wb[32 * r:32 * r + 32]
        return carry

    lax.fori_loop(0, rows // 128, window, 0)
    for h in range(heads):
        cols = slice(h * DH, (h + 1) * DH)
        for win, w, out in ((wink, wk, ck), (winv, wv, cv)):
            total = mm(win[0, :, cols], w[h, 0:DH, :], NN)
            for r in range(1, RATE):
                total += mm(win[r, :, cols], w[h, r * DH:(r + 1) * DH, :], NN)
            out[:, cols] = total.astype(BF16)
        cvt[h] = cv[:, cols].astype(F32).T.astype(BF16)
        row = lax.broadcasted_iota(jnp.int32, (rows, DH), 0)
        val = fv[:, cols]
        zero = jnp.zeros_like(val)
        vab[h, :, 0:DH] = jnp.where(row < s1, val, zero)
        vab[h, :, DH:] = jnp.where(row < s1, zero, val)
    vg[...] = jnp.zeros_like(vg)
    kg[...] = jnp.zeros_like(kg)
    lacc[...] = jnp.zeros_like(lacc)

    def block(i, carry):
        at = pl.ds(pl.multiple_of(i * BQ, BQ), BQ)
        tops = []
        for h in range(heads):
            cols = slice(h * DH, (h + 1) * DH)
            qb = q[at, cols]
            is_b = lax.broadcasted_iota(jnp.int32, (1, rows), 1) >= s1
            s = mm(qb, fk[:, cols], NT)
            m_all = jnp.max(s, axis=1, keepdims=True)
            m_tail = jnp.max(jnp.where(is_b, s, NEG), axis=1, keepdims=True)
            p = jnp.exp2((s - jnp.where(is_b, m_tail, m_all)) * c2)
            l_all = jnp.sum(p, axis=1, keepdims=True)
            l_tail = jnp.sum(jnp.where(is_b, p, 0.0), axis=1, keepdims=True)
            u = mm(p.astype(BF16), vab[h], NN)
            u_tail = u[:, DH:]
            w_tail = jnp.exp2((m_tail - m_all) * c2)
            fine = (u[:, :DH] + w_tail * u_tail) / ((l_all - l_tail) + w_tail * l_tail)
            acc_b[at, cols] = u_tail
            tops.append((m_tail, l_tail))
            st = mm(ck[:, cols], qb, NT)
            mc = jnp.max(st, axis=0, keepdims=True)
            pt = jnp.exp2((st - mc) * c2)
            lc = jnp.sum(pt, axis=0, keepdims=True)
            ptb = pt.astype(BF16)
            rc = mm(cvt[h], ptb, NN) / lc
            differ = fine.T - rc
            lacc[...] += differ * differ
            og = (-2.0 * differ / lc).astype(BF16)
            vg[h] += mm(ptb, og, NT)
            inner = mm(cv[:, cols], og, NN)
            offset = jnp.sum(og.astype(F32) * rc, axis=0, keepdims=True)
            sg = (pt * (inner - offset)).astype(BF16)
            kg[h] += mm(sg, qb, NN)
        half = lax.broadcasted_iota(jnp.int32, (BQ, DH), 1) < DH // 2
        m_b[at, :] = jnp.where(half, tops[0][0], tops[1][0])
        l_b[at, :] = jnp.where(half, tops[0][1], tops[1][1])
        return carry

    lax.fori_loop(0, rows // BQ, block, 0)
    loss[...] = jnp.full(loss.shape, jnp.sum(lacc[...]), F32)
    for h in range(heads):
        cols = slice(h * DH, (h + 1) * DH)
        kgb = (kg[h] * scale).astype(BF16)
        vgb = vg[h].astype(BF16)
        for r in range(RATE):
            gk[h, r * DH:(r + 1) * DH, :] = mm(wink[r, :, cols], kgb, TN).astype(BF16)
            gv[h, r * DH:(r + 1) * DH, :] = mm(winv[r, :, cols], vgb, TN).astype(BF16)


def attend_kernel(sc, q, k, v, mk, mv, acc_b, m_b, l_b, out):
    rows = q.shape[0]
    heads = q.shape[1] // DH
    crows = rows // RATE
    b0 = sc[0]
    lead = sc[2]
    c2 = math.log2(math.e) / math.sqrt(DH)
    for i in range(rows // BQ):
        lo, hi = i * BQ, (i + 1) * BQ
        for h in range(heads):
            cols = slice(h * DH, (h + 1) * DH)
            qb = q[lo:hi, cols]
            place = lax.broadcasted_iota(jnp.int32, (BQ, 1), 0) + lo
            before = place < b0
            first = jnp.where(before, 0, b0)
            s = mm(qb, k[0:hi, cols], NT)
            at = lax.broadcasted_iota(jnp.int32, (BQ, hi), 1)
            s = jnp.where(at >= first, s, NEG)
            tail = s[:, lo:hi]
            tri = (lax.broadcasted_iota(jnp.int32, (BQ, BQ), 1)
                   <= lax.broadcasted_iota(jnp.int32, (BQ, BQ), 0))
            tail = jnp.where(tri, tail, NEG)
            if i:
                s = jnp.concatenate((s[:, :lo], tail), axis=1)
            else:
                s = tail
            sm = mm(qb, mk[:, cols], NT)
            jm = lax.broadcasted_iota(jnp.int32, (BQ, crows), 1)
            sm = jnp.where(RATE * jm >= jnp.where(before, lead, RATE * crows), sm, NEG)
            spot = h * (DH // 2)
            m_f = jnp.where(before, m_b[lo:hi, spot:spot + 1], NEG)
            top = jnp.maximum(jnp.max(s, axis=1, keepdims=True), jnp.max(sm, axis=1, keepdims=True))
            top = jnp.maximum(top, m_f)
            p = jnp.exp2((s - top) * c2)
            pm = jnp.exp2((sm - top) * c2)
            wf = jnp.exp2((m_f - top) * c2)
            total = (jnp.sum(p, axis=1, keepdims=True) + jnp.sum(pm, axis=1, keepdims=True)
                     + wf * l_b[lo:hi, spot:spot + 1])
            acc = mm(p.astype(BF16), v[0:hi, cols], NN) + mm(pm.astype(BF16), mv[:, cols], NN)
            acc += wf * acc_b[lo:hi, cols]
            out[lo:hi, cols] = (acc / total).astype(BF16)


def on(seg=None, seq=None):
    target = {}
    if seg is not None:
        target["seg_0"] = seg // 2
        target["seg_1"] = lax.rem(seg, 2)
    if seq is not None:
        target["seq_0"] = seq // 4
        target["seq_1"] = lax.rem(seq, 4)
    return target


def places():
    seg = lax.axis_index("seg_0") * 2 + lax.axis_index("seg_1")
    z = lax.axis_index("seq_0")
    y = lax.axis_index("seq_1")
    return seg, z, y


def meet(seg, z, y):
    barrier = pltpu.get_barrier_semaphore()

    def greet_seq(d, carry):
        pl.semaphore_signal(barrier, inc=1, device_id=on(seq=hop(z, y, d)), device_id_type=MESH)
        return carry

    def greet_seg(d, carry):
        pl.semaphore_signal(barrier, inc=1, device_id=on(seg=lax.rem(seg + d, 8)), device_id_type=MESH)
        return carry

    lax.fori_loop(1, 16, greet_seq, 0)
    lax.fori_loop(1, 8, greet_seg, 0)
    pl.semaphore_wait(barrier, 22)


def hop(z, y, d):
    return lax.rem(z + d // 4, 4) * 4 + lax.rem(y + lax.rem(d, 4), 4)


def back(z, y, d):
    return lax.rem(z + 4 - d // 4, 4) * 4 + lax.rem(y + 4 - lax.rem(d, 4), 4)


def remote(src, dst, send, recv, target):
    return pltpu.make_async_remote_copy(
        src_ref=src, dst_ref=dst, send_sem=send, recv_sem=recv,
        device_id=target, device_id_type=MESH)


def exchange_kernel(q_in, k_in, v_in, pk_in, pv_in, q, k, v, fk, fv,
                    bounce, stage, own_sem, out_sem, in_sem, fsend, frecv,
                    psend, precv, rsend, rrecv, lsem):
    seg, z, y = places()
    me = z * 4 + y
    width = q.shape[2]
    ahead = lax.rem(seg + 1, 8)

    def cols(i):
        return pl.ds(pl.multiple_of(i * width, width), width)

    mine = [pltpu.make_async_copy(a.at[:, cols(me)], bounce.at[n], own_sem.at[n])
            for n, a in enumerate((k_in, v_in, q_in))]
    for c in mine:
        c.start()
    tap = pl.ds(pl.multiple_of(seg * 16, 16), 16)
    mine_p = [pltpu.make_async_copy(a.at[tap, cols(me)], stage.at[n, me], own_sem.at[3 + n])
              for n, a in enumerate((pk_in, pv_in))]
    for c in mine_p:
        c.start()
    meet(seg, z, y)

    def block(n, a, o, d):
        there = hop(z, y, d)
        return remote(a.at[:, cols(there)], o.at[me], out_sem.at[n, d], in_sem.at[n, me], on(seq=there))

    def arrival(n, a, o, d):
        src = back(z, y, d)
        return remote(a.at[:, cols(me)], o.at[src], out_sem.at[n, d], in_sem.at[n, src], on(seq=src))

    def piece(n, a, d):
        there = hop(z, y, d)
        return remote(a.at[tap, cols(there)], stage.at[n, me], psend.at[n, d], precv.at[n, me], on(seq=there))

    def piece_in(n, a, d):
        src = back(z, y, d)
        return remote(a.at[tap, cols(me)], stage.at[n, src], psend.at[n, d], precv.at[n, src], on(seq=src))

    def forward(n, o, f, src):
        return remote(o.at[src], f.at[src], fsend.at[n, src], frecv.at[n, src], on(seg=ahead))

    def forward_piece(n, f):
        return remote(stage.at[n], f.at[:, tap, :], rsend.at[n], rrecv.at[n, seg], on(seg=seg * 0))

    def each(f):
        def body(d, carry):
            f(d)
            return carry
        lax.fori_loop(1, 16, body, 0)

    each(lambda d: block(0, k_in, k, d).start())
    each(lambda d: block(1, v_in, v, d).start())
    each(lambda d: piece(0, pk_in, d).start())
    each(lambda d: piece(1, pv_in, d).start())
    each(lambda d: block(2, q_in, q, d).start())

    local = []
    for n, (c, o) in enumerate(zip(mine, (k, v, q))):
        c.wait()
        local.append(pltpu.make_async_copy(bounce.at[n], o.at[me], lsem.at[n]))
        local[-1].start()
    for c in local:
        c.wait()

    def pass_on(n, a, o, f):
        @pl.when(seg < 7)
        def _():
            forward(n, o, f, me).start()

        def body(d):
            arrival(n, a, o, d).wait_recv()

            @pl.when(seg < 7)
            def _():
                forward(n, o, f, back(z, y, d)).start()
        each(body)

    pass_on(0, k_in, k, fk)
    pass_on(1, v_in, v, fv)
    for n, (a, c, f) in enumerate(((pk_in, mine_p[0], fk), (pv_in, mine_p[1], fv))):
        c.wait()
        each(lambda d: piece_in(n, a, d).wait_recv())

        @pl.when(seg > 0)
        def _():
            forward_piece(n, f).start()

        @pl.when(seg == 0)
        def _():
            pltpu.make_async_copy(stage.at[n], f.at[:, tap, :], lsem.at[n]).start()
    each(lambda d: arrival(2, q_in, q, d).wait_recv())

    for n, (a, o) in enumerate(((k_in, k), (v_in, v), (q_in, q))):
        each(lambda d: block(n, a, o, d).wait_send())
    for n, a in enumerate((pk_in, pv_in)):
        each(lambda d: piece(n, a, d).wait_send())

    def every(f):
        def body(d, carry):
            f(d)
            return carry
        lax.fori_loop(0, 16, body, 0)

    @pl.when(seg < 7)
    def _():
        every(lambda d: forward(0, k, fk, d).wait_send())
        every(lambda d: forward(1, v, fv, d).wait_send())

    @pl.when(seg > 0)
    def _():
        every(lambda d: forward(0, k, fk, d).wait_recv())
        every(lambda d: forward(1, v, fv, d).wait_recv())
        forward_piece(0, fk).wait_send()
        forward_piece(1, fv).wait_send()

    @pl.when(seg == 0)
    def _():
        for n, f in enumerate((fk, fv)):
            pltpu.make_async_copy(stage.at[n], f.at[:, tap, :], lsem.at[n]).wait()

            def body(i, carry):
                at = pl.ds(pl.multiple_of(i * 16, 16), 16)
                remote(stage.at[n], f.at[:, at, :], rsend.at[n], rrecv.at[n, i], on(seg=i)).wait_recv()
                return carry
            lax.fori_loop(1, 8, body, 0)


def exchange(queries, keys, values, prior_keys, prior_values, seq_count, width):
    rows = queries.shape[0]
    block = jax.ShapeDtypeStruct((seq_count, rows, width), BF16)
    dma = pltpu.SemaphoreType.DMA
    outs = pl.pallas_call(
        exchange_kernel,
        out_shape=(block,) * 5,
        in_specs=[pl.BlockSpec(memory_space=pl.ANY)] * 5,
        out_specs=(pl.BlockSpec(memory_space=pl.ANY),) * 5,
        scratch_shapes=[
            pltpu.VMEM((3, rows, width), BF16),
            pltpu.VMEM((2, seq_count, 16, width), BF16),
            dma((5,)), dma((3, 16)), dma((3, 16)), dma((2, 16)), dma((2, 16)),
            dma((2, 16)), dma((2, 16)), dma((2,)), dma((2, 8)), dma((3,)),
        ],
        compiler_params=pltpu.CompilerParams(collective_id=0, has_side_effects=True),
        name="exchange",
    )(queries, keys, values, prior_keys, prior_values)
    return [o.reshape(seq_count * rows, width) for o in outs]


def shifted(block, axis, distance):
    count = lax.axis_size(axis)
    return lax.ppermute(block, axis, [(i, i + distance) for i in range(count - distance)])


def pick_entry(small_table, wanted):
    return jnp.sum(jnp.where(jnp.arange(small_table.shape[0]) == wanted, small_table, 0))


def vmem(n):
    return [pl.BlockSpec(memory_space=pltpu.VMEM)] * n


SMEM = pl.BlockSpec(memory_space=pltpu.SMEM)


def on_device(queries, keys, values, prior_keys, prior_values, conv_keys, conv_values, doc_starts):
    seq_count = lax.axis_size(SEQ)
    group = lax.axis_index(SEG)
    rows = queries.shape[0] * seq_count
    heads = conv_keys.shape[0]
    width = heads * DH
    crows = rows // RATE
    q, k, v, fk, fv = exchange(queries, keys, values, prior_keys, prior_values, seq_count, width)
    b0 = pick_entry(doc_starts, group)
    b1 = jnp.where(group >= 1, pick_entry(doc_starts, group - 1), rows)
    b2 = jnp.where(group >= 2, pick_entry(doc_starts, group - 2), rows)
    s1 = jnp.where(b1 < rows, b1, 0)
    s2 = jnp.where(b2 < rows, b2, 0)
    lead = jnp.where((group >= 1) & (b1 >= rows), s2, rows)
    sc = jnp.stack((b0, s1, lead, lead)).astype(jnp.int32)
    shape = jax.ShapeDtypeStruct
    limit = 60 << 20
    ck, cv, gk, gv, loss, acc_b, m_b, l_b = pl.pallas_call(
        recon_kernel,
        out_shape=(
            shape((crows, width), BF16), shape((crows, width), BF16),
            shape((heads, RATE * DH, DH), BF16), shape((heads, RATE * DH, DH), BF16),
            shape((8, 128), F32),
            shape((rows, width), F32), shape((rows, DH), F32), shape((rows, DH), F32),
        ),
        in_specs=[SMEM] + vmem(5),
        out_specs=tuple(vmem(8)),
        scratch_shapes=[
            pltpu.VMEM((RATE, crows, width), BF16), pltpu.VMEM((RATE, crows, width), BF16),
            pltpu.VMEM((heads, rows, 2 * DH), BF16),
            pltpu.VMEM((heads, crows, DH), F32), pltpu.VMEM((heads, crows, DH), F32),
            pltpu.VMEM((heads, DH, crows), BF16), pltpu.VMEM((DH, BQ), F32),
        ],
        compiler_params=pltpu.CompilerParams(vmem_limit_bytes=limit),
        name="recon",
    )(sc, q, fk, fv, conv_keys, conv_values)
    mk = shifted(ck, SEG, 1)
    mv = shifted(cv, SEG, 1)
    grads = lax.psum(jnp.concatenate((gk, gv)), SEG)
    total = loss[0, 0]
    for axis in SEG_SEQ:
        total = lax.psum(total, axis)
    attended = pl.pallas_call(
        attend_kernel,
        out_shape=shape((rows, width), BF16),
        in_specs=[SMEM] + vmem(8),
        out_specs=vmem(1)[0],
        compiler_params=pltpu.CompilerParams(vmem_limit_bytes=limit),
        name="attend",
    )(sc, q, k, v, mk, mv, acc_b, m_b, l_b)
    attended = lax.all_to_all(attended, SEQ, split_axis=0, concat_axis=1, tiled=True)
    recon_loss = total / (lax.axis_size(SEG) * rows)
    grads = grads.astype(F32)
    return (attended, ck, cv, recon_loss, grads[:heads], grads[heads:])


def solution(mesh):
    finer = Mesh(mesh.devices.reshape(4, 2, 4, 4), ("seg_0", "seg_1", "seq_0", "seq_1"))
    return jax.shard_map(
        on_device,
        mesh=finer,
        in_specs=(
            P(SEG_SEQ, None), P(SEG_SEQ, None), P(SEG_SEQ, None),
            P(SEQ, None), P(SEQ, None),
            P(SEQ, None, None), P(SEQ, None, None),
            P(),
        ),
        out_specs=(
            P(SEG_SEQ, None), P(SEG, SEQ), P(SEG, SEQ), P(),
            P(SEQ, None, None), P(SEQ, None, None),
        ),
        check_vma=False,
    )
```

```python
import functools
import math

import jax
import jax.numpy as jnp
from jax import lax
from jax.experimental import pallas as pl
from jax.experimental.pallas import tpu as pltpu
from jax.sharding import Mesh
from jax.sharding import PartitionSpec as P

RATE = 4
SEQ = ("seq_0", "seq_1")
SEG = ("seg_0", "seg_1")
SEG_SEQ = ("seg_0", "seg_1", "seq_0", "seq_1")
NEG = -1e30
MESH = pl.DeviceIdType.MESH
F32 = jnp.float32
BF16 = jnp.bfloat16
BQ = 256
DH = 128
NT = (((1,), (1,)), ((), ()))
NN = (((1,), (0,)), ((), ()))
TN = (((0,), (0,)), ((), ()))


def mm(a, b, dims):
    return lax.dot_general(a, b, dims, preferred_element_type=F32)


def on(seg=None, seq=None):
    target = {}
    if seg is not None:
        target["seg_0"] = seg // 2
        target["seg_1"] = lax.rem(seg, 2)
    if seq is not None:
        target["seq_0"] = seq // 4
        target["seq_1"] = lax.rem(seq, 4)
    return target


def places():
    seg = lax.axis_index("seg_0") * 2 + lax.axis_index("seg_1")
    z = lax.axis_index("seq_0")
    y = lax.axis_index("seq_1")
    return seg, z, y


def meet(seg, z, y):
    barrier = pltpu.get_barrier_semaphore()

    def greet_seq(d, carry):
        pl.semaphore_signal(barrier, inc=1, device_id=on(seq=hop(z, y, d)), device_id_type=MESH)
        return carry

    def greet_seg(d, carry):
        pl.semaphore_signal(barrier, inc=1, device_id=on(seg=lax.rem(seg + d, 8)), device_id_type=MESH)
        return carry

    lax.fori_loop(1, 16, greet_seq, 0)
    lax.fori_loop(1, 8, greet_seg, 0)
    pl.semaphore_wait(barrier, 22)


def hop(z, y, d):
    return lax.rem(z + d // 4, 4) * 4 + lax.rem(y + lax.rem(d, 4), 4)


def back(z, y, d):
    return lax.rem(z + 4 - d // 4, 4) * 4 + lax.rem(y + 4 - lax.rem(d, 4), 4)


def remote(src, dst, send, recv, target):
    return pltpu.make_async_remote_copy(
        src_ref=src, dst_ref=dst, send_sem=send, recv_sem=recv,
        device_id=target, device_id_type=MESH)


def recon_kernel(sc, q, fk, fv, wk, wv, ck, cv, grads, loss, acc_b, m_b, l_b, mk, mv,
                 wink, winv, vab, vg, kg, cvt, lacc, send, recv):
    seg, z, y = places()
    ahead, behind = lax.rem(seg + 1, 8), lax.rem(seg + 7, 8)
    barrier = pltpu.get_barrier_semaphore()
    for peer in (ahead, behind):
        pl.semaphore_signal(barrier, inc=1, device_id=on(seg=peer), device_id_type=MESH)
    rows = q.shape[0]
    heads = q.shape[1] // DH
    crows = rows // RATE
    s1 = sc[1]
    scale = 1.0 / math.sqrt(DH)
    c2 = scale * math.log2(math.e)
    r_i = lax.broadcasted_iota(jnp.int32, (128, 128), 0)
    c_i = lax.broadcasted_iota(jnp.int32, (128, 128), 1)
    perm = (c_i == RATE * (r_i % 32) + r_i // 32).astype(BF16)

    def window(b, carry):
        at = pl.ds(pl.multiple_of(b * 128, 128), 128)
        to = pl.ds(pl.multiple_of(b * 32, 32), 32)
        wa = mm(perm, fk[at, :], NN).astype(BF16)
        wb = mm(perm, fv[at, :], NN).astype(BF16)
        for r in range(RATE):
            wink[r, to, :] = wa[32 * r:32 * r + 32]
            winv[r, to, :] = wb[32 * r:32 * r + 32]
        return carry

    lax.fori_loop(0, rows // 128, window, 0)
    for h in range(heads):
        cols = slice(h * DH, (h + 1) * DH)
        for win, w, out in ((wink, wk, ck), (winv, wv, cv)):
            total = mm(win[0, :, cols], w[h, 0:DH, :], NN)
            for r in range(1, RATE):
                total += mm(win[r, :, cols], w[h, r * DH:(r + 1) * DH, :], NN)
            out[:, cols] = total.astype(BF16)
        cvt[h] = cv[:, cols].astype(F32).T.astype(BF16)
        row = lax.broadcasted_iota(jnp.int32, (rows, DH), 0)
        val = fv[:, cols]
        zero = jnp.zeros_like(val)
        vab[h, :, 0:DH] = jnp.where(row < s1, val, zero)
        vab[h, :, DH:] = jnp.where(row < s1, zero, val)
    pl.semaphore_wait(barrier, 2)
    shifts = [remote(a, b, send.at[n], recv.at[n], on(seg=ahead))
              for n, (a, b) in enumerate(((ck, mk), (cv, mv)))]

    @pl.when(seg < 7)
    def _():
        for c in shifts:
            c.start()

    @pl.when(seg == 0)
    def _():
        mk[...] = jnp.zeros_like(mk)
        mv[...] = jnp.zeros_like(mv)

    vg[...] = jnp.zeros_like(vg)
    kg[...] = jnp.zeros_like(kg)
    lacc[...] = jnp.zeros_like(lacc)

    def block(i, carry):
        at = pl.ds(pl.multiple_of(i * BQ, BQ), BQ)
        tops = []
        for h in range(heads):
            cols = slice(h * DH, (h + 1) * DH)
            qb = q[at, cols]
            is_b = lax.broadcasted_iota(jnp.int32, (1, rows), 1) >= s1
            s = mm(qb, fk[:, cols], NT)
            m_all = jnp.max(s, axis=1, keepdims=True)
            m_tail = jnp.max(jnp.where(is_b, s, NEG), axis=1, keepdims=True)
            p = jnp.exp2((s - jnp.where(is_b, m_tail, m_all)) * c2)
            l_all = jnp.sum(p, axis=1, keepdims=True)
            l_tail = jnp.sum(jnp.where(is_b, p, 0.0), axis=1, keepdims=True)
            u = mm(p.astype(BF16), vab[h], NN)
            u_tail = u[:, DH:]
            w_tail = jnp.exp2((m_tail - m_all) * c2)
            fine = (u[:, :DH] + w_tail * u_tail) / ((l_all - l_tail) + w_tail * l_tail)
            acc_b[at, cols] = u_tail
            tops.append((m_tail, l_tail))
            st = mm(ck[:, cols], qb, NT)
            mc = jnp.max(st, axis=0, keepdims=True)
            pt = jnp.exp2((st - mc) * c2)
            lc = jnp.sum(pt, axis=0, keepdims=True)
            ptb = pt.astype(BF16)
            rc = mm(cvt[h], ptb, NN) / lc
            differ = fine.T - rc
            lacc[...] += differ * differ
            og = (-2.0 * differ / lc).astype(BF16)
            vg[h] += mm(ptb, og, NT)
            inner = mm(cv[:, cols], og, NN)
            offset = jnp.sum(og.astype(F32) * rc, axis=0, keepdims=True)
            sg = (pt * (inner - offset)).astype(BF16)
            kg[h] += mm(sg, qb, NN)
        half = lax.broadcasted_iota(jnp.int32, (BQ, DH), 1) < DH // 2
        m_b[at, :] = jnp.where(half, tops[0][0], tops[1][0])
        l_b[at, :] = jnp.where(half, tops[0][1], tops[1][1])
        return carry

    lax.fori_loop(0, rows // BQ, block, 0)
    loss[...] = jnp.full(loss.shape, jnp.sum(lacc[...]), F32)
    for h in range(heads):
        cols = slice(h * DH, (h + 1) * DH)
        kgb = (kg[h] * scale).astype(BF16)
        vgb = vg[h].astype(BF16)
        for r in range(RATE):
            part = slice(r * DH, (r + 1) * DH)
            grads[h, part, :] = mm(wink[r, :, cols], kgb, TN).astype(BF16)
            grads[heads + h, part, :] = mm(winv[r, :, cols], vgb, TN).astype(BF16)

    @pl.when(seg < 7)
    def _():
        for c in shifts:
            c.wait_send()

    @pl.when(seg > 0)
    def _():
        for c in shifts:
            c.wait_recv()


def attend_kernel(sc, q, k, v, mk, mv, acc_b, m_b, l_b, grads, loss,
                  out, gk, gv, total_loss,
                  obuf, rs, ag, red, lseg, lseq, lsum,
                  osend, orecv, rsend, rrecv, asend, arecv, lsend, lrecv, tsend, trecv, own):
    seg, z, y = places()
    me = z * 4 + y
    rows = q.shape[0]
    width = q.shape[1]
    heads = width // DH
    crows = rows // RATE
    b0 = sc[0]
    lead = sc[2]
    c2 = math.log2(math.e) / math.sqrt(DH)
    share = rs.shape[2]

    def peer(d):
        return lax.rem(seg + d, 8)

    def share_of(i):
        return pl.ds(pl.multiple_of(i * share, share), share)

    def scatter(d):
        return remote(grads.at[:, share_of(peer(d)), :], rs.at[seg], rsend.at[d], rrecv.at[seg], on(seg=peer(d)))

    def scattered(d):
        return remote(grads.at[:, share_of(seg), :], rs.at[peer(d)], rsend.at[d], rrecv.at[peer(d)], on(seg=peer(d)))

    def gather(d):
        return remote(red, ag.at[seg], asend.at[d], arecv.at[seg], on(seg=peer(d)))

    def gathered(d):
        return remote(red, ag.at[peer(d)], asend.at[d], arecv.at[peer(d)], on(seg=peer(d)))

    def tell(d):
        return remote(loss, lseg.at[seg], lsend.at[d], lrecv.at[seg], on(seg=peer(d)))

    def told(d):
        return remote(loss, lseg.at[peer(d)], lsend.at[d], lrecv.at[peer(d)], on(seg=peer(d)))

    def spread(d):
        return remote(lsum, lseq.at[me], tsend.at[d], trecv.at[me], on(seq=hop(z, y, d)))

    def spreaded(d):
        src = back(z, y, d)
        return remote(lsum, lseq.at[src], tsend.at[d], trecv.at[src], on(seq=src))

    def cols_of(i):
        return pl.ds(pl.multiple_of(i * width, width), width)

    def rows_of(i):
        return pl.ds(pl.multiple_of(i * 128, 128), 128)

    def give(b):
        return remote(obuf.at[rows_of(b), :], out.at[:, cols_of(me)], osend.at[b], orecv.at[me], on(seq=b))

    def given(b):
        return remote(obuf.at[rows_of(me), :], out.at[:, cols_of(b)], osend.at[b], orecv.at[b], on(seq=b))

    keep = pltpu.make_async_copy(obuf.at[rows_of(me), :], out.at[:, cols_of(me)], own.at[0])

    def span(lo, hi, f):
        def body(d, carry):
            f(d)
            return carry
        lax.fori_loop(lo, hi, body, 0)

    meet(seg, z, y)
    span(1, 8, lambda d: scatter(d).start())
    span(1, 8, lambda d: tell(d).start())

    def attend_block(i):
        lo, hi = i * BQ, (i + 1) * BQ
        for h in range(heads):
            cols = slice(h * DH, (h + 1) * DH)
            qb = q[lo:hi, cols]
            place = lax.broadcasted_iota(jnp.int32, (BQ, 1), 0) + lo
            before = place < b0
            first = jnp.where(before, 0, b0)
            s = mm(qb, k[0:hi, cols], NT)
            at = lax.broadcasted_iota(jnp.int32, (BQ, hi), 1)
            s = jnp.where(at >= first, s, NEG)
            tail = s[:, lo:hi]
            tri = (lax.broadcasted_iota(jnp.int32, (BQ, BQ), 1)
                   <= lax.broadcasted_iota(jnp.int32, (BQ, BQ), 0))
            tail = jnp.where(tri, tail, NEG)
            if i:
                s = jnp.concatenate((s[:, :lo], tail), axis=1)
            else:
                s = tail
            sm = mm(qb, mk[:, cols], NT)
            jm = lax.broadcasted_iota(jnp.int32, (BQ, crows), 1)
            sm = jnp.where(RATE * jm >= jnp.where(before, lead, RATE * crows), sm, NEG)
            spot = h * (DH // 2)
            m_f = jnp.where(before, m_b[lo:hi, spot:spot + 1], NEG)
            top = jnp.maximum(jnp.max(s, axis=1, keepdims=True), jnp.max(sm, axis=1, keepdims=True))
            top = jnp.maximum(top, m_f)
            p = jnp.exp2((s - top) * c2)
            pm = jnp.exp2((sm - top) * c2)
            wf = jnp.exp2((m_f - top) * c2)
            total = (jnp.sum(p, axis=1, keepdims=True) + jnp.sum(pm, axis=1, keepdims=True)
                     + wf * l_b[lo:hi, spot:spot + 1])
            acc = mm(p.astype(BF16), v[0:hi, cols], NN) + mm(pm.astype(BF16), mv[:, cols], NN)
            acc += wf * acc_b[lo:hi, cols]
            obuf[lo:hi, cols] = (acc / total).astype(BF16)

    count = rows // BQ

    def step(t, carry):
        i = lax.rem(t + 1 + me // 2, count)
        for n in range(count):
            pl.when(i == n)(functools.partial(attend_block, n))
        for b in (2 * i, 2 * i + 1):
            @pl.when(b != me)
            def _():
                give(b).start()

            @pl.when(b == me)
            def _():
                keep.start()

        @pl.when(t == 2)
        def _():
            span(1, 8, lambda d: scattered(d).wait_recv())
            span(1, 8, lambda d: told(d).wait_recv())
            acc = grads[:, share_of(seg), :].astype(F32)
            for d in range(1, 8):
                acc += rs[peer(d)].astype(F32)
            red[...] = acc.astype(BF16)
            lseg[seg] = loss[...]
            tally = lseg[0]
            for d in range(1, 8):
                tally += lseg[d]
            lsum[...] = tally
            gk[:, share_of(seg), :] = red[0:heads].astype(F32)
            gv[:, share_of(seg), :] = red[heads:].astype(F32)

        @pl.when(t == 3)
        def _():
            span(1, 8, lambda d: gather(d).start())
            span(1, 16, lambda d: spread(d).start())
        return carry

    lax.fori_loop(0, count, step, 0)

    def collect(d):
        gathered(d).wait_recv()
        gk[:, share_of(peer(d)), :] = ag[peer(d), 0:heads].astype(F32)
        gv[:, share_of(peer(d)), :] = ag[peer(d), heads:].astype(F32)

    span(1, 8, collect)
    span(1, 16, lambda d: spreaded(d).wait_recv())
    lseq[me] = lsum[...]
    tally = lseq[0]
    for d in range(1, 16):
        tally += lseq[d]
    total_loss[...] = tally / (8 * rows)
    span(1, 8, lambda d: scatter(d).wait_send())
    span(1, 8, lambda d: gather(d).wait_send())
    span(1, 8, lambda d: tell(d).wait_send())
    span(1, 16, lambda d: spread(d).wait_send())

    def finish(d):
        give(hop(z, y, d)).wait_send()
        given(hop(z, y, d)).wait_recv()

    span(1, 16, finish)
    keep.wait()


def exchange_kernel(q_in, k_in, v_in, pk_in, pv_in, q, k, v, fk, fv,
                    bounce, stage, own_sem, out_sem, in_sem, fsend, frecv,
                    psend, precv, rsend, rrecv, lsem):
    seg, z, y = places()
    me = z * 4 + y
    width = q.shape[2]
    ahead = lax.rem(seg + 1, 8)

    def cols(i):
        return pl.ds(pl.multiple_of(i * width, width), width)

    mine = [pltpu.make_async_copy(a.at[:, cols(me)], bounce.at[n], own_sem.at[n])
            for n, a in enumerate((k_in, v_in, q_in))]
    for c in mine:
        c.start()
    tap = pl.ds(pl.multiple_of(seg * 16, 16), 16)
    mine_p = [pltpu.make_async_copy(a.at[tap, cols(me)], stage.at[n, me], own_sem.at[3 + n])
              for n, a in enumerate((pk_in, pv_in))]
    for c in mine_p:
        c.start()
    meet(seg, z, y)

    def block(n, a, o, d):
        there = hop(z, y, d)
        return remote(a.at[:, cols(there)], o.at[me], out_sem.at[n, d], in_sem.at[n, me], on(seq=there))

    def arrival(n, a, o, d):
        src = back(z, y, d)
        return remote(a.at[:, cols(me)], o.at[src], out_sem.at[n, d], in_sem.at[n, src], on(seq=src))

    def piece(n, a, d):
        there = hop(z, y, d)
        return remote(a.at[tap, cols(there)], stage.at[n, me], psend.at[n, d], precv.at[n, me], on(seq=there))

    def piece_in(n, a, d):
        src = back(z, y, d)
        return remote(a.at[tap, cols(me)], stage.at[n, src], psend.at[n, d], precv.at[n, src], on(seq=src))

    def forward(n, o, f, src):
        return remote(o.at[src], f.at[src], fsend.at[n, src], frecv.at[n, src], on(seg=ahead))

    def forward_piece(n, f):
        return remote(stage.at[n], f.at[:, tap, :], rsend.at[n], rrecv.at[n, seg], on(seg=seg * 0))

    def each(f):
        def body(d, carry):
            f(d)
            return carry
        lax.fori_loop(1, 16, body, 0)

    each(lambda d: block(0, k_in, k, d).start())
    each(lambda d: block(1, v_in, v, d).start())
    each(lambda d: piece(0, pk_in, d).start())
    each(lambda d: piece(1, pv_in, d).start())
    each(lambda d: block(2, q_in, q, d).start())

    local = []
    for n, (c, o) in enumerate(zip(mine, (k, v, q))):
        c.wait()
        local.append(pltpu.make_async_copy(bounce.at[n], o.at[me], lsem.at[n]))
        local[-1].start()
    for c in local:
        c.wait()

    def pass_on(n, a, o, f):
        @pl.when(seg < 7)
        def _():
            forward(n, o, f, me).start()

        def body(d):
            arrival(n, a, o, d).wait_recv()

            @pl.when(seg < 7)
            def _():
                forward(n, o, f, back(z, y, d)).start()
        each(body)

    pass_on(0, k_in, k, fk)
    pass_on(1, v_in, v, fv)
    for n, (a, c, f) in enumerate(((pk_in, mine_p[0], fk), (pv_in, mine_p[1], fv))):
        c.wait()
        each(lambda d: piece_in(n, a, d).wait_recv())

        @pl.when(seg > 0)
        def _():
            forward_piece(n, f).start()

        @pl.when(seg == 0)
        def _():
            pltpu.make_async_copy(stage.at[n], f.at[:, tap, :], lsem.at[n]).start()
    each(lambda d: arrival(2, q_in, q, d).wait_recv())

    for n, (a, o) in enumerate(((k_in, k), (v_in, v), (q_in, q))):
        each(lambda d: block(n, a, o, d).wait_send())
    for n, a in enumerate((pk_in, pv_in)):
        each(lambda d: piece(n, a, d).wait_send())

    def every(f):
        def body(d, carry):
            f(d)
            return carry
        lax.fori_loop(0, 16, body, 0)

    @pl.when(seg < 7)
    def _():
        every(lambda d: forward(0, k, fk, d).wait_send())
        every(lambda d: forward(1, v, fv, d).wait_send())

    @pl.when(seg > 0)
    def _():
        every(lambda d: forward(0, k, fk, d).wait_recv())
        every(lambda d: forward(1, v, fv, d).wait_recv())
        forward_piece(0, fk).wait_send()
        forward_piece(1, fv).wait_send()

    @pl.when(seg == 0)
    def _():
        for n, f in enumerate((fk, fv)):
            pltpu.make_async_copy(stage.at[n], f.at[:, tap, :], lsem.at[n]).wait()

            def body(i, carry):
                at = pl.ds(pl.multiple_of(i * 16, 16), 16)
                remote(stage.at[n], f.at[:, at, :], rsend.at[n], rrecv.at[n, i], on(seg=i)).wait_recv()
                return carry
            lax.fori_loop(1, 8, body, 0)


def exchange(queries, keys, values, prior_keys, prior_values, seq_count, width):
    rows = queries.shape[0]
    block = jax.ShapeDtypeStruct((seq_count, rows, width), BF16)
    dma = pltpu.SemaphoreType.DMA
    outs = pl.pallas_call(
        exchange_kernel,
        out_shape=(block,) * 5,
        in_specs=[pl.BlockSpec(memory_space=pl.ANY)] * 5,
        out_specs=(pl.BlockSpec(memory_space=pl.ANY),) * 5,
        scratch_shapes=[
            pltpu.VMEM((3, rows, width), BF16),
            pltpu.VMEM((2, seq_count, 16, width), BF16),
            dma((5,)), dma((3, 16)), dma((3, 16)), dma((2, 16)), dma((2, 16)),
            dma((2, 16)), dma((2, 16)), dma((2,)), dma((2, 8)), dma((3,)),
        ],
        compiler_params=pltpu.CompilerParams(collective_id=0, has_side_effects=True),
        name="exchange",
    )(queries, keys, values, prior_keys, prior_values)
    return [o.reshape(seq_count * rows, width) for o in outs]


def pick_entry(small_table, wanted):
    return jnp.sum(jnp.where(jnp.arange(small_table.shape[0]) == wanted, small_table, 0))


def vmem(n):
    return [pl.BlockSpec(memory_space=pltpu.VMEM)] * n


SMEM = pl.BlockSpec(memory_space=pltpu.SMEM)


def on_device(queries, keys, values, prior_keys, prior_values, conv_keys, conv_values, doc_starts):
    seq_count = lax.axis_size(SEQ)
    group = lax.axis_index(SEG)
    rows = queries.shape[0] * seq_count
    heads = conv_keys.shape[0]
    width = heads * DH
    crows = rows // RATE
    q, k, v, fk, fv = exchange(queries, keys, values, prior_keys, prior_values, seq_count, width)
    b0 = pick_entry(doc_starts, group)
    b1 = jnp.where(group >= 1, pick_entry(doc_starts, group - 1), rows)
    b2 = jnp.where(group >= 2, pick_entry(doc_starts, group - 2), rows)
    s1 = jnp.where(b1 < rows, b1, 0)
    s2 = jnp.where(b2 < rows, b2, 0)
    lead = jnp.where((group >= 1) & (b1 >= rows), s2, rows)
    sc = jnp.stack((b0, s1, lead, lead)).astype(jnp.int32)
    shape = jax.ShapeDtypeStruct
    limit = 60 << 20
    dma = pltpu.SemaphoreType.DMA
    ck, cv, grads, loss, acc_b, m_b, l_b, mk, mv = pl.pallas_call(
        recon_kernel,
        out_shape=(
            shape((crows, width), BF16), shape((crows, width), BF16),
            shape((2 * heads, RATE * DH, DH), BF16),
            shape((8, 128), F32),
            shape((rows, width), F32), shape((rows, DH), F32), shape((rows, DH), F32),
            shape((crows, width), BF16), shape((crows, width), BF16),
        ),
        in_specs=[SMEM] + vmem(5),
        out_specs=tuple(vmem(9)),
        scratch_shapes=[
            pltpu.VMEM((RATE, crows, width), BF16), pltpu.VMEM((RATE, crows, width), BF16),
            pltpu.VMEM((heads, rows, 2 * DH), BF16),
            pltpu.VMEM((heads, crows, DH), F32), pltpu.VMEM((heads, crows, DH), F32),
            pltpu.VMEM((heads, DH, crows), BF16), pltpu.VMEM((DH, BQ), F32),
            dma((2,)), dma((2,)),
        ],
        compiler_params=pltpu.CompilerParams(
            vmem_limit_bytes=limit, collective_id=1, has_side_effects=True),
        name="recon",
    )(sc, q, fk, fv, conv_keys, conv_values)
    share = RATE * DH // 8
    attended, gk, gv, total = pl.pallas_call(
        attend_kernel,
        out_shape=(
            shape((rows // seq_count, seq_count * width), BF16),
            shape((heads, RATE * DH, DH), F32), shape((heads, RATE * DH, DH), F32),
            shape((8, 128), F32),
        ),
        in_specs=[SMEM] + vmem(10),
        out_specs=(pl.BlockSpec(memory_space=pl.ANY), *vmem(3)),
        scratch_shapes=[
            pltpu.VMEM((rows, width), BF16),
            pltpu.VMEM((8, 2 * heads, share, DH), BF16),
            pltpu.VMEM((8, 2 * heads, share, DH), BF16),
            pltpu.VMEM((2 * heads, share, DH), BF16),
            pltpu.VMEM((8, 8, 128), F32), pltpu.VMEM((16, 8, 128), F32), pltpu.VMEM((8, 128), F32),
            dma((16,)), dma((16,)), dma((8,)), dma((8,)), dma((8,)), dma((8,)),
            dma((8,)), dma((8,)), dma((16,)), dma((16,)), dma((1,)),
        ],
        compiler_params=pltpu.CompilerParams(
            vmem_limit_bytes=limit, collective_id=2, has_side_effects=True),
        name="attend",
    )(sc, q, k, v, mk, mv, acc_b, m_b, l_b, grads, loss)
    return (attended, ck, cv, total[0, 0], gk, gv)


def solution(mesh):
    finer = Mesh(mesh.devices.reshape(4, 2, 4, 4), ("seg_0", "seg_1", "seq_0", "seq_1"))
    return jax.shard_map(
        on_device,
        mesh=finer,
        in_specs=(
            P(SEG_SEQ, None), P(SEG_SEQ, None), P(SEG_SEQ, None),
            P(SEQ, None), P(SEQ, None),
            P(SEQ, None, None), P(SEQ, None, None),
            P(),
        ),
        out_specs=(
            P(SEG_SEQ, None), P(SEG, SEQ), P(SEG, SEQ), P(),
            P(SEQ, None, None), P(SEQ, None, None),
        ),
        check_vma=False,
    )
```

```python
import functools
import math

import jax
import jax.numpy as jnp
from jax import lax
from jax.experimental import pallas as pl
from jax.experimental.pallas import tpu as pltpu
from jax.sharding import Mesh
from jax.sharding import PartitionSpec as P

RATE = 4
SEQ = ("seq_0", "seq_1")
SEG = ("seg_0", "seg_1")
SEG_SEQ = ("seg_0", "seg_1", "seq_0", "seq_1")
NEG = -1e30
MESH = pl.DeviceIdType.MESH
F32 = jnp.float32
BF16 = jnp.bfloat16
BQ = 256
DH = 128
NT = (((1,), (1,)), ((), ()))
NN = (((1,), (0,)), ((), ()))
TN = (((0,), (0,)), ((), ()))


def mm(a, b, dims):
    return lax.dot_general(a, b, dims, preferred_element_type=F32)


def on(seg=None, seq=None):
    target = {}
    if seg is not None:
        target["seg_0"] = seg // 2
        target["seg_1"] = lax.rem(seg, 2)
    if seq is not None:
        target["seq_0"] = seq // 4
        target["seq_1"] = lax.rem(seq, 4)
    return target


def places():
    seg = lax.axis_index("seg_0") * 2 + lax.axis_index("seg_1")
    z = lax.axis_index("seq_0")
    y = lax.axis_index("seq_1")
    return seg, z, y


def meet(seg, z, y):
    barrier = pltpu.get_barrier_semaphore()

    def greet_seq(d, carry):
        pl.semaphore_signal(barrier, inc=1, device_id=on(seq=hop(z, y, d)), device_id_type=MESH)
        return carry

    def greet_seg(d, carry):
        pl.semaphore_signal(barrier, inc=1, device_id=on(seg=lax.rem(seg + d, 8)), device_id_type=MESH)
        return carry

    lax.fori_loop(1, 16, greet_seq, 0)
    lax.fori_loop(1, 8, greet_seg, 0)
    pl.semaphore_wait(barrier, 22)


def hop(z, y, d):
    return lax.rem(z + d // 4, 4) * 4 + lax.rem(y + lax.rem(d, 4), 4)


def back(z, y, d):
    return lax.rem(z + 4 - d // 4, 4) * 4 + lax.rem(y + 4 - lax.rem(d, 4), 4)


def remote(src, dst, send, recv, target):
    return pltpu.make_async_remote_copy(
        src_ref=src, dst_ref=dst, send_sem=send, recv_sem=recv,
        device_id=target, device_id_type=MESH)


def recon_kernel(sc, q, fk, fv, wk, wv, ck, cv, grads, loss, acc_b, m_b, l_b, mk, mv,
                 wink, winv, vab, fk2, q2, ck2, ckh, cvh, cvt, sbuf, tops, ptf, ptbuf, rcb, lcb, ubuf, sums, vg, kg, lacc,
                 send, recv):
    seg, z, y = places()
    ahead, behind = lax.rem(seg + 1, 8), lax.rem(seg + 7, 8)
    barrier = pltpu.get_barrier_semaphore()
    for peer in (ahead, behind):
        pl.semaphore_signal(barrier, inc=1, device_id=on(seg=peer), device_id_type=MESH)
    heads, rows = q.shape[0], q.shape[1]
    crows = rows // RATE
    s1 = sc[1]
    scale = 1.0 / math.sqrt(DH)
    c2 = scale * math.log2(math.e)
    r_i = lax.broadcasted_iota(jnp.int32, (128, 128), 0)
    c_i = lax.broadcasted_iota(jnp.int32, (128, 128), 1)
    perm = (c_i == RATE * (r_i % 32) + r_i // 32).astype(BF16)

    def window(b, carry):
        at = pl.ds(pl.multiple_of(b * 128, 128), 128)
        to = pl.ds(pl.multiple_of(b * 32, 32), 32)
        head_row = lax.broadcasted_iota(jnp.int32, (128, DH), 0) + b * 128 < s1
        for h in range(heads):
            val = fv[h, at, :]
            wa = mm(perm, fk[h, at, :], NN).astype(BF16)
            wb = mm(perm, val, NN).astype(BF16)
            for r in range(RATE):
                wink[h, r, to, :] = wa[32 * r:32 * r + 32]
                winv[h, r, to, :] = wb[32 * r:32 * r + 32]
            fk2[h, at, 0:DH] = fk[h, at, :]
            fk2[h, at, DH:] = fk[h, at, :]
            scaled = q[h, at, :].astype(F32) * c2
            high = scaled.astype(BF16)
            q2[h, at, 0:DH] = high
            q2[h, at, DH:] = (scaled - high.astype(F32)).astype(BF16)
            zero = jnp.zeros_like(val)
            vab[h, at, 0:DH] = jnp.where(head_row, val, zero)
            vab[h, at, DH:] = jnp.where(head_row, zero, val)
        return carry

    lax.fori_loop(0, rows // 128, window, 0)
    for h in range(heads):
        for win, w, out, keep in ((wink, wk, ck, ckh), (winv, wv, cv, cvh)):
            total = mm(win[h, 0], w[h, 0:DH, :], NN)
            for r in range(1, RATE):
                total += mm(win[h, r], w[h, r * DH:(r + 1) * DH, :], NN)
            keep[h] = total.astype(BF16)
            out[:, h * DH:(h + 1) * DH] = keep[h]
        ck2[h, :, 0:DH] = ckh[h]
        ck2[h, :, DH:] = ckh[h]
        cvt[h] = cvh[h].astype(F32).T.astype(BF16)
    pl.semaphore_wait(barrier, 2)
    shifts = [remote(a, b, send.at[n], recv.at[n], on(seg=ahead))
              for n, (a, b) in enumerate(((ck, mk), (cv, mv)))]

    @pl.when(seg < 7)
    def _():
        for c in shifts:
            c.start()

    @pl.when(seg == 0)
    def _():
        mk[...] = jnp.zeros_like(mk)
        mv[...] = jnp.zeros_like(mv)

    for a in (vg, kg, lacc):
        a[...] = jnp.zeros_like(a)
    for a in (ptf, ptbuf, rcb, ubuf, tops):
        a[1] = jnp.zeros(a.shape[1:], a.dtype)
    lcb[1] = jnp.ones(lcb.shape[1:], F32)
    sums[1, 0] = jnp.ones(sums.shape[2:], F32)
    sums[1, 1] = jnp.zeros(sums.shape[2:], F32)

    count = rows // BQ
    items = heads * count
    chunk = 512
    chunks = rows // chunk

    def where_is(t):
        h = t // count
        i = lax.rem(t, count)
        return h, pl.ds(pl.multiple_of(i * BQ, BQ), BQ)

    def is_tail(c):
        return lax.broadcasted_iota(jnp.int32, (BQ, chunk), 1) >= s1 - c * chunk

    def fold(x, op):
        out = x[:, 0:128]
        for j in range(1, chunk // 128):
            out = op(out, x[:, j * 128:(j + 1) * 128])
        return out

    def score_chunk(h, qb, c, state, slot):
        s = mm(qb, fk2[h, c * chunk:(c + 1) * chunk, :], NT)
        sbuf[slot, :, c * chunk:(c + 1) * chunk] = s
        a = fold(s, jnp.maximum)
        b = fold(jnp.where(is_tail(c), s, NEG), jnp.maximum)
        return (a, b) if state is None else (jnp.maximum(state[0], a), jnp.maximum(state[1], b))

    def set_tops(state, slot):
        tops[slot, 0] = jnp.broadcast_to(jnp.max(state[0], axis=1, keepdims=True), (BQ, 128))
        tops[slot, 1] = jnp.broadcast_to(jnp.max(state[1], axis=1, keepdims=True), (BQ, 128))

    def grad_steps(t, b):
        h, at = where_is(t)
        hold = {}

        def zero():
            la = jnp.sum(sums[b, 0], axis=1, keepdims=True)
            lt = jnp.sum(sums[b, 1], axis=1, keepdims=True)
            u = ubuf[b, :, 0:DH]
            u_tail = ubuf[b, :, DH:]
            m_all, m_tail = tops[b, 0], tops[b, 1]
            w_tail = jnp.exp2(m_tail - m_all)
            hold["fine"] = (u + w_tail * u_tail) / ((la - lt) + w_tail * lt)
            acc_b[h, at, :] = u_tail
            m_b[h, at, :] = m_tail * (1.0 / c2)
            l_b[h, at, :] = jnp.broadcast_to(lt, (BQ, DH))

        def one():
            differ = hold["fine"].T - rcb[b]
            lacc[...] += differ * differ
            og = (-2.0 * differ / lcb[b, 0:1, :]).astype(BF16)
            hold["og"] = og
            hold["offset"] = jnp.sum(og.astype(F32) * rcb[b], axis=0, keepdims=True)

        def two():
            hold["inner"] = mm(cvh[h], hold["og"], NN)
            vg[h] += mm(ptbuf[b], hold["og"], NT)

        def three():
            hold["sg"] = (ptf[b] * (hold["inner"] - hold["offset"])).astype(BF16)
            kg[h] += mm(hold["sg"], q[h, at, :], NN)
        return zero, one, two, three

    def comp_steps(h, qb, b):
        hold = {}

        def zero():
            hold["st"] = mm(ck2[h], qb, NT)
            hold["mc"] = jnp.max(hold["st"], axis=0, keepdims=True)

        def one():
            pt = jnp.exp2(hold["st"] - hold["mc"])
            ptf[b] = pt
            hold["lc"] = jnp.sum(pt, axis=0, keepdims=True)
            ptbuf[b] = pt.astype(BF16)

        def two():
            rcb[b] = mm(cvt[h], ptbuf[b], NN) / hold["lc"]
            lcb[b] = jnp.broadcast_to(hold["lc"], lcb.shape[1:])
        return zero, one, two, lambda: None

    state = None
    for c in range(chunks):
        state = score_chunk(0, q2[0, 0:BQ, :], c, state, 0)
    set_tops(state, 0)

    def body(j, carry):
        run(2 * j, 0)
        run(2 * j + 1, 1)
        return carry

    def run(t, slot):
        h, at = where_is(t)
        nh, nat = where_is(jnp.minimum(t + 1, items - 1))
        other = 1 - slot
        qb, qn = q2[h, at, :], q2[nh, nat, :]
        pieces = grad_steps(jnp.maximum(t - 1, 0), other)
        comp = comp_steps(h, qb, slot)
        wide_all = jnp.concatenate([tops[slot, 0]] * (chunk // 128), axis=1)
        wide_tail = jnp.concatenate([tops[slot, 1]] * (chunk // 128), axis=1)
        state, u, l_all, l_tail = None, None, None, None
        for c in range(chunks):
            state = score_chunk(nh, qn, c, state, other)
            comp[c]()
            tail = is_tail(c)
            s = sbuf[slot, :, c * chunk:(c + 1) * chunk]
            p = jnp.exp2((s - jnp.where(tail, wide_tail, wide_all)))
            a = fold(p, jnp.add)
            b = fold(jnp.where(tail, p, 0.0), jnp.add)
            part = mm(p.astype(BF16), vab[h, c * chunk:(c + 1) * chunk, :], NN)
            if c == 0:
                u, l_all, l_tail = part, a, b
            else:
                u, l_all, l_tail = u + part, l_all + a, l_tail + b
            pieces[c]()
        set_tops(state, other)
        ubuf[slot] = u
        sums[slot, 0] = l_all
        sums[slot, 1] = l_tail

    lax.fori_loop(0, items // 2, body, 0)
    for f in grad_steps(items - 1, 1):
        f()
    loss[...] = jnp.full(loss.shape, jnp.sum(lacc[...]), F32)
    for h in range(heads):
        kgb = (kg[h] * scale).astype(BF16)
        vgb = vg[h].astype(BF16)
        for r in range(RATE):
            part = slice(r * DH, (r + 1) * DH)
            grads[h, part, :] = mm(wink[h, r], kgb, TN).astype(BF16)
            grads[heads + h, part, :] = mm(winv[h, r], vgb, TN).astype(BF16)

    @pl.when(seg < 7)
    def _():
        for c in shifts:
            c.wait_send()

    @pl.when(seg > 0)
    def _():
        for c in shifts:
            c.wait_recv()


def attend_kernel(sc, q, k, v, mk, mv, acc_b, m_b, l_b, grads, loss,
                  out, gk, gv, total_loss,
                  obuf, rs, ag, red, lseg, lseq, lsum,
                  osend, orecv, rsend, rrecv, asend, arecv, lsend, lrecv, tsend, trecv, own):
    seg, z, y = places()
    me = z * 4 + y
    heads, rows = q.shape[0], q.shape[1]
    width = heads * DH
    crows = rows // RATE
    b0 = sc[0]
    lead = sc[2]
    c2 = math.log2(math.e) / math.sqrt(DH)
    share = rs.shape[2]

    def peer(d):
        return lax.rem(seg + d, 8)

    def share_of(i):
        return pl.ds(pl.multiple_of(i * share, share), share)

    def scatter(d):
        return remote(grads.at[:, share_of(peer(d)), :], rs.at[seg], rsend.at[d], rrecv.at[seg], on(seg=peer(d)))

    def scattered(d):
        return remote(grads.at[:, share_of(seg), :], rs.at[peer(d)], rsend.at[d], rrecv.at[peer(d)], on(seg=peer(d)))

    def gather(d):
        return remote(red, ag.at[seg], asend.at[d], arecv.at[seg], on(seg=peer(d)))

    def gathered(d):
        return remote(red, ag.at[peer(d)], asend.at[d], arecv.at[peer(d)], on(seg=peer(d)))

    def tell(d):
        return remote(loss, lseg.at[seg], lsend.at[d], lrecv.at[seg], on(seg=peer(d)))

    def told(d):
        return remote(loss, lseg.at[peer(d)], lsend.at[d], lrecv.at[peer(d)], on(seg=peer(d)))

    def spread(d):
        return remote(lsum, lseq.at[me], tsend.at[d], trecv.at[me], on(seq=hop(z, y, d)))

    def spreaded(d):
        src = back(z, y, d)
        return remote(lsum, lseq.at[src], tsend.at[d], trecv.at[src], on(seq=src))

    def cols_of(i):
        return pl.ds(pl.multiple_of(i * width, width), width)

    def rows_of(i):
        return pl.ds(pl.multiple_of(i * 128, 128), 128)

    def give(b):
        return remote(obuf.at[rows_of(b), :], out.at[:, cols_of(me)], osend.at[b], orecv.at[me], on(seq=b))

    def given(b):
        return remote(obuf.at[rows_of(me), :], out.at[:, cols_of(b)], osend.at[b], orecv.at[b], on(seq=b))

    keep = pltpu.make_async_copy(obuf.at[rows_of(me), :], out.at[:, cols_of(me)], own.at[0])

    def span(lo, hi, f):
        def body(d, carry):
            f(d)
            return carry
        lax.fori_loop(lo, hi, body, 0)

    meet(seg, z, y)
    span(1, 8, lambda d: scatter(d).start())
    span(1, 8, lambda d: tell(d).start())

    def attend_block(i):
        lo, hi = i * BQ, (i + 1) * BQ
        for h in range(heads):
            cols = slice(h * DH, (h + 1) * DH)
            qb = q[h, lo:hi, :]
            place = lax.broadcasted_iota(jnp.int32, (BQ, 1), 0) + lo
            before = place < b0
            first = jnp.where(before, 0, b0)
            s = mm(qb, k[h, 0:hi, :], NT)
            at = lax.broadcasted_iota(jnp.int32, (BQ, hi), 1)
            s = jnp.where(at >= first, s, NEG)
            tail = s[:, lo:hi]
            tri = (lax.broadcasted_iota(jnp.int32, (BQ, BQ), 1)
                   <= lax.broadcasted_iota(jnp.int32, (BQ, BQ), 0))
            tail = jnp.where(tri, tail, NEG)
            if i:
                s = jnp.concatenate((s[:, :lo], tail), axis=1)
            else:
                s = tail
            sm = mm(qb, mk[:, cols], NT)
            jm = lax.broadcasted_iota(jnp.int32, (BQ, crows), 1)
            sm = jnp.where(RATE * jm >= jnp.where(before, lead, RATE * crows), sm, NEG)
            m_f = jnp.where(before, m_b[h, lo:hi, 0:1], NEG)
            top = jnp.maximum(jnp.max(s, axis=1, keepdims=True), jnp.max(sm, axis=1, keepdims=True))
            top = jnp.maximum(top, m_f)
            p = jnp.exp2((s - top) * c2)
            pm = jnp.exp2((sm - top) * c2)
            wf = jnp.exp2((m_f - top) * c2)
            total = (jnp.sum(p, axis=1, keepdims=True) + jnp.sum(pm, axis=1, keepdims=True)
                     + wf * l_b[h, lo:hi, 0:1])
            acc = mm(p.astype(BF16), v[h, 0:hi, :], NN) + mm(pm.astype(BF16), mv[:, cols], NN)
            acc += wf * acc_b[h, lo:hi, :]
            obuf[lo:hi, cols] = (acc / total).astype(BF16)

    count = rows // BQ

    def step(t, carry):
        i = lax.rem(t + 1 + me // 2, count)
        for n in range(count):
            pl.when(i == n)(functools.partial(attend_block, n))
        for b in (2 * i, 2 * i + 1):
            @pl.when(b != me)
            def _():
                give(b).start()

            @pl.when(b == me)
            def _():
                keep.start()

        @pl.when(t == 2)
        def _():
            span(1, 8, lambda d: scattered(d).wait_recv())
            span(1, 8, lambda d: told(d).wait_recv())
            acc = grads[:, share_of(seg), :].astype(F32)
            for d in range(1, 8):
                acc += rs[peer(d)].astype(F32)
            red[...] = acc.astype(BF16)
            lseg[seg] = loss[...]
            tally = lseg[0]
            for d in range(1, 8):
                tally += lseg[d]
            lsum[...] = tally
            gk[:, share_of(seg), :] = red[0:heads].astype(F32)
            gv[:, share_of(seg), :] = red[heads:].astype(F32)

        @pl.when(t == 3)
        def _():
            span(1, 8, lambda d: gather(d).start())
            span(1, 16, lambda d: spread(d).start())
        return carry

    lax.fori_loop(0, count, step, 0)

    def collect(d):
        gathered(d).wait_recv()
        gk[:, share_of(peer(d)), :] = ag[peer(d), 0:heads].astype(F32)
        gv[:, share_of(peer(d)), :] = ag[peer(d), heads:].astype(F32)

    span(1, 8, collect)
    span(1, 16, lambda d: spreaded(d).wait_recv())
    lseq[me] = lsum[...]
    tally = lseq[0]
    for d in range(1, 16):
        tally += lseq[d]
    total_loss[...] = tally / (8 * rows)
    span(1, 8, lambda d: scatter(d).wait_send())
    span(1, 8, lambda d: gather(d).wait_send())
    span(1, 8, lambda d: tell(d).wait_send())
    span(1, 16, lambda d: spread(d).wait_send())

    def finish(d):
        give(hop(z, y, d)).wait_send()
        given(hop(z, y, d)).wait_recv()

    span(1, 16, finish)
    keep.wait()


def exchange_kernel(q_in, k_in, v_in, pk_in, pv_in, q, k, v, fk, fv,
                    bounce, stage, own_sem, out_sem, in_sem, fsend, frecv,
                    psend, precv, rsend, rrecv, lsem):
    seg, z, y = places()
    me = z * 4 + y
    heads = q.shape[0]
    ahead = lax.rem(seg + 1, 8)

    def cols(i, h):
        return pl.ds(pl.multiple_of((i * heads + h) * DH, DH), DH)

    def rows_of(i):
        return pl.ds(pl.multiple_of(i * 128, 128), 128)

    def each(lo, hi, f):
        def body(d, carry):
            f(d)
            return carry
        lax.fori_loop(lo, hi, body, 0)

    ins, outs = (k_in, v_in, q_in), (k, v, q)
    priors, fines = (pk_in, pv_in), (fk, fv)
    tap = pl.ds(pl.multiple_of(seg * 16, 16), 16)
    mine = [[pltpu.make_async_copy(ins[n].at[:, cols(me, h)], bounce.at[n, h], own_sem.at[n, h])
             for h in range(heads)] for n in range(3)]
    mine_p = [[pltpu.make_async_copy(priors[n].at[tap, cols(me, h)], stage.at[n, h, me], own_sem.at[3 + n, h])
               for h in range(heads)] for n in range(2)]
    for c in mine + mine_p:
        for e in c:
            e.start()
    meet(seg, z, y)

    def block(n, h, d):
        there = hop(z, y, d)
        return remote(ins[n].at[:, cols(there, h)], outs[n].at[h, rows_of(me), :],
                      out_sem.at[n, h, d], in_sem.at[n, h, me], on(seq=there))

    def arrival(n, h, d):
        src = back(z, y, d)
        return remote(ins[n].at[:, cols(me, h)], outs[n].at[h, rows_of(src), :],
                      out_sem.at[n, h, d], in_sem.at[n, h, src], on(seq=src))

    def piece(n, h, d):
        there = hop(z, y, d)
        return remote(priors[n].at[tap, cols(there, h)], stage.at[n, h, me],
                      psend.at[n, h, d], precv.at[n, h, me], on(seq=there))

    def piece_in(n, h, d):
        src = back(z, y, d)
        return remote(priors[n].at[tap, cols(me, h)], stage.at[n, h, src],
                      psend.at[n, h, d], precv.at[n, h, src], on(seq=src))

    def forward(n, h, src):
        return remote(outs[n].at[h, rows_of(src), :], fines[n].at[h, rows_of(src), :],
                      fsend.at[n, h, src], frecv.at[n, h, src], on(seg=ahead))

    def strip(n, h, at):
        return fines[n].reshape(heads, 16, 128, DH).at[h, :, at, :]

    def forward_piece(n, h):
        return remote(stage.at[n, h], strip(n, h, tap), rsend.at[n, h], rrecv.at[n, h, seg], on(seg=seg * 0))

    def both(f):
        def body(d):
            for h in range(heads):
                f(h, d)
        return body

    def start_all(n):
        each(1, 16, both(lambda h, d: block(n, h, d).start()))

    start_all(0)
    start_all(1)
    for n in range(2):
        each(1, 16, both(lambda h, d: piece(n, h, d).start()))
    start_all(2)

    local = []
    for n in range(3):
        for h in range(heads):
            mine[n][h].wait()
            local.append(pltpu.make_async_copy(bounce.at[n, h], outs[n].at[h, rows_of(me), :], lsem.at[n, h]))
            local[-1].start()
    for c in local:
        c.wait()

    def pass_on(n):
        @pl.when(seg < 7)
        def _():
            for h in range(heads):
                forward(n, h, me).start()

        def body(h, d):
            arrival(n, h, d).wait_recv()

            @pl.when(seg < 7)
            def _():
                forward(n, h, back(z, y, d)).start()
        each(1, 16, both(body))

    pass_on(0)
    pass_on(1)
    for n in range(2):
        for h in range(heads):
            mine_p[n][h].wait()
        each(1, 16, both(lambda h, d: piece_in(n, h, d).wait_recv()))
        for h in range(heads):
            @pl.when(seg > 0)
            def _():
                forward_piece(n, h).start()

            @pl.when(seg == 0)
            def _():
                pltpu.make_async_copy(stage.at[n, h], strip(n, h, tap), lsem.at[n, h]).start()
    each(1, 16, both(lambda h, d: arrival(2, h, d).wait_recv()))
    for n in range(3):
        each(1, 16, both(lambda h, d: block(n, h, d).wait_send()))
    for n in range(2):
        each(1, 16, both(lambda h, d: piece(n, h, d).wait_send()))

    @pl.when(seg < 7)
    def _():
        for n in range(2):
            each(0, 16, both(lambda h, d: forward(n, h, d).wait_send()))

    @pl.when(seg > 0)
    def _():
        for n in range(2):
            each(0, 16, both(lambda h, d: forward(n, h, d).wait_recv()))
            for h in range(heads):
                forward_piece(n, h).wait_send()

    @pl.when(seg == 0)
    def _():
        for n in range(2):
            for h in range(heads):
                pltpu.make_async_copy(stage.at[n, h], strip(n, h, tap), lsem.at[n, h]).wait()

            def body(h, i):
                at = pl.ds(pl.multiple_of(i * 16, 16), 16)
                remote(stage.at[n, h], strip(n, h, at), rsend.at[n, h], rrecv.at[n, h, i], on(seg=i)).wait_recv()
            each(1, 8, both(body))


def exchange(queries, keys, values, prior_keys, prior_values, seq_count, heads):
    rows = queries.shape[0]
    block = jax.ShapeDtypeStruct((heads, seq_count * rows, DH), BF16)
    dma = pltpu.SemaphoreType.DMA
    return pl.pallas_call(
        exchange_kernel,
        out_shape=(block,) * 5,
        in_specs=[pl.BlockSpec(memory_space=pl.ANY)] * 5,
        out_specs=(pl.BlockSpec(memory_space=pl.ANY),) * 5,
        scratch_shapes=[
            pltpu.VMEM((3, heads, rows, DH), BF16),
            pltpu.VMEM((2, heads, seq_count, 16, DH), BF16),
            dma((5, heads)), dma((3, heads, 16)), dma((3, heads, 16)), dma((2, heads, 16)), dma((2, heads, 16)),
            dma((2, heads, 16)), dma((2, heads, 16)), dma((2, heads)), dma((2, heads, 8)), dma((3, heads)),
        ],
        compiler_params=pltpu.CompilerParams(collective_id=0, has_side_effects=True),
        name="exchange",
    )(queries, keys, values, prior_keys, prior_values)


def pick_entry(small_table, wanted):
    return jnp.sum(jnp.where(jnp.arange(small_table.shape[0]) == wanted, small_table, 0))


def vmem(n):
    return [pl.BlockSpec(memory_space=pltpu.VMEM)] * n


SMEM = pl.BlockSpec(memory_space=pltpu.SMEM)


def on_device(queries, keys, values, prior_keys, prior_values, conv_keys, conv_values, doc_starts):
    seq_count = lax.axis_size(SEQ)
    group = lax.axis_index(SEG)
    rows = queries.shape[0] * seq_count
    heads = conv_keys.shape[0]
    width = heads * DH
    crows = rows // RATE
    q, k, v, fk, fv = exchange(queries, keys, values, prior_keys, prior_values, seq_count, heads)
    b0 = pick_entry(doc_starts, group)
    b1 = jnp.where(group >= 1, pick_entry(doc_starts, group - 1), rows)
    b2 = jnp.where(group >= 2, pick_entry(doc_starts, group - 2), rows)
    s1 = jnp.where(b1 < rows, b1, 0)
    s2 = jnp.where(b2 < rows, b2, 0)
    lead = jnp.where((group >= 1) & (b1 >= rows), s2, rows)
    sc = jnp.stack((b0, s1, lead, lead)).astype(jnp.int32)
    shape = jax.ShapeDtypeStruct
    limit = 60 << 20
    dma = pltpu.SemaphoreType.DMA
    ck, cv, grads, loss, acc_b, m_b, l_b, mk, mv = pl.pallas_call(
        recon_kernel,
        out_shape=(
            shape((crows, width), BF16), shape((crows, width), BF16),
            shape((2 * heads, RATE * DH, DH), BF16),
            shape((8, 128), F32),
            *[shape((heads, rows, DH), F32)] * 3,
            shape((crows, width), BF16), shape((crows, width), BF16),
        ),
        in_specs=[SMEM] + vmem(5),
        out_specs=tuple(vmem(9)),
        scratch_shapes=[
            pltpu.VMEM((heads, RATE, crows, DH), BF16), pltpu.VMEM((heads, RATE, crows, DH), BF16),
            *[pltpu.VMEM((heads, rows, 2 * DH), BF16)] * 3, pltpu.VMEM((heads, crows, 2 * DH), BF16),
            pltpu.VMEM((heads, crows, DH), BF16), pltpu.VMEM((heads, crows, DH), BF16),
            pltpu.VMEM((heads, DH, crows), BF16),
            pltpu.VMEM((2, BQ, rows), F32), pltpu.VMEM((2, 2, BQ, 128), F32),
            pltpu.VMEM((2, crows, BQ), F32), pltpu.VMEM((2, crows, BQ), BF16),
            pltpu.VMEM((2, DH, BQ), F32), pltpu.VMEM((2, 8, BQ), F32),
            pltpu.VMEM((2, BQ, 2 * DH), F32), pltpu.VMEM((2, 2, BQ, 128), F32),
            pltpu.VMEM((heads, crows, DH), F32), pltpu.VMEM((heads, crows, DH), F32),
            pltpu.VMEM((DH, BQ), F32),
            dma((2,)), dma((2,)),
        ],
        compiler_params=pltpu.CompilerParams(
            vmem_limit_bytes=limit, collective_id=1, has_side_effects=True),
        name="recon",
    )(sc, q, fk, fv, conv_keys, conv_values)
    share = RATE * DH // 8
    attended, gk, gv, total = pl.pallas_call(
        attend_kernel,
        out_shape=(
            shape((rows // seq_count, seq_count * width), BF16),
            shape((heads, RATE * DH, DH), F32), shape((heads, RATE * DH, DH), F32),
            shape((8, 128), F32),
        ),
        in_specs=[SMEM] + vmem(10),
        out_specs=(pl.BlockSpec(memory_space=pl.ANY), *vmem(3)),
        scratch_shapes=[
            pltpu.VMEM((rows, width), BF16),
            pltpu.VMEM((8, 2 * heads, share, DH), BF16),
            pltpu.VMEM((8, 2 * heads, share, DH), BF16),
            pltpu.VMEM((2 * heads, share, DH), BF16),
            pltpu.VMEM((8, 8, 128), F32), pltpu.VMEM((16, 8, 128), F32), pltpu.VMEM((8, 128), F32),
            dma((16,)), dma((16,)), dma((8,)), dma((8,)), dma((8,)), dma((8,)),
            dma((8,)), dma((8,)), dma((16,)), dma((16,)), dma((1,)),
        ],
        compiler_params=pltpu.CompilerParams(
            vmem_limit_bytes=limit, collective_id=2, has_side_effects=True),
        name="attend",
    )(sc, q, k, v, mk, mv, acc_b, m_b, l_b, grads, loss)
    return (attended, ck, cv, total[0, 0], gk, gv)


def solution(mesh):
    finer = Mesh(mesh.devices.reshape(4, 2, 4, 4), ("seg_0", "seg_1", "seq_0", "seq_1"))
    return jax.shard_map(
        on_device,
        mesh=finer,
        in_specs=(
            P(SEG_SEQ, None), P(SEG_SEQ, None), P(SEG_SEQ, None),
            P(SEQ, None), P(SEQ, None),
            P(SEQ, None, None), P(SEQ, None, None),
            P(),
        ),
        out_specs=(
            P(SEG_SEQ, None), P(SEG, SEQ), P(SEG, SEQ), P(),
            P(SEQ, None, None), P(SEQ, None, None),
        ),
        check_vma=False,
    )
```

```python
import functools
import math

import jax
import jax.numpy as jnp
from jax import lax
from jax.experimental import pallas as pl
from jax.experimental.pallas import tpu as pltpu
from jax.sharding import Mesh
from jax.sharding import PartitionSpec as P

RATE = 4
SEQ = ("seq_0", "seq_1")
SEG = ("seg_0", "seg_1")
SEG_SEQ = ("seg_0", "seg_1", "seq_0", "seq_1")
NEG = -1e30
MESH = pl.DeviceIdType.MESH
F32 = jnp.float32
BF16 = jnp.bfloat16
BQ = 256
DH = 128
CHUNK = 512
NT = (((1,), (1,)), ((), ()))
NN = (((1,), (0,)), ((), ()))
TN = (((0,), (0,)), ((), ()))


def mm(a, b, dims):
    return lax.dot_general(a, b, dims, preferred_element_type=F32)


def on(seg=None, seq=None):
    target = {}
    if seg is not None:
        target["seg_0"] = seg // 2
        target["seg_1"] = lax.rem(seg, 2)
    if seq is not None:
        target["seq_0"] = seq // 4
        target["seq_1"] = lax.rem(seq, 4)
    return target


def hop(z, y, d):
    return lax.rem(z + d // 4, 4) * 4 + lax.rem(y + lax.rem(d, 4), 4)


def back(z, y, d):
    return lax.rem(z + 4 - d // 4, 4) * 4 + lax.rem(y + 4 - lax.rem(d, 4), 4)


def remote(src, dst, send, recv, target):
    return pltpu.make_async_remote_copy(
        src_ref=src, dst_ref=dst, send_sem=send, recv_sem=recv,
        device_id=target, device_id_type=MESH)


def span(lo, hi, f):
    def body(d, carry):
        f(d)
        return carry
    lax.fori_loop(lo, hi, body, 0)


def fold(x, op):
    out = x[:, 0:128]
    for j in range(1, x.shape[1] // 128):
        out = op(out, x[:, j * 128:(j + 1) * 128])
    return out


def layer_kernel(
        starts, q_in, k_in, v_in, pk_in, pv_in, wk, wv,
        out, ck, cv, gk, gv, total_loss,
        q, k, v, fk, fv, stage, mk, mv,
        wink, winv, vab, fk2, q2, k2, ck2, mk2, ckh, cvh, cvt,
        sbuf, tops, ptf, ptbuf, rcb, lcb, ubuf, sums, vg, kg, lacc,
        acc_b, m_b, l_b, obuf, grads, rs, ag, red, loss, lseg, lseq, lsum,
        own_sem, out_sem, in_sem, fsend, frecv, psend, precv, rsend, rrecv, psem,
        msend, mrecv, gsend, grecv, asend, arecv, lsend, lrecv, tsend, trecv,
        osend, orecv, keep_sem):
    seg = lax.axis_index("seg_0") * 2 + lax.axis_index("seg_1")
    z = lax.axis_index("seq_0")
    y = lax.axis_index("seq_1")
    me = z * 4 + y
    heads, rows = q.shape[0], q.shape[1]
    crows = rows // RATE
    share = RATE * DH // 8
    ahead = lax.rem(seg + 1, 8)
    scale = 1.0 / math.sqrt(DH)
    c2 = scale * math.log2(math.e)

    b0 = starts[seg]
    b1 = jnp.where(seg >= 1, starts[jnp.maximum(seg - 1, 0)], rows)
    b2 = jnp.where(seg >= 2, starts[jnp.maximum(seg - 2, 0)], rows)
    s1 = jnp.where(b1 < rows, b1, 0)
    s2 = jnp.where(b2 < rows, b2, 0)
    lead = jnp.where((seg >= 1) & (b1 >= rows), s2, rows)

    ins, outs = (k_in, v_in, q_in), (k, v, q)
    priors, fines = (pk_in, pv_in), (fk, fv)
    tap = pl.ds(pl.multiple_of(seg * 16, 16), 16)

    def cols(i, h):
        return pl.ds(pl.multiple_of((i * heads + h) * DH, DH), DH)

    def rows_of(i):
        return pl.ds(pl.multiple_of(i * 128, 128), 128)

    def peer(d):
        return lax.rem(seg + d, 8)

    def mine(n, h):
        return pltpu.make_async_copy(ins[n].at[:, cols(me, h)], outs[n].at[h, rows_of(me), :], own_sem.at[n, h])

    def mine_p(n, h):
        return pltpu.make_async_copy(priors[n].at[tap, cols(me, h)], stage.at[n, h, me], own_sem.at[3 + n, h])

    def block(n, h, d):
        there = hop(z, y, d)
        return remote(ins[n].at[:, cols(there, h)], outs[n].at[h, rows_of(me), :],
                      out_sem.at[n, h, d], in_sem.at[n, h, me], on(seq=there))

    def arrival(n, h, d):
        src = back(z, y, d)
        return remote(ins[n].at[:, cols(me, h)], outs[n].at[h, rows_of(src), :],
                      out_sem.at[n, h, d], in_sem.at[n, h, src], on(seq=src))

    def piece(n, h, d):
        there = hop(z, y, d)
        return remote(priors[n].at[tap, cols(there, h)], stage.at[n, h, me],
                      psend.at[n, h, d], precv.at[n, h, me], on(seq=there))

    def piece_in(n, h, d):
        src = back(z, y, d)
        return remote(priors[n].at[tap, cols(me, h)], stage.at[n, h, src],
                      psend.at[n, h, d], precv.at[n, h, src], on(seq=src))

    def forward(n, h, src):
        return remote(outs[n].at[h, rows_of(src), :], fines[n].at[h, rows_of(src), :],
                      fsend.at[n, h, src], frecv.at[n, h, src], on(seg=ahead))

    def strip(n, h, at):
        return fines[n].reshape(heads, 16, 128, DH).at[h, :, at, :]

    def forward_piece(n, h):
        return remote(stage.at[n, h], strip(n, h, tap), rsend.at[n, h], rrecv.at[n, h, seg], on(seg=seg * 0))

    def keep_piece(n, h):
        return pltpu.make_async_copy(stage.at[n, h], strip(n, h, tap), psem.at[n, h])

    def memory(n, h):
        return remote((ckh, cvh)[n].at[h], (mk, mv)[n].at[h], msend.at[n, h], mrecv.at[n, h], on(seg=ahead))

    def share_of(i):
        return pl.ds(pl.multiple_of(i * share, share), share)

    def scatter(h, d):
        return remote(grads.at[h, :, share_of(peer(d)), :], rs.at[h, seg], gsend.at[h, d], grecv.at[h, seg],
                      on(seg=peer(d)))

    def scattered(h, d):
        return remote(grads.at[h, :, share_of(seg), :], rs.at[h, peer(d)], gsend.at[h, d], grecv.at[h, peer(d)],
                      on(seg=peer(d)))

    def gather(h, d):
        return remote(red.at[h], ag.at[h, seg], asend.at[h, d], arecv.at[h, seg], on(seg=peer(d)))

    def gathered(h, d):
        return remote(red.at[h], ag.at[h, peer(d)], asend.at[h, d], arecv.at[h, peer(d)], on(seg=peer(d)))

    def tell(d):
        return remote(loss, lseg.at[seg], lsend.at[d], lrecv.at[seg], on(seg=peer(d)))

    def told(d):
        return remote(loss, lseg.at[peer(d)], lsend.at[d], lrecv.at[peer(d)], on(seg=peer(d)))

    def spread(d):
        return remote(lsum, lseq.at[me], tsend.at[d], trecv.at[me], on(seq=hop(z, y, d)))

    def spreaded(d):
        src = back(z, y, d)
        return remote(lsum, lseq.at[src], tsend.at[d], trecv.at[src], on(seq=src))

    def give(h, b):
        return remote(obuf.at[h, rows_of(b), :], out.at[:, cols(me, h)], osend.at[h, b], orecv.at[h, me], on(seq=b))

    def given(h, b):
        return remote(obuf.at[h, rows_of(me), :], out.at[:, cols(b, h)], osend.at[h, b], orecv.at[h, b], on(seq=b))

    def keep(h):
        return pltpu.make_async_copy(obuf.at[h, rows_of(me), :], out.at[:, cols(me, h)], keep_sem.at[h])

    for h in range(heads):
        for n in range(3):
            mine(n, h).start()
        for n in range(2):
            mine_p(n, h).start()
    barrier = pltpu.get_barrier_semaphore()
    span(1, 16, lambda d: pl.semaphore_signal(barrier, inc=1, device_id=on(seq=hop(z, y, d)), device_id_type=MESH))
    span(1, 8, lambda d: pl.semaphore_signal(barrier, inc=1, device_id=on(seg=peer(d)), device_id_type=MESH))
    pl.semaphore_wait(barrier, 22)

    def start_head(h, carry):
        span(1, 16, lambda d: block(0, h, d).start())
        span(1, 16, lambda d: block(1, h, d).start())
        for n in range(2):
            span(1, 16, lambda d: piece(n, h, d).start())
        span(1, 16, lambda d: block(2, h, d).start())
        return carry

    lax.fori_loop(0, heads, start_head, 0)

    def pass_on(n, h):
        mine(n, h).wait()

        @pl.when(seg < 7)
        def _():
            forward(n, h, me).start()

        def body(d):
            arrival(n, h, d).wait_recv()

            @pl.when(seg < 7)
            def _():
                forward(n, h, back(z, y, d)).start()
        span(1, 16, body)

    def pass_pieces(h):
        for n in range(2):
            mine_p(n, h).wait()
            span(1, 16, lambda d: piece_in(n, h, d).wait_recv())

            @pl.when(seg > 0)
            def _():
                forward_piece(n, h).start()

            @pl.when(seg == 0)
            def _():
                keep_piece(n, h).start()

    pass_on(0, 0)
    pass_on(1, 0)
    pass_pieces(0)

    r_i = lax.broadcasted_iota(jnp.int32, (128, 128), 0)
    c_i = lax.broadcasted_iota(jnp.int32, (128, 128), 1)
    perm = (c_i == RATE * (r_i % 32) + r_i // 32).astype(BF16)
    lacc[...] = jnp.zeros_like(lacc)
    count = rows // BQ
    chunks = rows // CHUNK

    def block_rows(i):
        return pl.ds(pl.multiple_of(i * BQ, BQ), BQ)

    def is_tail(c):
        return lax.broadcasted_iota(jnp.int32, (BQ, CHUNK), 1) >= s1 - c * CHUNK

    def score_chunk(qb, c, state, slot):
        s = mm(qb, fk2[c * CHUNK:(c + 1) * CHUNK, :], NT)
        sbuf[slot, :, c * CHUNK:(c + 1) * CHUNK] = s
        a = fold(s, jnp.maximum)
        b = fold(jnp.where(is_tail(c), s, NEG), jnp.maximum)
        return (a, b) if state is None else (jnp.maximum(state[0], a), jnp.maximum(state[1], b))

    def set_tops(state, slot):
        tops[slot, 0] = jnp.broadcast_to(jnp.max(state[0], axis=1, keepdims=True), (BQ, 128))
        tops[slot, 1] = jnp.broadcast_to(jnp.max(state[1], axis=1, keepdims=True), (BQ, 128))

    def grad_steps(h, t, b):
        at = block_rows(t)
        hold = {}

        def zero():
            la = jnp.sum(sums[b, 0], axis=1, keepdims=True)
            lt = jnp.sum(sums[b, 1], axis=1, keepdims=True)
            u = ubuf[b, :, 0:DH]
            u_tail = ubuf[b, :, DH:]
            m_all, m_tail = tops[b, 0], tops[b, 1]
            w_tail = jnp.exp2(m_tail - m_all)
            hold["fine"] = (u + w_tail * u_tail) / ((la - lt) + w_tail * lt)
            acc_b[at, :] = u_tail
            m_b[at, :] = m_tail
            l_b[at, :] = jnp.broadcast_to(lt, (BQ, DH))

        def one():
            differ = hold["fine"].T - rcb[b]
            lacc[...] += differ * differ
            og = (-2.0 * differ / lcb[b, 0:1, :]).astype(BF16)
            hold["og"] = og
            hold["offset"] = jnp.sum(og.astype(F32) * rcb[b], axis=0, keepdims=True)

        def two():
            hold["inner"] = mm(cvh[h], hold["og"], NN)
            vg[...] += mm(ptbuf[b], hold["og"], NT)

        def three():
            hold["sg"] = (ptf[b] * (hold["inner"] - hold["offset"])).astype(BF16)
            kg[...] += mm(hold["sg"], q[h, at, :], NN)
        return zero, one, two, three

    def comp_steps(qb, b):
        hold = {}

        def zero():
            hold["st"] = mm(ck2[...], qb, NT)
            hold["mc"] = jnp.max(hold["st"], axis=0, keepdims=True)

        def one():
            pt = jnp.exp2(hold["st"] - hold["mc"])
            ptf[b] = pt
            hold["lc"] = jnp.sum(pt, axis=0, keepdims=True)
            ptbuf[b] = pt.astype(BF16)

        def two():
            rcb[b] = mm(cvt[...], ptbuf[b], NN) / hold["lc"]
            lcb[b] = jnp.broadcast_to(hold["lc"], lcb.shape[1:])
        return zero, one, two, lambda: None

    def run(h, t, slot):
        other = 1 - slot
        qb = q2[block_rows(t), :]
        qn = q2[block_rows(jnp.minimum(t + 1, count - 1)), :]
        pieces = grad_steps(h, jnp.maximum(t - 1, 0), other)
        comp = comp_steps(qb, slot)
        wide_all = jnp.concatenate([tops[slot, 0]] * (CHUNK // 128), axis=1)
        wide_tail = jnp.concatenate([tops[slot, 1]] * (CHUNK // 128), axis=1)
        state, u, l_all, l_tail = None, None, None, None
        for c in range(chunks):
            state = score_chunk(qn, c, state, other)
            comp[c]()
            tail = is_tail(c)
            s = sbuf[slot, :, c * CHUNK:(c + 1) * CHUNK]
            p = jnp.exp2(s - jnp.where(tail, wide_tail, wide_all))
            a = fold(p, jnp.add)
            b = fold(jnp.where(tail, p, 0.0), jnp.add)
            part = mm(p.astype(BF16), vab[c * CHUNK:(c + 1) * CHUNK, :], NN)
            if c == 0:
                u, l_all, l_tail = part, a, b
            else:
                u, l_all, l_tail = u + part, l_all + a, l_tail + b
            pieces[c]()
        set_tops(state, other)
        ubuf[slot] = u
        sums[slot, 0] = l_all
        sums[slot, 1] = l_tail

    def attend_pair(h, n):
        parts = []
        for i in (n, count - 1 - n):
            lo, hi = i * BQ, (i + 1) * BQ
            qb = q2[lo:hi, :]
            place = lax.broadcasted_iota(jnp.int32, (BQ, 1), 0) + lo
            before = place < b0
            s = mm(qb, k2[0:hi, :], NT)
            at = lax.broadcasted_iota(jnp.int32, (BQ, hi), 1)
            s = jnp.where(at >= jnp.where(before, 0, b0), s, NEG)
            tri = (lax.broadcasted_iota(jnp.int32, (BQ, BQ), 1)
                   <= lax.broadcasted_iota(jnp.int32, (BQ, BQ), 0))
            tail = jnp.where(tri, s[:, lo:hi], NEG)
            s = jnp.concatenate((s[:, :lo], tail), axis=1) if i else tail
            sm = mm(qb, mk2[...], NT)
            jm = lax.broadcasted_iota(jnp.int32, (BQ, crows), 1)
            sm = jnp.where(RATE * jm >= jnp.where(before, lead, RATE * crows), sm, NEG)
            parts.append((lo, hi, before, s, sm))
        for lo, hi, before, s, sm in parts:
            m_f = jnp.where(before, m_b[lo:hi, 0:1], NEG)
            top = jnp.max(jnp.maximum(fold(s, jnp.maximum), fold(sm, jnp.maximum)), axis=1, keepdims=True)
            top = jnp.maximum(top, m_f)
            p = jnp.exp2(s - top)
            pm = jnp.exp2(sm - top)
            wf = jnp.exp2(m_f - top)
            total = jnp.sum(fold(p, jnp.add) + fold(pm, jnp.add), axis=1, keepdims=True)
            total += wf * l_b[lo:hi, 0:1]
            acc = mm(p.astype(BF16), v[h, 0:hi, :], NN) + mm(pm.astype(BF16), mv[h], NN)
            acc += wf * acc_b[lo:hi, :]
            obuf[h, lo:hi, :] = (acc / total).astype(BF16)

    def one_head(h, carry):
        span(1, 16, lambda d: arrival(2, h, d).wait_recv())
        mine(2, h).wait()

        @pl.when(seg > 0)
        def _():
            for n in range(2):
                span(0, 16, lambda d: forward(n, h, d).wait_recv())

        @pl.when(seg == 0)
        def _():
            for n in range(2):
                keep_piece(n, h).wait()

                def body(i):
                    at = pl.ds(pl.multiple_of(i * 16, 16), 16)
                    remote(stage.at[n, h], strip(n, h, at), rsend.at[n, h], rrecv.at[n, h, i], on(seg=i)).wait_recv()
                span(1, 8, body)

        def window(b):
            at = pl.ds(pl.multiple_of(b * 128, 128), 128)
            to = pl.ds(pl.multiple_of(b * 32, 32), 32)
            head_row = lax.broadcasted_iota(jnp.int32, (128, DH), 0) + b * 128 < s1
            key, val = fk[h, at, :], fv[h, at, :]
            wa = mm(perm, key, NN).astype(BF16)
            wb = mm(perm, val, NN).astype(BF16)
            for r in range(RATE):
                wink[r, to, :] = wa[32 * r:32 * r + 32]
                winv[r, to, :] = wb[32 * r:32 * r + 32]
            zero = jnp.zeros_like(val)
            vab[at, 0:DH] = jnp.where(head_row, val, zero)
            vab[at, DH:] = jnp.where(head_row, zero, val)
            fk2[at, 0:DH] = key
            fk2[at, DH:] = key
            mine_k = k[h, at, :]
            k2[at, 0:DH] = mine_k
            k2[at, DH:] = mine_k
            scaled = q[h, at, :].astype(F32) * c2
            high = scaled.astype(BF16)
            q2[at, 0:DH] = high
            q2[at, DH:] = (scaled - high.astype(F32)).astype(BF16)

        span(0, rows // 128, window)
        lane = pl.ds(pl.multiple_of(h * DH, DH), DH)
        for win, w, o, kept in ((wink, wk, ck, ckh), (winv, wv, cv, cvh)):
            total = mm(win[0], w[h, 0:DH, :], NN)
            for r in range(1, RATE):
                total += mm(win[r], w[h, r * DH:(r + 1) * DH, :], NN)
            total = total.astype(BF16)
            kept[h] = total
            o[:, lane] = total
        ck2[:, 0:DH] = ckh[h]
        ck2[:, DH:] = ckh[h]
        cvt[...] = cvh[h].astype(F32).T.astype(BF16)

        for a in (vg, kg):
            a[...] = jnp.zeros_like(a)
        for a in (ptf, ptbuf, rcb, ubuf, tops):
            a[1] = jnp.zeros(a.shape[1:], a.dtype)
        lcb[1] = jnp.ones(lcb.shape[1:], F32)
        sums[1, 0] = jnp.ones(sums.shape[2:], F32)
        sums[1, 1] = jnp.zeros(sums.shape[2:], F32)

        @pl.when(seg < 7)
        def _():
            for n in range(2):
                memory(n, h).start()

        state = None
        for c in range(chunks):
            state = score_chunk(q2[0:BQ, :], c, state, 0)
        set_tops(state, 0)

        def two(j):
            run(h, 2 * j, 0)
            run(h, 2 * j + 1, 1)

            @pl.when((h == 0) & (j == 0))
            def _():
                pass_on(0, 1)

            @pl.when((h == 0) & (j == 2))
            def _():
                pass_on(1, 1)
                pass_pieces(1)

        span(0, count // 2, two)
        for f in grad_steps(h, count - 1, 1):
            f()

        kgb = (kg[...] * scale).astype(BF16)
        vgb = vg[...].astype(BF16)
        for r in range(RATE):
            part = slice(r * DH, (r + 1) * DH)
            grads[h, 0, part, :] = mm(wink[r], kgb, TN).astype(BF16)
            grads[h, 1, part, :] = mm(winv[r], vgb, TN).astype(BF16)

        @pl.when(seg > 0)
        def _():
            for n in range(2):
                memory(n, h).wait_recv()

        @pl.when(seg == 0)
        def _():
            mk[h] = jnp.zeros(mk.shape[1:], BF16)
            mv[h] = jnp.zeros(mv.shape[1:], BF16)

        mk2[:, 0:DH] = mk[h]
        mk2[:, DH:] = mk[h]
        span(1, 8, lambda d: scatter(h, d).start())

        @pl.when(h == heads - 1)
        def _():
            loss[...] = jnp.full(loss.shape, jnp.sum(lacc[...]), F32)
            lseg[seg] = loss[...]

        pairs = count // 2

        def step(t):
            i = lax.rem(t + 1 + me // 2, pairs)

            @pl.when((h == heads - 1) & (t == 0))
            def _():
                span(1, 8, lambda d: tell(d).start())

            for n in range(pairs):
                pl.when(i == n)(functools.partial(attend_pair, h, n))
            for b in (2 * i, 2 * i + 1, 2 * (count - 1 - i), 2 * (count - 1 - i) + 1):
                @pl.when(b != me)
                def _():
                    give(h, b).start()

                @pl.when(b == me)
                def _():
                    keep(h).start()

            @pl.when(t == pairs - 1 - h)
            def _():
                span(1, 8, lambda d: scattered(h, d).wait_recv())
                acc = grads[h, :, share_of(seg), :].astype(F32)
                for d in range(1, 8):
                    acc += rs[h, peer(d)].astype(F32)
                red[h] = acc.astype(BF16)
                gk[h, share_of(seg), :] = red[h, 0].astype(F32)
                gv[h, share_of(seg), :] = red[h, 1].astype(F32)
                span(1, 8, lambda d: gather(h, d).start())

            @pl.when((h == heads - 1) & (t == pairs - 2))
            def _():
                span(1, 8, lambda d: told(d).wait_recv())
                tally = lseg[0]
                for d in range(1, 8):
                    tally += lseg[d]
                lsum[...] = tally
                lseq[me] = tally
                span(1, 16, lambda d: spread(d).start())

        span(0, pairs, step)
        return carry

    lax.fori_loop(0, heads, one_head, 0)

    def finish(h, carry):
        def collect(d):
            gathered(h, d).wait_recv()
            gk[h, share_of(peer(d)), :] = ag[h, peer(d), 0].astype(F32)
            gv[h, share_of(peer(d)), :] = ag[h, peer(d), 1].astype(F32)

        span(1, 8, collect)
        span(1, 8, lambda d: scatter(h, d).wait_send())
        span(1, 8, lambda d: gather(h, d).wait_send())
        for n in range(3):
            span(1, 16, lambda d: block(n, h, d).wait_send())
        for n in range(2):
            span(1, 16, lambda d: piece(n, h, d).wait_send())

        @pl.when(seg < 7)
        def _():
            for n in range(2):
                span(0, 16, lambda d: forward(n, h, d).wait_send())
                memory(n, h).wait_send()

        @pl.when(seg > 0)
        def _():
            for n in range(2):
                forward_piece(n, h).wait_send()

        def last(d):
            give(h, hop(z, y, d)).wait_send()
            given(h, hop(z, y, d)).wait_recv()

        span(1, 16, last)
        keep(h).wait()
        return carry

    span(1, 16, lambda d: spreaded(d).wait_recv())
    tally = lseq[0]
    for d in range(1, 16):
        tally += lseq[d]
    total_loss[0, 0] = jnp.max(tally) / (8 * rows)
    span(1, 8, lambda d: tell(d).wait_send())
    span(1, 16, lambda d: spread(d).wait_send())
    lax.fori_loop(0, heads, finish, 0)


def on_device(queries, keys, values, prior_keys, prior_values, conv_keys, conv_values, doc_starts):
    seq_count = lax.axis_size(SEQ)
    piece = queries.shape[0]
    rows = piece * seq_count
    heads = conv_keys.shape[0]
    width = heads * DH
    crows = rows // RATE
    share = RATE * DH // 8
    shape = jax.ShapeDtypeStruct
    dma = pltpu.SemaphoreType.DMA
    anyspec = pl.BlockSpec(memory_space=pl.ANY)
    vm = pl.BlockSpec(memory_space=pltpu.VMEM)
    sm = pl.BlockSpec(memory_space=pltpu.SMEM)

    def vmem(*dims, kind=BF16):
        return pltpu.VMEM(dims, kind)

    attended, ck, cv, gk, gv, total = pl.pallas_call(
        layer_kernel,
        out_shape=(
            shape((piece, seq_count * width), BF16),
            shape((crows, width), BF16), shape((crows, width), BF16),
            shape((heads, RATE * DH, DH), F32), shape((heads, RATE * DH, DH), F32),
            shape((1, 1), F32),
        ),
        in_specs=[sm] + [anyspec] * 5 + [vm] * 2,
        out_specs=(anyspec, vm, vm, vm, vm, sm),
        scratch_shapes=[
            *[vmem(heads, rows, DH)] * 5,
            vmem(2, heads, seq_count, 16, DH),
            *[vmem(heads, crows, DH)] * 2,
            *[vmem(RATE, crows, DH)] * 2,
            *[vmem(rows, 2 * DH)] * 4,
            *[vmem(crows, 2 * DH)] * 2,
            *[vmem(heads, crows, DH)] * 2,
            vmem(DH, crows),
            vmem(2, BQ, rows, kind=F32), vmem(2, 2, BQ, 128, kind=F32),
            vmem(2, crows, BQ, kind=F32), vmem(2, crows, BQ),
            vmem(2, DH, BQ, kind=F32), vmem(2, 8, BQ, kind=F32),
            vmem(2, BQ, 2 * DH, kind=F32), vmem(2, 2, BQ, 128, kind=F32),
            vmem(crows, DH, kind=F32), vmem(crows, DH, kind=F32),
            vmem(DH, BQ, kind=F32),
            *[vmem(rows, DH, kind=F32)] * 3,
            vmem(heads, rows, DH),
            vmem(heads, 2, RATE * DH, DH),
            vmem(heads, 8, 2, share, DH), vmem(heads, 8, 2, share, DH),
            vmem(heads, 2, share, DH),
            vmem(8, 128, kind=F32), vmem(8, 8, 128, kind=F32), vmem(16, 8, 128, kind=F32), vmem(8, 128, kind=F32),
            dma((5, heads)), dma((3, heads, 16)), dma((3, heads, 16)),
            dma((2, heads, 16)), dma((2, heads, 16)), dma((2, heads, 16)), dma((2, heads, 16)),
            dma((2, heads)), dma((2, heads, 8)), dma((2, heads)),
            dma((2, heads)), dma((2, heads)),
            dma((heads, 8)), dma((heads, 8)), dma((heads, 8)), dma((heads, 8)),
            dma((8,)), dma((8,)), dma((16,)), dma((16,)),
            dma((heads, 16)), dma((heads, 16)), dma((heads,)),
        ],
        compiler_params=pltpu.CompilerParams(
            vmem_limit_bytes=60 << 20, collective_id=0, has_side_effects=True),
        name="layer",
    )(doc_starts, queries, keys, values, prior_keys, prior_values, conv_keys, conv_values)
    return (attended, ck, cv, total[0, 0], gk, gv)


def solution(mesh):
    finer = Mesh(mesh.devices.reshape(4, 2, 4, 4), ("seg_0", "seg_1", "seq_0", "seq_1"))
    return jax.shard_map(
        on_device,
        mesh=finer,
        in_specs=(
            P(SEG_SEQ, None), P(SEG_SEQ, None), P(SEG_SEQ, None),
            P(SEQ, None), P(SEQ, None),
            P(SEQ, None, None), P(SEQ, None, None),
            P(),
        ),
        out_specs=(
            P(SEG_SEQ, None), P(SEG, SEQ), P(SEG, SEQ), P(),
            P(SEQ, None, None), P(SEQ, None, None),
        ),
        check_vma=False,
    )
```

```python
import functools
import math

import jax
import jax.numpy as jnp
from jax import lax
from jax.experimental import pallas as pl
from jax.experimental.pallas import tpu as pltpu
from jax.sharding import Mesh
from jax.sharding import PartitionSpec as P

RATE = 4
SEQ = ("seq_0", "seq_1")
SEG = ("seg_0", "seg_1")
SEG_SEQ = ("seg_0", "seg_1", "seq_0", "seq_1")
NEG = -1e30
MESH = pl.DeviceIdType.MESH
F32 = jnp.float32
BF16 = jnp.bfloat16
BQ = 256
DH = 128
CHUNK = 512
NT = (((1,), (1,)), ((), ()))
NN = (((1,), (0,)), ((), ()))
TN = (((0,), (0,)), ((), ()))


def mm(a, b, dims):
    return lax.dot_general(a, b, dims, preferred_element_type=F32)


def on(seg=None, seq=None):
    target = {}
    if seg is not None:
        target["seg_0"] = seg // 2
        target["seg_1"] = lax.rem(seg, 2)
    if seq is not None:
        target["seq_0"] = seq // 4
        target["seq_1"] = lax.rem(seq, 4)
    return target


def hop(z, y, d):
    return lax.rem(z + d // 4, 4) * 4 + lax.rem(y + lax.rem(d, 4), 4)


def back(z, y, d):
    return lax.rem(z + 4 - d // 4, 4) * 4 + lax.rem(y + 4 - lax.rem(d, 4), 4)


def remote(src, dst, send, recv, target):
    return pltpu.make_async_remote_copy(
        src_ref=src, dst_ref=dst, send_sem=send, recv_sem=recv,
        device_id=target, device_id_type=MESH)


def done(like, sem):
    pltpu.make_async_copy(like, like, sem).wait()


def span(lo, hi, f):
    def body(d, carry):
        f(d)
        return carry
    lax.fori_loop(lo, hi, body, 0)


def fold(x, op):
    out = x[:, 0:128]
    for j in range(1, x.shape[1] // 128):
        out = op(out, x[:, j * 128:(j + 1) * 128])
    return out


def layer_kernel(
        starts, q_in, k_in, v_in, pk_in, pv_in, wk, wv,
        out, ck, cv, gk, gv, total_loss,
        q, k, v, fk, fv, stage, mk, mv,
        wink, winv, vab, fk2, q2, k2, ck2, mk2, ckh, cvh, cvt,
        sbuf, tops, ptf, ptbuf, rcb, lcb, ubuf, sums, vg, kg, lacc,
        acc_b, m_b, l_b, obuf, grads, rs, ag, red, loss, lseg, lseq, lsum,
        own_sem, out_sem, in_sem, fsend, frecv, psend, precv, rsend, rrecv, psem,
        msend, mrecv, gsend, grecv, asend, arecv, lsend, lrecv, tsend, trecv,
        osend, orecv, keep_sem):
    seg = lax.axis_index("seg_0") * 2 + lax.axis_index("seg_1")
    z = lax.axis_index("seq_0")
    y = lax.axis_index("seq_1")
    me = z * 4 + y
    heads, rows = q.shape[0], q.shape[1]
    crows = rows // RATE
    share = RATE * DH // 8
    ahead = lax.rem(seg + 1, 8)
    scale = 1.0 / math.sqrt(DH)
    c2 = scale * math.log2(math.e)

    b0 = starts[seg]
    b1 = jnp.where(seg >= 1, starts[jnp.maximum(seg - 1, 0)], rows)
    b2 = jnp.where(seg >= 2, starts[jnp.maximum(seg - 2, 0)], rows)
    s1 = jnp.where(b1 < rows, b1, 0)
    s2 = jnp.where(b2 < rows, b2, 0)
    lead = jnp.where((seg >= 1) & (b1 >= rows), s2, rows)

    ins, outs = (k_in, v_in, q_in), (k, v, q)
    priors, fines = (pk_in, pv_in), (fk, fv)
    tap = pl.ds(pl.multiple_of(seg * 16, 16), 16)

    def cols(i, h):
        return pl.ds(pl.multiple_of((i * heads + h) * DH, DH), DH)

    def rows_of(i):
        return pl.ds(pl.multiple_of(i * 128, 128), 128)

    def peer(d):
        return lax.rem(seg + d, 8)

    def mine(n, h):
        return pltpu.make_async_copy(ins[n].at[:, cols(me, h)], outs[n].at[h, rows_of(me), :], own_sem.at[n, h])

    def mine_p(n, h):
        return pltpu.make_async_copy(priors[n].at[tap, cols(me, h)], stage.at[n, h, me], own_sem.at[3 + n, h])

    def block(n, h, d):
        there = hop(z, y, d)
        return remote(ins[n].at[:, cols(there, h)], outs[n].at[h, rows_of(me), :],
                      out_sem.at[n, h], in_sem.at[n, h, d // 4], on(seq=there))

    def four(g):
        return pl.ds(pl.multiple_of(lax.rem(z + 4 - g, 4) * 512, 512), 512)

    def arrived(n, h, g):
        if isinstance(g, int) and g == 0:
            mine(n, h).wait()
            done(outs[n].at[h, pl.ds(0, 384), :], in_sem.at[n, h, 0])
        else:
            done(outs[n].at[h, four(g), :], in_sem.at[n, h, g])

    def piece(n, h, d):
        there = hop(z, y, d)
        return remote(priors[n].at[tap, cols(there, h)], stage.at[n, h, me],
                      psend.at[n, h], precv.at[n, h], on(seq=there))

    def forward(n, h, g):
        return remote(outs[n].at[h, four(g), :], fines[n].at[h, four(g), :],
                      fsend.at[n, h], frecv.at[n, h], on(seg=ahead))

    def strip(n, h, at):
        return fines[n].reshape(heads, 16, 128, DH).at[h, :, at, :]

    def forward_piece(n, h):
        return remote(stage.at[n, h], strip(n, h, tap), rsend.at[n, h], rrecv.at[n, h], on(seg=seg * 0))

    def keep_piece(n, h):
        return pltpu.make_async_copy(stage.at[n, h], strip(n, h, tap), psem.at[n, h])

    def memory(n, h):
        return remote((ckh, cvh)[n].at[h], (mk, mv)[n].at[h], msend.at[n, h], mrecv.at[n, h], on(seg=ahead))

    def share_of(i):
        return pl.ds(pl.multiple_of(i * share, share), share)

    def scatter(h, d):
        return remote(grads.at[h, :, share_of(peer(d)), :], rs.at[h, seg], gsend.at[h], grecv.at[h],
                      on(seg=peer(d)))

    def gather(h, d):
        return remote(red.at[h], ag.at[h, seg], asend.at[h], arecv.at[h], on(seg=peer(d)))

    def tell(d):
        return remote(loss, lseg.at[seg], lsend.at[0], lrecv.at[0], on(seg=peer(d)))

    def spread(d):
        return remote(lsum, lseq.at[me], tsend.at[0], trecv.at[0], on(seq=hop(z, y, d)))

    def give(h, b):
        return remote(obuf.at[h, rows_of(b), :], out.at[:, cols(me, h)], osend.at[h], orecv.at[h], on(seq=b))

    def keep(h):
        return pltpu.make_async_copy(obuf.at[h, rows_of(me), :], out.at[:, cols(me, h)], keep_sem.at[h])

    for h in range(heads):
        for n in range(3):
            mine(n, h).start()
        for n in range(2):
            mine_p(n, h).start()
    barrier = pltpu.get_barrier_semaphore()
    span(1, 16, lambda d: pl.semaphore_signal(barrier, inc=1, device_id=on(seq=hop(z, y, d)), device_id_type=MESH))
    span(1, 8, lambda d: pl.semaphore_signal(barrier, inc=1, device_id=on(seg=peer(d)), device_id_type=MESH))
    pl.semaphore_wait(barrier, 22)

    def start_head(h, carry):
        def pieces():
            for n in range(2):
                span(1, 16, lambda d: piece(n, h, d).start())

        pl.when(h == 0)(pieces)
        span(1, 16, lambda d: block(0, h, d).start())
        span(1, 16, lambda d: block(1, h, d).start())
        pl.when(h > 0)(pieces)
        span(1, 16, lambda d: block(2, h, d).start())
        return carry

    lax.fori_loop(0, heads, start_head, 0)

    def pass_on(n, h, groups=(0, 1, 2, 3)):
        for g in groups:
            arrived(n, h, g)

            @pl.when(seg < 7)
            def _():
                forward(n, h, g).start()

    def pass_pieces(h):
        for n in range(2):
            mine_p(n, h).wait()
            done(stage.at[n, h, pl.ds(0, 15)], precv.at[n, h])

            @pl.when(seg > 0)
            def _():
                forward_piece(n, h).start()

            @pl.when(seg == 0)
            def _():
                keep_piece(n, h).start()

    pass_pieces(0)
    pass_on(0, 0)
    pass_on(1, 0)

    r_i = lax.broadcasted_iota(jnp.int32, (128, 128), 0)
    c_i = lax.broadcasted_iota(jnp.int32, (128, 128), 1)
    perm = (c_i == RATE * (r_i % 32) + r_i // 32).astype(BF16)
    lacc[...] = jnp.zeros_like(lacc)
    count = rows // BQ
    chunks = rows // CHUNK

    def block_rows(i):
        return pl.ds(pl.multiple_of(i * BQ, BQ), BQ)

    def block_of(t):
        return 2 * lax.rem(z + 4 - t // 2, 4) + lax.rem(t, 2)

    def is_tail(c):
        return lax.broadcasted_iota(jnp.int32, (BQ, CHUNK), 1) >= s1 - c * CHUNK

    def score_chunk(qb, c, state, slot):
        s = mm(qb, fk2[c * CHUNK:(c + 1) * CHUNK, :], NT)
        sbuf[slot, :, c * CHUNK:(c + 1) * CHUNK] = s
        a = fold(s, jnp.maximum)
        b = fold(jnp.where(is_tail(c), s, NEG), jnp.maximum)
        return (a, b) if state is None else (jnp.maximum(state[0], a), jnp.maximum(state[1], b))

    def set_tops(state, slot):
        tops[slot, 0] = jnp.broadcast_to(jnp.max(state[0], axis=1, keepdims=True), (BQ, 128))
        tops[slot, 1] = jnp.broadcast_to(jnp.max(state[1], axis=1, keepdims=True), (BQ, 128))

    def grad_steps(h, t, b):
        at = block_rows(block_of(t))
        hold = {}

        def zero():
            la = jnp.sum(sums[b, 0], axis=1, keepdims=True)
            lt = jnp.sum(sums[b, 1], axis=1, keepdims=True)
            u = ubuf[b, :, 0:DH]
            u_tail = ubuf[b, :, DH:]
            m_all, m_tail = tops[b, 0], tops[b, 1]
            w_tail = jnp.exp2(m_tail - m_all)
            hold["fine"] = (u + w_tail * u_tail) / ((la - lt) + w_tail * lt)
            acc_b[at, :] = u_tail
            m_b[at, :] = m_tail
            l_b[at, :] = jnp.broadcast_to(lt, (BQ, DH))

        def one():
            differ = hold["fine"].T - rcb[b]
            lacc[...] += differ * differ
            og = (-2.0 * differ / lcb[b, 0:1, :]).astype(BF16)
            hold["og"] = og
            hold["offset"] = jnp.sum(og.astype(F32) * rcb[b], axis=0, keepdims=True)

        def two():
            hold["inner"] = mm(cvh[h], hold["og"], NN)
            vg[...] += mm(ptbuf[b], hold["og"], NT)

        def three():
            hold["sg"] = (ptf[b] * (hold["inner"] - hold["offset"])).astype(BF16)
            kg[...] += mm(hold["sg"], q[h, at, :], NN)
        return zero, one, two, three

    def comp_steps(qb, b):
        hold = {}

        def zero():
            hold["st"] = mm(ck2[...], qb, NT)
            hold["mc"] = jnp.max(hold["st"], axis=0, keepdims=True)

        def one():
            pt = jnp.exp2(hold["st"] - hold["mc"])
            ptf[b] = pt
            hold["lc"] = jnp.sum(pt, axis=0, keepdims=True)
            ptbuf[b] = pt.astype(BF16)

        def two():
            rcb[b] = mm(cvt[...], ptbuf[b], NN) / hold["lc"]
            lcb[b] = jnp.broadcast_to(hold["lc"], lcb.shape[1:])
        return zero, one, two, lambda: None

    def run(h, t, slot):
        other = 1 - slot
        qb = q2[block_rows(block_of(t)), :]
        qn = q2[block_rows(block_of(jnp.minimum(t + 1, count - 1))), :]
        pieces = grad_steps(h, jnp.maximum(t - 1, 0), other)
        comp = comp_steps(qb, slot)
        wide_all = jnp.concatenate([tops[slot, 0]] * (CHUNK // 128), axis=1)
        wide_tail = jnp.concatenate([tops[slot, 1]] * (CHUNK // 128), axis=1)
        state, u, l_all, l_tail = None, None, None, None
        for c in range(chunks):
            state = score_chunk(qn, c, state, other)
            comp[c]()
            tail = is_tail(c)
            s = sbuf[slot, :, c * CHUNK:(c + 1) * CHUNK]
            p = jnp.exp2(s - jnp.where(tail, wide_tail, wide_all))
            a = fold(p, jnp.add)
            b = fold(jnp.where(tail, p, 0.0), jnp.add)
            part = mm(p.astype(BF16), vab[c * CHUNK:(c + 1) * CHUNK, :], NN)
            if c == 0:
                u, l_all, l_tail = part, a, b
            else:
                u, l_all, l_tail = u + part, l_all + a, l_tail + b
            pieces[c]()
        set_tops(state, other)
        ubuf[slot] = u
        sums[slot, 0] = l_all
        sums[slot, 1] = l_tail

    def attend_pair(h, n):
        parts = []
        for i in (n, count - 1 - n):
            lo, hi = i * BQ, (i + 1) * BQ
            qb = q2[lo:hi, :]
            place = lax.broadcasted_iota(jnp.int32, (BQ, 1), 0) + lo
            before = place < b0
            s = mm(qb, k2[0:hi, :], NT)
            at = lax.broadcasted_iota(jnp.int32, (BQ, hi), 1)
            s = jnp.where(at >= jnp.where(before, 0, b0), s, NEG)
            tri = (lax.broadcasted_iota(jnp.int32, (BQ, BQ), 1)
                   <= lax.broadcasted_iota(jnp.int32, (BQ, BQ), 0))
            tail = jnp.where(tri, s[:, lo:hi], NEG)
            s = jnp.concatenate((s[:, :lo], tail), axis=1) if i else tail
            sm = mm(qb, mk2[...], NT)
            jm = lax.broadcasted_iota(jnp.int32, (BQ, crows), 1)
            sm = jnp.where(RATE * jm >= jnp.where(before, lead, RATE * crows), sm, NEG)
            parts.append((lo, hi, before, s, sm))
        for lo, hi, before, s, sm in parts:
            m_f = jnp.where(before, m_b[lo:hi, 0:1], NEG)
            top = jnp.max(jnp.maximum(fold(s, jnp.maximum), fold(sm, jnp.maximum)), axis=1, keepdims=True)
            top = jnp.maximum(top, m_f)
            p = jnp.exp2(s - top)
            pm = jnp.exp2(sm - top)
            wf = jnp.exp2(m_f - top)
            total = jnp.sum(fold(p, jnp.add) + fold(pm, jnp.add), axis=1, keepdims=True)
            total += wf * l_b[lo:hi, 0:1]
            acc = mm(p.astype(BF16), v[h, 0:hi, :], NN) + mm(pm.astype(BF16), mv[h], NN)
            acc += wf * acc_b[lo:hi, :]
            obuf[h, lo:hi, :] = (acc / total).astype(BF16)

    def one_head(h, carry):
        @pl.when(seg > 0)
        def _():
            for n in range(2):
                done(fines[n].at[h], frecv.at[n, h])

        @pl.when(seg == 0)
        def _():
            for n in range(2):
                keep_piece(n, h).wait()

                done(strip(n, h, pl.ds(0, 112)), rrecv.at[n, h])

        def window(b):
            at = pl.ds(pl.multiple_of(b * 128, 128), 128)
            to = pl.ds(pl.multiple_of(b * 32, 32), 32)
            head_row = lax.broadcasted_iota(jnp.int32, (128, DH), 0) + b * 128 < s1
            key, val = fk[h, at, :], fv[h, at, :]
            wa = mm(perm, key, NN).astype(BF16)
            wb = mm(perm, val, NN).astype(BF16)
            for r in range(RATE):
                wink[r, to, :] = wa[32 * r:32 * r + 32]
                winv[r, to, :] = wb[32 * r:32 * r + 32]
            zero = jnp.zeros_like(val)
            vab[at, 0:DH] = jnp.where(head_row, val, zero)
            vab[at, DH:] = jnp.where(head_row, zero, val)
            fk2[at, 0:DH] = key
            fk2[at, DH:] = key
            mine_k = k[h, at, :]
            k2[at, 0:DH] = mine_k
            k2[at, DH:] = mine_k

        def query_group(j):
            first = lax.rem(z + 4 - j, 4)

            arrived(2, h, j)
            for r in range(4):
                at = rows_of(4 * first + r)
                scaled = q[h, at, :].astype(F32) * c2
                high = scaled.astype(BF16)
                q2[at, 0:DH] = high
                q2[at, DH:] = (scaled - high.astype(F32)).astype(BF16)

        span(0, rows // 128, window)
        lane = pl.ds(pl.multiple_of(h * DH, DH), DH)
        for win, w, o, kept in ((wink, wk, ck, ckh), (winv, wv, cv, cvh)):
            total = mm(win[0], w[h, 0:DH, :], NN)
            for r in range(1, RATE):
                total += mm(win[r], w[h, r * DH:(r + 1) * DH, :], NN)
            total = total.astype(BF16)
            kept[h] = total
            o[:, lane] = total
        ck2[:, 0:DH] = ckh[h]
        ck2[:, DH:] = ckh[h]
        cvt[...] = cvh[h].astype(F32).T.astype(BF16)

        for a in (vg, kg):
            a[...] = jnp.zeros_like(a)
        for a in (ptf, ptbuf, rcb, ubuf, tops):
            a[1] = jnp.zeros(a.shape[1:], a.dtype)
        lcb[1] = jnp.ones(lcb.shape[1:], F32)
        sums[1, 0] = jnp.ones(sums.shape[2:], F32)
        sums[1, 1] = jnp.zeros(sums.shape[2:], F32)

        @pl.when(seg < 7)
        def _():
            for n in range(2):
                memory(n, h).start()

        query_group(0)
        state = None
        for c in range(chunks):
            state = score_chunk(q2[block_rows(block_of(0)), :], c, state, 0)
        set_tops(state, 0)

        def two(j):
            @pl.when(j < count // 2 - 1)
            def _():
                query_group(j + 1)

            run(h, 2 * j, 0)
            run(h, 2 * j + 1, 1)

            @pl.when((h == 0) & (j == 2))
            def _():
                pass_on(0, 1, (0, 1))

            @pl.when((h == 0) & (j == 3))
            def _():
                pass_on(0, 1, (2, 3))

        span(0, count // 2, two)
        for f in grad_steps(h, count - 1, 1):
            f()

        kgb = (kg[...] * scale).astype(BF16)
        vgb = vg[...].astype(BF16)
        for r in range(RATE):
            part = slice(r * DH, (r + 1) * DH)
            grads[h, 0, part, :] = mm(wink[r], kgb, TN).astype(BF16)
            grads[h, 1, part, :] = mm(winv[r], vgb, TN).astype(BF16)

        @pl.when(seg > 0)
        def _():
            for n in range(2):
                memory(n, h).wait_recv()

        @pl.when(seg == 0)
        def _():
            mk[h] = jnp.zeros(mk.shape[1:], BF16)
            mv[h] = jnp.zeros(mv.shape[1:], BF16)

        mk2[:, 0:DH] = mk[h]
        mk2[:, DH:] = mk[h]
        span(1, 8, lambda d: scatter(h, d).start())

        @pl.when(h == heads - 1)
        def _():
            loss[...] = jnp.full(loss.shape, jnp.sum(lacc[...]), F32)
            lseg[seg] = loss[...]

        pairs = count // 2

        def step(t):
            i = lax.rem(t + 1 + jnp.minimum(me // 2, count - 1 - me // 2), pairs)

            @pl.when((h == heads - 1) & (t == 0))
            def _():
                span(1, 8, lambda d: tell(d).start())

            for n in range(pairs):
                pl.when(i == n)(functools.partial(attend_pair, h, n))
            for b in (2 * i, 2 * i + 1, 2 * (count - 1 - i), 2 * (count - 1 - i) + 1):
                @pl.when(b != me)
                def _():
                    give(h, b).start()

                @pl.when(b == me)
                def _():
                    keep(h).start()

            @pl.when((h == 0) & (t == 0))
            def _():
                pass_on(1, 1, (0, 1))

            @pl.when((h == 0) & (t == 1))
            def _():
                pass_on(1, 1, (2, 3))

            @pl.when((h == 0) & (t == 2))
            def _():
                pass_pieces(1)

            @pl.when(t == pairs - 1 - h)
            def _():
                done(rs.at[h, pl.ds(0, 7)], grecv.at[h])
                acc = grads[h, :, share_of(seg), :].astype(F32)
                for d in range(1, 8):
                    acc += rs[h, peer(d)].astype(F32)
                red[h] = acc.astype(BF16)
                gk[h, share_of(seg), :] = red[h, 0].astype(F32)
                gv[h, share_of(seg), :] = red[h, 1].astype(F32)
                span(1, 8, lambda d: gather(h, d).start())

            @pl.when((h == heads - 1) & (t == pairs - 2))
            def _():
                done(lseg.at[pl.ds(0, 7)], lrecv.at[0])
                tally = lseg[0]
                for d in range(1, 8):
                    tally += lseg[d]
                lsum[...] = tally
                lseq[me] = tally
                span(1, 16, lambda d: spread(d).start())

        span(0, pairs, step)
        return carry

    lax.fori_loop(0, heads, one_head, 0)

    def finish(h, carry):
        done(ag.at[h, pl.ds(0, 7)], arecv.at[h])

        def collect(d):
            gk[h, share_of(peer(d)), :] = ag[h, peer(d), 0].astype(F32)
            gv[h, share_of(peer(d)), :] = ag[h, peer(d), 1].astype(F32)

        span(1, 8, collect)
        done(rs.at[h, pl.ds(0, 7)], gsend.at[h])
        done(ag.at[h, pl.ds(0, 7)], asend.at[h])
        for n in range(3):
            done(outs[n].at[h, pl.ds(0, 1920), :], out_sem.at[n, h])
        for n in range(2):
            done(stage.at[n, h, pl.ds(0, 15)], psend.at[n, h])

        @pl.when(seg < 7)
        def _():
            for n in range(2):
                done(outs[n].at[h], fsend.at[n, h])
                memory(n, h).wait_send()

        @pl.when(seg > 0)
        def _():
            for n in range(2):
                forward_piece(n, h).wait_send()

        done(obuf.at[h, pl.ds(0, 1920), :], osend.at[h])
        done(out.at[:, pl.ds(0, 1920)], orecv.at[h])
        keep(h).wait()
        return carry

    done(lseq.at[pl.ds(0, 15)], trecv.at[0])
    tally = lseq[0]
    for d in range(1, 16):
        tally += lseq[d]
    total_loss[0, 0] = jnp.max(tally) / (8 * rows)
    done(lseg.at[pl.ds(0, 7)], lsend.at[0])
    done(lseq.at[pl.ds(0, 15)], tsend.at[0])
    lax.fori_loop(0, heads, finish, 0)


def on_device(queries, keys, values, prior_keys, prior_values, conv_keys, conv_values, doc_starts):
    seq_count = lax.axis_size(SEQ)
    piece = queries.shape[0]
    rows = piece * seq_count
    heads = conv_keys.shape[0]
    width = heads * DH
    crows = rows // RATE
    share = RATE * DH // 8
    shape = jax.ShapeDtypeStruct
    dma = pltpu.SemaphoreType.DMA
    anyspec = pl.BlockSpec(memory_space=pl.ANY)
    vm = pl.BlockSpec(memory_space=pltpu.VMEM)
    sm = pl.BlockSpec(memory_space=pltpu.SMEM)

    def vmem(*dims, kind=BF16):
        return pltpu.VMEM(dims, kind)

    attended, ck, cv, gk, gv, total = pl.pallas_call(
        layer_kernel,
        out_shape=(
            shape((piece, seq_count * width), BF16),
            shape((crows, width), BF16), shape((crows, width), BF16),
            shape((heads, RATE * DH, DH), F32), shape((heads, RATE * DH, DH), F32),
            shape((1, 1), F32),
        ),
        in_specs=[sm] + [anyspec] * 5 + [vm] * 2,
        out_specs=(anyspec, vm, vm, vm, vm, sm),
        scratch_shapes=[
            *[vmem(heads, rows, DH)] * 5,
            vmem(2, heads, seq_count, 16, DH),
            *[vmem(heads, crows, DH)] * 2,
            *[vmem(RATE, crows, DH)] * 2,
            *[vmem(rows, 2 * DH)] * 4,
            *[vmem(crows, 2 * DH)] * 2,
            *[vmem(heads, crows, DH)] * 2,
            vmem(DH, crows),
            vmem(2, BQ, rows, kind=F32), vmem(2, 2, BQ, 128, kind=F32),
            vmem(2, crows, BQ, kind=F32), vmem(2, crows, BQ),
            vmem(2, DH, BQ, kind=F32), vmem(2, 8, BQ, kind=F32),
            vmem(2, BQ, 2 * DH, kind=F32), vmem(2, 2, BQ, 128, kind=F32),
            vmem(crows, DH, kind=F32), vmem(crows, DH, kind=F32),
            vmem(DH, BQ, kind=F32),
            *[vmem(rows, DH, kind=F32)] * 3,
            vmem(heads, rows, DH),
            vmem(heads, 2, RATE * DH, DH),
            vmem(heads, 8, 2, share, DH), vmem(heads, 8, 2, share, DH),
            vmem(heads, 2, share, DH),
            vmem(8, 128, kind=F32), vmem(8, 8, 128, kind=F32), vmem(16, 8, 128, kind=F32), vmem(8, 128, kind=F32),
            dma((5, heads)), dma((3, heads)), dma((3, heads, 4)),
            dma((2, heads)), dma((2, heads)), dma((2, heads)), dma((2, heads)),
            dma((2, heads)), dma((2, heads)), dma((2, heads)),
            dma((2, heads)), dma((2, heads)),
            dma((heads,)), dma((heads,)), dma((heads,)), dma((heads,)),
            dma((1,)), dma((1,)), dma((1,)), dma((1,)),
            dma((heads,)), dma((heads,)), dma((heads,)),
        ],
        compiler_params=pltpu.CompilerParams(
            vmem_limit_bytes=60 << 20, collective_id=0, has_side_effects=True),
        name="layer",
    )(doc_starts, queries, keys, values, prior_keys, prior_values, conv_keys, conv_values)
    return (attended, ck, cv, total[0, 0], gk, gv)


def solution(mesh):
    finer = Mesh(mesh.devices.reshape(4, 2, 4, 4), ("seg_0", "seg_1", "seq_0", "seq_1"))
    return jax.shard_map(
        on_device,
        mesh=finer,
        in_specs=(
            P(SEG_SEQ, None), P(SEG_SEQ, None), P(SEG_SEQ, None),
            P(SEQ, None), P(SEQ, None),
            P(SEQ, None, None), P(SEQ, None, None),
            P(),
        ),
        out_specs=(
            P(SEG_SEQ, None), P(SEG, SEQ), P(SEG, SEQ), P(),
            P(SEQ, None, None), P(SEQ, None, None),
        ),
        check_vma=False,
    )
```

```python
import functools
import math

import jax
import jax.numpy as jnp
from jax import lax
from jax.experimental import pallas as pl
from jax.experimental.pallas import tpu as pltpu
from jax.sharding import Mesh
from jax.sharding import PartitionSpec as P

RATE = 4
SEQ = ("seq_0", "seq_1")
SEG = ("seg_0", "seg_1")
SEG_SEQ = ("seg_0", "seg_1", "seq_0", "seq_1")
NEG = -1e30
MESH = pl.DeviceIdType.MESH
F32 = jnp.float32
BF16 = jnp.bfloat16
BQ = 256
DH = 128
CHUNK = 512
NT = (((1,), (1,)), ((), ()))
NN = (((1,), (0,)), ((), ()))
TN = (((0,), (0,)), ((), ()))


def mm(a, b, dims):
    return lax.dot_general(a, b, dims, preferred_element_type=F32)


def on(seg=None, seq=None):
    target = {}
    if seg is not None:
        target["seg_0"] = seg // 2
        target["seg_1"] = lax.rem(seg, 2)
    if seq is not None:
        target["seq_0"] = seq // 4
        target["seq_1"] = lax.rem(seq, 4)
    return target


def hop(z, y, d):
    return lax.rem(z + d // 4, 4) * 4 + lax.rem(y + lax.rem(d, 4), 4)


def back(z, y, d):
    return lax.rem(z + 4 - d // 4, 4) * 4 + lax.rem(y + 4 - lax.rem(d, 4), 4)


def remote(src, dst, send, recv, target):
    return pltpu.make_async_remote_copy(
        src_ref=src, dst_ref=dst, send_sem=send, recv_sem=recv,
        device_id=target, device_id_type=MESH)


def done(like, sem):
    pltpu.make_async_copy(like, like, sem).wait()


def span(lo, hi, f):
    def body(d, carry):
        f(d)
        return carry
    lax.fori_loop(lo, hi, body, 0)


def fold(x, op):
    out = x[:, 0:128]
    for j in range(1, x.shape[1] // 128):
        out = op(out, x[:, j * 128:(j + 1) * 128])
    return out


def layer_kernel(
        starts, q_in, k_in, v_in, pk_in, pv_in, wk, wv,
        out, ck, cv, gk, gv, total_loss,
        q, k, v, fk, fv, stage, mk, mv,
        wink, winv, vab, fk2, q2, k2, ck2, mk2, ckh, cvh, cvt,
        sbuf, tops, ptf, ptbuf, rcb, lcb, ubuf, sums, vg, kg, lacc,
        acc_b, m_b, l_b, obuf, grads, rs, ag, red, loss, lseg, lseq, lsum,
        own_sem, out_sem, in_sem, fsend, frecv, psend, precv, rsend, rrecv, psem,
        msend, mrecv, gsend, grecv, asend, arecv, lsend, lrecv, tsend, trecv,
        osend, orecv, keep_sem):
    seg = lax.axis_index("seg_0") * 2 + lax.axis_index("seg_1")
    z = lax.axis_index("seq_0")
    y = lax.axis_index("seq_1")
    me = z * 4 + y
    heads, rows = q.shape[0], q.shape[1]
    crows = rows // RATE
    share = RATE * DH // 8
    ahead = lax.rem(seg + 1, 8)
    scale = 1.0 / math.sqrt(DH)
    c2 = scale * math.log2(math.e)

    b0 = starts[seg]
    b1 = jnp.where(seg >= 1, starts[jnp.maximum(seg - 1, 0)], rows)
    b2 = jnp.where(seg >= 2, starts[jnp.maximum(seg - 2, 0)], rows)
    s1 = jnp.where(b1 < rows, b1, 0)
    s2 = jnp.where(b2 < rows, b2, 0)
    lead = jnp.where((seg >= 1) & (b1 >= rows), s2, rows)

    ins, outs = (k_in, v_in, q_in), (k, v, q)
    priors, fines = (pk_in, pv_in), (fk, fv)
    tap = pl.ds(pl.multiple_of(seg * 16, 16), 16)

    def cols(i, h):
        return pl.ds(pl.multiple_of((i * heads + h) * DH, DH), DH)

    def rows_of(i):
        return pl.ds(pl.multiple_of(i * 128, 128), 128)

    def peer(d):
        return lax.rem(seg + d, 8)

    def mine(n, h):
        return pltpu.make_async_copy(ins[n].at[:, cols(me, h)], outs[n].at[h, rows_of(me), :], own_sem.at[n, h])

    def mine_p(n, h):
        return pltpu.make_async_copy(priors[n].at[tap, cols(me, h)], stage.at[n, h, me], own_sem.at[3 + n, h])

    def block(n, h, d):
        there = hop(z, y, d)
        return remote(ins[n].at[:, cols(there, h)], outs[n].at[h, rows_of(me), :],
                      out_sem.at[n, h], in_sem.at[n, h, d // 4], on(seq=there))

    def four(g):
        return pl.ds(pl.multiple_of(lax.rem(z + 4 - g, 4) * 512, 512), 512)

    def arrived(n, h, g):
        if isinstance(g, int) and g == 0:
            mine(n, h).wait()
            done(outs[n].at[h, pl.ds(0, 384), :], in_sem.at[n, h, 0])
        else:
            done(outs[n].at[h, four(g), :], in_sem.at[n, h, g])

    def piece(n, h, d):
        there = hop(z, y, d)
        return remote(priors[n].at[tap, cols(there, h)], stage.at[n, h, me],
                      psend.at[n, h], precv.at[n, h], on(seq=there))

    def forward(n, h, g):
        return remote(outs[n].at[h, four(g), :], fines[n].at[h, four(g), :],
                      fsend.at[n, h], frecv.at[n, h], on(seg=ahead))

    def strip(n, h, at):
        return fines[n].reshape(heads, 16, 128, DH).at[h, :, at, :]

    def forward_piece(n, h):
        return remote(stage.at[n, h], strip(n, h, tap), rsend.at[n, h], rrecv.at[n, h], on(seg=seg * 0))

    def keep_piece(n, h):
        return pltpu.make_async_copy(stage.at[n, h], strip(n, h, tap), psem.at[n, h])

    def memory(n, h):
        return remote((ckh, cvh)[n].at[h], (mk, mv)[n].at[h], msend.at[n, h], mrecv.at[n, h], on(seg=ahead))

    def share_of(i):
        return pl.ds(pl.multiple_of(i * share, share), share)

    def scatter(h, d):
        return remote(grads.at[h, :, share_of(peer(d)), :], rs.at[h, seg], gsend.at[h], grecv.at[h],
                      on(seg=peer(d)))

    def gather(h, d):
        return remote(red.at[h], ag.at[h, seg], asend.at[h], arecv.at[h], on(seg=peer(d)))

    def tell(d):
        return remote(loss, lseg.at[seg], lsend.at[0], lrecv.at[0], on(seg=peer(d)))

    def spread(d):
        return remote(lsum, lseq.at[me], tsend.at[0], trecv.at[0], on(seq=hop(z, y, d)))

    def give(h, b):
        return remote(obuf.at[h, rows_of(b), :], out.at[:, cols(me, h)], osend.at[h], orecv.at[h], on(seq=b))

    def keep(h):
        return pltpu.make_async_copy(obuf.at[h, rows_of(me), :], out.at[:, cols(me, h)], keep_sem.at[h])

    for h in range(heads):
        for n in range(3):
            mine(n, h).start()
        for n in range(2):
            mine_p(n, h).start()
    barrier = pltpu.get_barrier_semaphore()
    span(1, 16, lambda d: pl.semaphore_signal(barrier, inc=1, device_id=on(seq=hop(z, y, d)), device_id_type=MESH))
    span(1, 8, lambda d: pl.semaphore_signal(barrier, inc=1, device_id=on(seg=peer(d)), device_id_type=MESH))
    pl.semaphore_wait(barrier, 22)

    def start_head(h, carry):
        def pieces():
            for n in range(2):
                span(1, 16, lambda d: piece(n, h, d).start())

        pl.when(h == 0)(pieces)
        span(1, 16, lambda d: block(0, h, d).start())
        span(1, 16, lambda d: block(1, h, d).start())
        pl.when(h > 0)(pieces)
        span(1, 16, lambda d: block(2, h, d).start())
        return carry

    lax.fori_loop(0, heads, start_head, 0)

    def pass_on(n, h, groups=(0, 1, 2, 3)):
        for g in groups:
            arrived(n, h, g)

            @pl.when(seg < 7)
            def _():
                forward(n, h, g).start()

    def pass_pieces(h):
        for n in range(2):
            mine_p(n, h).wait()
            done(stage.at[n, h, pl.ds(0, 15)], precv.at[n, h])

            @pl.when(seg > 0)
            def _():
                forward_piece(n, h).start()

            @pl.when(seg == 0)
            def _():
                keep_piece(n, h).start()

    pass_pieces(0)
    pass_on(0, 0)
    pass_on(1, 0)

    r_i = lax.broadcasted_iota(jnp.int32, (128, 128), 0)
    c_i = lax.broadcasted_iota(jnp.int32, (128, 128), 1)
    perm = (c_i == RATE * (r_i % 32) + r_i // 32).astype(BF16)
    lacc[...] = jnp.zeros_like(lacc)
    count = rows // BQ
    chunks = rows // CHUNK

    def block_rows(i):
        return pl.ds(pl.multiple_of(i * BQ, BQ), BQ)

    def block_of(t):
        return 2 * lax.rem(z + 4 - t // 2, 4) + lax.rem(t, 2)

    def is_tail(c):
        return lax.broadcasted_iota(jnp.int32, (BQ, CHUNK), 1) >= s1 - c * CHUNK

    def score_chunk(qb, c, state, slot):
        s = mm(qb, fk2[c * CHUNK:(c + 1) * CHUNK, :], NT)
        sbuf[slot, :, c * CHUNK:(c + 1) * CHUNK] = s
        a = fold(s, jnp.maximum)
        b = fold(jnp.where(is_tail(c), s, NEG), jnp.maximum)
        return (a, b) if state is None else (jnp.maximum(state[0], a), jnp.maximum(state[1], b))

    def set_tops(state, slot):
        tops[slot, 0] = jnp.broadcast_to(jnp.max(state[0], axis=1, keepdims=True), (BQ, 128))
        tops[slot, 1] = jnp.broadcast_to(jnp.max(state[1], axis=1, keepdims=True), (BQ, 128))

    def grad_steps(h, t, b):
        at = block_rows(block_of(t))
        hold = {}

        def zero():
            la = jnp.sum(sums[b, 0], axis=1, keepdims=True)
            lt = jnp.sum(sums[b, 1], axis=1, keepdims=True)
            u = ubuf[b, :, 0:DH]
            u_tail = ubuf[b, :, DH:]
            m_all, m_tail = tops[b, 0], tops[b, 1]
            w_tail = jnp.exp2(m_tail - m_all)
            hold["fine"] = (u + w_tail * u_tail) / ((la - lt) + w_tail * lt)
            acc_b[at, :] = u_tail
            m_b[at, :] = m_tail
            l_b[at, :] = jnp.broadcast_to(lt, (BQ, DH))

        def one():
            differ = hold["fine"].T - rcb[b]
            lacc[...] += differ * differ
            og = (-2.0 * differ / lcb[b, 0:1, :]).astype(BF16)
            hold["og"] = og
            hold["offset"] = jnp.sum(og.astype(F32) * rcb[b], axis=0, keepdims=True)

        def two():
            hold["inner"] = mm(cvh[h], hold["og"], NN)
            vg[...] += mm(ptbuf[b], hold["og"], NT)

        def three():
            hold["sg"] = (ptf[b] * (hold["inner"] - hold["offset"])).astype(BF16)
            kg[...] += mm(hold["sg"], q[h, at, :], NN)
        return zero, one, two, three

    def comp_steps(qb, b):
        hold = {}

        def zero():
            hold["st"] = mm(ck2[...], qb, NT)
            hold["mc"] = jnp.max(hold["st"], axis=0, keepdims=True)

        def one():
            pt = jnp.exp2(hold["st"] - hold["mc"])
            ptf[b] = pt
            hold["lc"] = jnp.sum(pt, axis=0, keepdims=True)
            ptbuf[b] = pt.astype(BF16)

        def two():
            rcb[b] = mm(cvt[...], ptbuf[b], NN) / hold["lc"]
            lcb[b] = jnp.broadcast_to(hold["lc"], lcb.shape[1:])
        return zero, one, two, lambda: None

    def run(h, t, slot):
        other = 1 - slot
        qb = q2[block_rows(block_of(t)), :]
        qn = q2[block_rows(block_of(jnp.minimum(t + 1, count - 1))), :]
        pieces = grad_steps(h, jnp.maximum(t - 1, 0), other)
        comp = comp_steps(qb, slot)
        wide_all = jnp.concatenate([tops[slot, 0]] * (CHUNK // 128), axis=1)
        wide_tail = jnp.concatenate([tops[slot, 1]] * (CHUNK // 128), axis=1)
        state, u, l_all, l_tail = None, None, None, None
        for c in range(chunks):
            state = score_chunk(qn, c, state, other)
            comp[c]()
            tail = is_tail(c)
            s = sbuf[slot, :, c * CHUNK:(c + 1) * CHUNK]
            p = jnp.exp2(s - jnp.where(tail, wide_tail, wide_all))
            a = fold(p, jnp.add)
            b = fold(jnp.where(tail, p, 0.0), jnp.add)
            part = mm(p.astype(BF16), vab[c * CHUNK:(c + 1) * CHUNK, :], NN)
            if c == 0:
                u, l_all, l_tail = part, a, b
            else:
                u, l_all, l_tail = u + part, l_all + a, l_tail + b
            pieces[c]()
        set_tops(state, other)
        ubuf[slot] = u
        sums[slot, 0] = l_all
        sums[slot, 1] = l_tail

    def attend_pair(h, n):
        parts = []
        for i in (n, count - 1 - n):
            lo, hi = i * BQ, (i + 1) * BQ
            qb = q2[lo:hi, :]
            place = lax.broadcasted_iota(jnp.int32, (BQ, 1), 0) + lo
            before = place < b0
            s = mm(qb, k2[0:hi, :], NT)
            at = lax.broadcasted_iota(jnp.int32, (BQ, hi), 1)
            s = jnp.where(at >= jnp.where(before, 0, b0), s, NEG)
            tri = (lax.broadcasted_iota(jnp.int32, (BQ, BQ), 1)
                   <= lax.broadcasted_iota(jnp.int32, (BQ, BQ), 0))
            tail = jnp.where(tri, s[:, lo:hi], NEG)
            s = jnp.concatenate((s[:, :lo], tail), axis=1) if i else tail
            sm = mm(qb, mk2[...], NT)
            jm = lax.broadcasted_iota(jnp.int32, (BQ, crows), 1)
            sm = jnp.where(RATE * jm >= jnp.where(before, lead, RATE * crows), sm, NEG)
            parts.append((lo, hi, before, s, sm))
        for lo, hi, before, s, sm in parts:
            m_f = jnp.where(before, m_b[lo:hi, 0:1], NEG)
            top = jnp.max(jnp.maximum(fold(s, jnp.maximum), fold(sm, jnp.maximum)), axis=1, keepdims=True)
            top = jnp.maximum(top, m_f)
            p = jnp.exp2(s - top)
            pm = jnp.exp2(sm - top)
            wf = jnp.exp2(m_f - top)
            total = jnp.sum(fold(p, jnp.add) + fold(pm, jnp.add), axis=1, keepdims=True)
            total += wf * l_b[lo:hi, 0:1]
            acc = mm(p.astype(BF16), v[h, 0:hi, :], NN) + mm(pm.astype(BF16), mv[h], NN)
            acc += wf * acc_b[lo:hi, :]
            obuf[h, lo:hi, :] = (acc / total).astype(BF16)

    def one_head(h, carry):
        k2[:, 0:DH] = k[h]
        k2[:, DH:] = k[h]

        @pl.when(seg > 0)
        def _():
            for n in range(2):
                done(fines[n].at[h], frecv.at[n, h])

        @pl.when(seg == 0)
        def _():
            for n in range(2):
                keep_piece(n, h).wait()

                done(strip(n, h, pl.ds(0, 112)), rrecv.at[n, h])

        def window(b):
            at = pl.ds(pl.multiple_of(b * 128, 128), 128)
            to = pl.ds(pl.multiple_of(b * 32, 32), 32)
            head_row = lax.broadcasted_iota(jnp.int32, (128, DH), 0) + b * 128 < s1
            key, val = fk[h, at, :], fv[h, at, :]
            wa = mm(perm, key, NN).astype(BF16)
            wb = mm(perm, val, NN).astype(BF16)
            for r in range(RATE):
                wink[r, to, :] = wa[32 * r:32 * r + 32]
                winv[r, to, :] = wb[32 * r:32 * r + 32]
            zero = jnp.zeros_like(val)
            vab[at, 0:DH] = jnp.where(head_row, val, zero)
            vab[at, DH:] = jnp.where(head_row, zero, val)
            fk2[at, 0:DH] = key
            fk2[at, DH:] = key

        def query_group(j):
            first = lax.rem(z + 4 - j, 4)

            arrived(2, h, j)
            for r in range(4):
                at = rows_of(4 * first + r)
                scaled = q[h, at, :].astype(F32) * c2
                high = scaled.astype(BF16)
                q2[at, 0:DH] = high
                q2[at, DH:] = (scaled - high.astype(F32)).astype(BF16)

        def windows(b):
            window(2 * b)
            window(2 * b + 1)

        span(0, rows // 256, windows)
        lane = pl.ds(pl.multiple_of(h * DH, DH), DH)
        for win, w, o, kept in ((wink, wk, ck, ckh), (winv, wv, cv, cvh)):
            total = mm(win[0], w[h, 0:DH, :], NN)
            for r in range(1, RATE):
                total += mm(win[r], w[h, r * DH:(r + 1) * DH, :], NN)
            total = total.astype(BF16)
            kept[h] = total
            o[:, lane] = total
        ck2[:, 0:DH] = ckh[h]
        ck2[:, DH:] = ckh[h]
        cvt[...] = cvh[h].astype(F32).T.astype(BF16)

        for a in (vg, kg):
            a[...] = jnp.zeros_like(a)
        for a in (ptf, ptbuf, rcb, ubuf, tops):
            a[1] = jnp.zeros(a.shape[1:], a.dtype)
        lcb[1] = jnp.ones(lcb.shape[1:], F32)
        sums[1, 0] = jnp.ones(sums.shape[2:], F32)
        sums[1, 1] = jnp.zeros(sums.shape[2:], F32)

        @pl.when(seg < 7)
        def _():
            for n in range(2):
                memory(n, h).start()

        query_group(0)
        state = None
        for c in range(chunks):
            state = score_chunk(q2[block_rows(block_of(0)), :], c, state, 0)
        set_tops(state, 0)

        def two(j):
            @pl.when(j < count // 2 - 1)
            def _():
                query_group(j + 1)

            run(h, 2 * j, 0)
            run(h, 2 * j + 1, 1)

            @pl.when((h == 0) & (j == 1))
            def _():
                pass_on(0, 1, (0, 1))

            @pl.when((h == 0) & (j == 2))
            def _():
                pass_on(0, 1, (2, 3))

            @pl.when((h == 0) & (j == 3))
            def _():
                pass_on(1, 1, (0, 1))

        span(0, count // 2, two)
        for f in grad_steps(h, count - 1, 1):
            f()

        kgb = (kg[...] * scale).astype(BF16)
        vgb = vg[...].astype(BF16)
        for r in range(RATE):
            part = slice(r * DH, (r + 1) * DH)
            grads[h, 0, part, :] = mm(wink[r], kgb, TN).astype(BF16)
            grads[h, 1, part, :] = mm(winv[r], vgb, TN).astype(BF16)

        @pl.when(seg > 0)
        def _():
            for n in range(2):
                memory(n, h).wait_recv()

        @pl.when(seg == 0)
        def _():
            mk[h] = jnp.zeros(mk.shape[1:], BF16)
            mv[h] = jnp.zeros(mv.shape[1:], BF16)

        mk2[:, 0:DH] = mk[h]
        mk2[:, DH:] = mk[h]
        span(1, 8, lambda d: scatter(h, d).start())

        @pl.when(h == heads - 1)
        def _():
            loss[...] = jnp.full(loss.shape, jnp.sum(lacc[...]), F32)
            lseg[seg] = loss[...]

        pairs = count // 2

        def step(t):
            i = lax.rem(t + 1 + jnp.minimum(me // 2, count - 1 - me // 2), pairs)

            @pl.when((h == heads - 1) & (t == 0))
            def _():
                span(1, 8, lambda d: tell(d).start())

            for n in range(pairs):
                pl.when(i == n)(functools.partial(attend_pair, h, n))
            for b in (2 * i, 2 * i + 1, 2 * (count - 1 - i), 2 * (count - 1 - i) + 1):
                @pl.when(b != me)
                def _():
                    give(h, b).start()

                @pl.when(b == me)
                def _():
                    keep(h).start()

            @pl.when((h == 0) & (t == 0))
            def _():
                pass_on(1, 1, (2, 3))

            @pl.when((h == 0) & (t == 1))
            def _():
                pass_pieces(1)

            @pl.when(t == pairs - 1 - h)
            def _():
                done(rs.at[h, pl.ds(0, 7)], grecv.at[h])
                acc = grads[h, :, share_of(seg), :].astype(F32)
                for d in range(1, 8):
                    acc += rs[h, peer(d)].astype(F32)
                red[h] = acc.astype(BF16)
                gk[h, share_of(seg), :] = red[h, 0].astype(F32)
                gv[h, share_of(seg), :] = red[h, 1].astype(F32)
                span(1, 8, lambda d: gather(h, d).start())

            @pl.when((h == heads - 1) & (t == pairs - 3))
            def _():
                done(lseg.at[pl.ds(0, 7)], lrecv.at[0])
                tally = lseg[0]
                for d in range(1, 8):
                    tally += lseg[d]
                lsum[...] = tally
                lseq[me] = tally
                span(1, 16, lambda d: spread(d).start())

        span(0, pairs, step)
        return carry

    lax.fori_loop(0, heads, one_head, 0)

    def finish(h, carry):
        done(ag.at[h, pl.ds(0, 7)], arecv.at[h])

        def collect(d):
            gk[h, share_of(peer(d)), :] = ag[h, peer(d), 0].astype(F32)
            gv[h, share_of(peer(d)), :] = ag[h, peer(d), 1].astype(F32)

        span(1, 8, collect)
        done(rs.at[h, pl.ds(0, 7)], gsend.at[h])
        done(ag.at[h, pl.ds(0, 7)], asend.at[h])
        for n in range(3):
            done(outs[n].at[h, pl.ds(0, 1920), :], out_sem.at[n, h])
        for n in range(2):
            done(stage.at[n, h, pl.ds(0, 15)], psend.at[n, h])

        @pl.when(seg < 7)
        def _():
            for n in range(2):
                done(outs[n].at[h], fsend.at[n, h])
                memory(n, h).wait_send()

        @pl.when(seg > 0)
        def _():
            for n in range(2):
                forward_piece(n, h).wait_send()

        done(obuf.at[h, pl.ds(0, 1920), :], osend.at[h])
        done(out.at[:, pl.ds(0, 1920)], orecv.at[h])
        keep(h).wait()
        return carry

    done(lseq.at[pl.ds(0, 15)], trecv.at[0])
    tally = lseq[0]
    for d in range(1, 16):
        tally += lseq[d]
    total_loss[0, 0] = jnp.max(tally) / (8 * rows)
    done(lseg.at[pl.ds(0, 7)], lsend.at[0])
    done(lseq.at[pl.ds(0, 15)], tsend.at[0])
    lax.fori_loop(0, heads, finish, 0)


def hand_out(*refs):
    count = len(refs) // 2
    for a, b in zip(refs[:count], refs[count:]):
        if a.shape == (1, 1):
            b[0, 0] = a[0, 0]
        else:
            b[...] = a[...]


def on_device(queries, keys, values, prior_keys, prior_values, conv_keys, conv_values, doc_starts):
    seq_count = lax.axis_size(SEQ)
    piece = queries.shape[0]
    rows = piece * seq_count
    heads = conv_keys.shape[0]
    width = heads * DH
    crows = rows // RATE
    share = RATE * DH // 8
    shape = jax.ShapeDtypeStruct
    dma = pltpu.SemaphoreType.DMA
    anyspec = pl.BlockSpec(memory_space=pl.ANY)
    vm = pl.BlockSpec(memory_space=pltpu.VMEM)
    sm = pl.BlockSpec(memory_space=pltpu.SMEM)

    def vmem(*dims, kind=BF16):
        return pltpu.VMEM(dims, kind)

    results = pl.pallas_call(
        layer_kernel,
        out_shape=(
            shape((piece, seq_count * width), BF16),
            shape((crows, width), BF16), shape((crows, width), BF16),
            shape((heads, RATE * DH, DH), F32), shape((heads, RATE * DH, DH), F32),
            shape((1, 1), F32),
        ),
        in_specs=[sm] + [anyspec] * 5 + [vm] * 2,
        out_specs=(anyspec, vm, vm, vm, vm, sm),
        scratch_shapes=[
            *[vmem(heads, rows, DH)] * 5,
            vmem(2, heads, seq_count, 16, DH),
            *[vmem(heads, crows, DH)] * 2,
            *[vmem(RATE, crows, DH)] * 2,
            *[vmem(rows, 2 * DH)] * 4,
            *[vmem(crows, 2 * DH)] * 2,
            *[vmem(heads, crows, DH)] * 2,
            vmem(DH, crows),
            vmem(2, BQ, rows, kind=F32), vmem(2, 2, BQ, 128, kind=F32),
            vmem(2, crows, BQ, kind=F32), vmem(2, crows, BQ),
            vmem(2, DH, BQ, kind=F32), vmem(2, 8, BQ, kind=F32),
            vmem(2, BQ, 2 * DH, kind=F32), vmem(2, 2, BQ, 128, kind=F32),
            vmem(crows, DH, kind=F32), vmem(crows, DH, kind=F32),
            vmem(DH, BQ, kind=F32),
            *[vmem(rows, DH, kind=F32)] * 3,
            vmem(heads, rows, DH),
            vmem(heads, 2, RATE * DH, DH),
            vmem(heads, 8, 2, share, DH), vmem(heads, 8, 2, share, DH),
            vmem(heads, 2, share, DH),
            vmem(8, 128, kind=F32), vmem(8, 8, 128, kind=F32), vmem(16, 8, 128, kind=F32), vmem(8, 128, kind=F32),
            dma((5, heads)), dma((3, heads)), dma((3, heads, 4)),
            dma((2, heads)), dma((2, heads)), dma((2, heads)), dma((2, heads)),
            dma((2, heads)), dma((2, heads)), dma((2, heads)),
            dma((2, heads)), dma((2, heads)),
            dma((heads,)), dma((heads,)), dma((heads,)), dma((heads,)),
            dma((1,)), dma((1,)), dma((1,)), dma((1,)),
            dma((heads,)), dma((heads,)), dma((heads,)),
        ],
        compiler_params=pltpu.CompilerParams(
            vmem_limit_bytes=60 << 20, collective_id=0, has_side_effects=True),
        name="layer",
    )(doc_starts, queries, keys, values, prior_keys, prior_values, conv_keys, conv_values)
    attended, ck, cv, gk, gv, total = pl.pallas_call(
        hand_out,
        out_shape=[shape(r.shape, r.dtype) for r in results],
        in_specs=[vm] * 5 + [sm],
        out_specs=[vm] * 5 + [sm],
        compiler_params=pltpu.CompilerParams(vmem_limit_bytes=67043328),
        name="hand_out",
    )(*results)
    return (attended, ck, cv, total[0, 0], gk, gv)


def solution(mesh):
    finer = Mesh(mesh.devices.reshape(4, 2, 4, 4), ("seg_0", "seg_1", "seq_0", "seq_1"))
    return jax.shard_map(
        on_device,
        mesh=finer,
        in_specs=(
            P(SEG_SEQ, None), P(SEG_SEQ, None), P(SEG_SEQ, None),
            P(SEQ, None), P(SEQ, None),
            P(SEQ, None, None), P(SEQ, None, None),
            P(),
        ),
        out_specs=(
            P(SEG_SEQ, None), P(SEG, SEQ), P(SEG, SEQ), P(),
            P(SEQ, None, None), P(SEQ, None, None),
        ),
        check_vma=False,
    )
```

```python
import functools
import math

import jax
import jax.numpy as jnp
from jax import lax
from jax.experimental import pallas as pl
from jax.experimental.pallas import tpu as pltpu
from jax.sharding import Mesh
from jax.sharding import PartitionSpec as P

RATE = 4
SEQ = ("seq_0", "seq_1")
SEG = ("seg_0", "seg_1")
SEG_SEQ = ("seg_0", "seg_1", "seq_0", "seq_1")
NEG = -1e30
MESH = pl.DeviceIdType.MESH
F32 = jnp.float32
BF16 = jnp.bfloat16
BQ = 256
DH = 128
CHUNK = 512
NT = (((1,), (1,)), ((), ()))
NN = (((1,), (0,)), ((), ()))
TN = (((0,), (0,)), ((), ()))


def mm(a, b, dims):
    return lax.dot_general(a, b, dims, preferred_element_type=F32)


def on(seg=None, seq=None):
    target = {}
    if seg is not None:
        target["seg_0"] = seg // 2
        target["seg_1"] = lax.rem(seg, 2)
    if seq is not None:
        target["seq_0"] = seq // 4
        target["seq_1"] = lax.rem(seq, 4)
    return target


def hop(z, y, d):
    return lax.rem(z + d // 4, 4) * 4 + lax.rem(y + lax.rem(d, 4), 4)


def back(z, y, d):
    return lax.rem(z + 4 - d // 4, 4) * 4 + lax.rem(y + 4 - lax.rem(d, 4), 4)


def remote(src, dst, send, recv, target):
    return pltpu.make_async_remote_copy(
        src_ref=src, dst_ref=dst, send_sem=send, recv_sem=recv,
        device_id=target, device_id_type=MESH)


def done(like, sem):
    pltpu.make_async_copy(like, like, sem).wait()


def span(lo, hi, f):
    def body(d, carry):
        f(d)
        return carry
    lax.fori_loop(lo, hi, body, 0)


def fold(x, op):
    out = x[:, 0:128]
    for j in range(1, x.shape[1] // 128):
        out = op(out, x[:, j * 128:(j + 1) * 128])
    return out


def layer_kernel(
        starts, q_in, k_in, v_in, pk_in, pv_in, wk, wv,
        out, ck, cv, gk, gv, total_loss,
        q, k, v, fk, fv, stage, mk, mv,
        wink, winv, vab, fk2, q2, k2, ck2, mk2, ckh, cvh, cvt,
        sbuf, tops, ptf, ptbuf, rcb, lcb, ubuf, sums, vg, kg, lacc,
        acc_b, m_b, l_b, obuf, grads, rs, ag, red, loss, lseg, lseq, lsum,
        own_sem, out_sem, in_sem, fsend, frecv, psend, precv, rsend, rrecv, psem,
        msend, mrecv, gsend, grecv, asend, arecv, lsend, lrecv, tsend, trecv,
        osend, orecv, keep_sem):
    seg = lax.axis_index("seg_0") * 2 + lax.axis_index("seg_1")
    z = lax.axis_index("seq_0")
    y = lax.axis_index("seq_1")
    me = z * 4 + y
    heads, rows = q.shape[0], q.shape[1]
    crows = rows // RATE
    share = RATE * DH // 8
    ahead = lax.rem(seg + 1, 8)
    scale = 1.0 / math.sqrt(DH)
    c2 = scale * math.log2(math.e)

    b0 = starts[seg]
    b1 = jnp.where(seg >= 1, starts[jnp.maximum(seg - 1, 0)], rows)
    b2 = jnp.where(seg >= 2, starts[jnp.maximum(seg - 2, 0)], rows)
    s1 = jnp.where(b1 < rows, b1, 0)
    s2 = jnp.where(b2 < rows, b2, 0)
    lead = jnp.where((seg >= 1) & (b1 >= rows), s2, rows)

    ins, outs = (k_in, v_in, q_in), (k, v, q)
    priors, fines = (pk_in, pv_in), (fk, fv)
    tap = pl.ds(pl.multiple_of(seg * 16, 16), 16)

    def cols(i, h):
        return pl.ds(pl.multiple_of((i * heads + h) * DH, DH), DH)

    def rows_of(i):
        return pl.ds(pl.multiple_of(i * 128, 128), 128)

    def peer(d):
        return lax.rem(seg + d, 8)

    def mine(n, h):
        return pltpu.make_async_copy(ins[n].at[:, cols(me, h)], outs[n].at[h, rows_of(me), :], own_sem.at[n, h])

    def mine_p(n, h):
        return pltpu.make_async_copy(priors[n].at[tap, cols(me, h)], stage.at[n, h, me], own_sem.at[3 + n, h])

    def block(n, h, d):
        there = hop(z, y, d)
        return remote(ins[n].at[:, cols(there, h)], outs[n].at[h, rows_of(me), :],
                      out_sem.at[n, h], in_sem.at[n, h, d // 4], on(seq=there))

    def four(g):
        return pl.ds(pl.multiple_of(lax.rem(z + 4 - g, 4) * 512, 512), 512)

    def arrived(n, h, g):
        if isinstance(g, int) and g == 0:
            mine(n, h).wait()
            done(outs[n].at[h, pl.ds(0, 384), :], in_sem.at[n, h, 0])
        else:
            done(outs[n].at[h, four(g), :], in_sem.at[n, h, g])

    def piece(n, h, d):
        there = hop(z, y, d)
        return remote(priors[n].at[tap, cols(there, h)], stage.at[n, h, me],
                      psend.at[n, h], precv.at[n, h], on(seq=there))

    def forward(n, h, g):
        return remote(outs[n].at[h, four(g), :], fines[n].at[h, four(g), :],
                      fsend.at[n, h], frecv.at[n, h], on(seg=ahead))

    def strip(n, h, at):
        return fines[n].reshape(heads, 16, 128, DH).at[h, :, at, :]

    def forward_piece(n, h):
        return remote(stage.at[n, h], strip(n, h, tap), rsend.at[n, h], rrecv.at[n, h], on(seg=seg * 0))

    def keep_piece(n, h):
        return pltpu.make_async_copy(stage.at[n, h], strip(n, h, tap), psem.at[n, h])

    def memory(n, h):
        return remote((ckh, cvh)[n].at[h], (mk, mv)[n].at[h], msend.at[n, h], mrecv.at[n, h], on(seg=ahead))

    def share_of(i):
        return pl.ds(pl.multiple_of(i * share, share), share)

    def scatter(h, d):
        return remote(grads.at[h, :, share_of(peer(d)), :], rs.at[h, seg], gsend.at[h], grecv.at[h],
                      on(seg=peer(d)))

    def gather(h, d):
        return remote(red.at[h], ag.at[h, seg], asend.at[h], arecv.at[h], on(seg=peer(d)))

    def tell(d):
        return remote(loss, lseg.at[seg], lsend.at[0], lrecv.at[0], on(seg=peer(d)))

    def spread(d):
        return remote(lsum, lseq.at[me], tsend.at[0], trecv.at[0], on(seq=hop(z, y, d)))

    def give(h, b):
        return remote(obuf.at[h, rows_of(b), :], out.at[:, cols(me, h)], osend.at[h], orecv.at[h], on(seq=b))

    def keep(h):
        return pltpu.make_async_copy(obuf.at[h, rows_of(me), :], out.at[:, cols(me, h)], keep_sem.at[h])

    for h in range(heads):
        for n in range(3):
            mine(n, h).start()
        for n in range(2):
            mine_p(n, h).start()
    barrier = pltpu.get_barrier_semaphore()
    span(1, 16, lambda d: pl.semaphore_signal(barrier, inc=1, device_id=on(seq=hop(z, y, d)), device_id_type=MESH))
    span(1, 8, lambda d: pl.semaphore_signal(barrier, inc=1, device_id=on(seg=peer(d)), device_id_type=MESH))
    pl.semaphore_wait(barrier, 22)

    def start_head(h, carry):
        def pieces():
            for n in range(2):
                span(1, 16, lambda d: piece(n, h, d).start())

        pieces()
        span(1, 16, lambda d: block(0, h, d).start())
        span(1, 16, lambda d: block(1, h, d).start())
        span(1, 16, lambda d: block(2, h, d).start())
        return carry

    lax.fori_loop(0, heads, start_head, 0)

    def pass_on(n, h, groups=(0, 1, 2, 3)):
        for g in groups:
            arrived(n, h, g)

            @pl.when(seg < 7)
            def _():
                forward(n, h, g).start()

    def pass_pieces(h):
        for n in range(2):
            mine_p(n, h).wait()
            done(stage.at[n, h, pl.ds(0, 15)], precv.at[n, h])

            @pl.when(seg > 0)
            def _():
                forward_piece(n, h).start()

            @pl.when(seg == 0)
            def _():
                keep_piece(n, h).start()

    pass_pieces(0)
    pass_on(0, 0)
    pass_on(1, 0)

    r_i = lax.broadcasted_iota(jnp.int32, (128, 128), 0)
    c_i = lax.broadcasted_iota(jnp.int32, (128, 128), 1)
    perm = (c_i == RATE * (r_i % 32) + r_i // 32).astype(BF16)
    lacc[...] = jnp.zeros_like(lacc)
    count = rows // BQ
    chunks = rows // CHUNK

    def block_rows(i):
        return pl.ds(pl.multiple_of(i * BQ, BQ), BQ)

    def block_of(t):
        return 2 * lax.rem(z + 4 - t // 2, 4) + lax.rem(t, 2)

    def is_tail(c):
        return lax.broadcasted_iota(jnp.int32, (BQ, CHUNK), 1) >= s1 - c * CHUNK

    def score_chunk(qb, c, state, slot):
        s = mm(qb, fk2[c * CHUNK:(c + 1) * CHUNK, :], NT)
        sbuf[slot, :, c * CHUNK:(c + 1) * CHUNK] = s
        a = fold(s, jnp.maximum)
        b = fold(jnp.where(is_tail(c), s, NEG), jnp.maximum)
        return (a, b) if state is None else (jnp.maximum(state[0], a), jnp.maximum(state[1], b))

    def set_tops(state, slot):
        tops[slot, 0] = jnp.broadcast_to(jnp.max(state[0], axis=1, keepdims=True), (BQ, 128))
        tops[slot, 1] = jnp.broadcast_to(jnp.max(state[1], axis=1, keepdims=True), (BQ, 128))

    def grad_steps(h, t, b):
        at = block_rows(block_of(t))
        hold = {}

        def zero():
            la = jnp.sum(sums[b, 0], axis=1, keepdims=True)
            lt = jnp.sum(sums[b, 1], axis=1, keepdims=True)
            u = ubuf[b, :, 0:DH]
            u_tail = ubuf[b, :, DH:]
            m_all, m_tail = tops[b, 0], tops[b, 1]
            w_tail = jnp.exp2(m_tail - m_all)
            hold["fine"] = (u + w_tail * u_tail) / ((la - lt) + w_tail * lt)
            acc_b[at, :] = u_tail
            m_b[at, :] = m_tail
            l_b[at, :] = jnp.broadcast_to(lt, (BQ, DH))

        def one():
            differ = hold["fine"].T - rcb[b]
            lacc[...] += differ * differ
            og = (-2.0 * differ / lcb[b, 0:1, :]).astype(BF16)
            hold["og"] = og
            hold["offset"] = jnp.sum(og.astype(F32) * rcb[b], axis=0, keepdims=True)

        def two():
            hold["inner"] = mm(cvh[h], hold["og"], NN)
            vg[...] += mm(ptbuf[b], hold["og"], NT)

        def three():
            hold["sg"] = (ptf[b] * (hold["inner"] - hold["offset"])).astype(BF16)
            kg[...] += mm(hold["sg"], q[h, at, :], NN)
        return zero, one, two, three

    def comp_steps(qb, b):
        hold = {}

        def zero():
            hold["st"] = mm(ck2[...], qb, NT)
            hold["mc"] = jnp.max(hold["st"], axis=0, keepdims=True)

        def one():
            pt = jnp.exp2(hold["st"] - hold["mc"])
            ptf[b] = pt
            hold["lc"] = jnp.sum(pt, axis=0, keepdims=True)
            ptbuf[b] = pt.astype(BF16)

        def two():
            rcb[b] = mm(cvt[...], ptbuf[b], NN) / hold["lc"]
            lcb[b] = jnp.broadcast_to(hold["lc"], lcb.shape[1:])
        return zero, one, two, lambda: None

    def run(h, t, slot):
        other = 1 - slot
        qb = q2[block_rows(block_of(t)), :]
        qn = q2[block_rows(block_of(jnp.minimum(t + 1, count - 1))), :]
        pieces = grad_steps(h, jnp.maximum(t - 1, 0), other)
        comp = comp_steps(qb, slot)
        wide_all = jnp.concatenate([tops[slot, 0]] * (CHUNK // 128), axis=1)
        wide_tail = jnp.concatenate([tops[slot, 1]] * (CHUNK // 128), axis=1)
        state, u, l_all, l_tail = None, None, None, None
        for c in range(chunks):
            state = score_chunk(qn, c, state, other)
            comp[c]()
            tail = is_tail(c)
            s = sbuf[slot, :, c * CHUNK:(c + 1) * CHUNK]
            p = jnp.exp2(s - jnp.where(tail, wide_tail, wide_all))
            a = fold(p, jnp.add)
            b = fold(jnp.where(tail, p, 0.0), jnp.add)
            part = mm(p.astype(BF16), vab[c * CHUNK:(c + 1) * CHUNK, :], NN)
            if c == 0:
                u, l_all, l_tail = part, a, b
            else:
                u, l_all, l_tail = u + part, l_all + a, l_tail + b
            pieces[c]()
        set_tops(state, other)
        ubuf[slot] = u
        sums[slot, 0] = l_all
        sums[slot, 1] = l_tail

    def attend_pair(h, n):
        parts = []
        for i in (n, count - 1 - n):
            lo, hi = i * BQ, (i + 1) * BQ
            qb = q2[lo:hi, :]
            place = lax.broadcasted_iota(jnp.int32, (BQ, 1), 0) + lo
            before = place < b0
            s = mm(qb, k2[0:hi, :], NT)
            at = lax.broadcasted_iota(jnp.int32, (BQ, hi), 1)
            s = jnp.where(at >= jnp.where(before, 0, b0), s, NEG)
            tri = (lax.broadcasted_iota(jnp.int32, (BQ, BQ), 1)
                   <= lax.broadcasted_iota(jnp.int32, (BQ, BQ), 0))
            tail = jnp.where(tri, s[:, lo:hi], NEG)
            s = jnp.concatenate((s[:, :lo], tail), axis=1) if i else tail
            sm = mm(qb, mk2[...], NT)
            jm = lax.broadcasted_iota(jnp.int32, (BQ, crows), 1)
            sm = jnp.where(RATE * jm >= jnp.where(before, lead, RATE * crows), sm, NEG)
            parts.append((lo, hi, before, s, sm))
        for lo, hi, before, s, sm in parts:
            m_f = jnp.where(before, m_b[lo:hi, 0:1], NEG)
            top = jnp.max(jnp.maximum(fold(s, jnp.maximum), fold(sm, jnp.maximum)), axis=1, keepdims=True)
            top = jnp.maximum(top, m_f)
            p = jnp.exp2(s - top)
            pm = jnp.exp2(sm - top)
            wf = jnp.exp2(m_f - top)
            total = jnp.sum(fold(p, jnp.add) + fold(pm, jnp.add), axis=1, keepdims=True)
            total += wf * l_b[lo:hi, 0:1]
            acc = mm(p.astype(BF16), v[h, 0:hi, :], NN) + mm(pm.astype(BF16), mv[h], NN)
            acc += wf * acc_b[lo:hi, :]
            obuf[h, lo:hi, :] = (acc / total).astype(BF16)

    def one_head(h, carry):
        k2[:, 0:DH] = k[h]
        k2[:, DH:] = k[h]

        @pl.when(seg > 0)
        def _():
            for n in range(2):
                done(fines[n].at[h], frecv.at[n, h])

        @pl.when(seg == 0)
        def _():
            for n in range(2):
                keep_piece(n, h).wait()

                done(strip(n, h, pl.ds(0, 112)), rrecv.at[n, h])

        def window(b):
            at = pl.ds(pl.multiple_of(b * 128, 128), 128)
            to = pl.ds(pl.multiple_of(b * 32, 32), 32)
            head_row = lax.broadcasted_iota(jnp.int32, (128, DH), 0) + b * 128 < s1
            key, val = fk[h, at, :], fv[h, at, :]
            wa = mm(perm, key, NN).astype(BF16)
            wb = mm(perm, val, NN).astype(BF16)
            for r in range(RATE):
                wink[r, to, :] = wa[32 * r:32 * r + 32]
                winv[r, to, :] = wb[32 * r:32 * r + 32]
            zero = jnp.zeros_like(val)
            vab[at, 0:DH] = jnp.where(head_row, val, zero)
            vab[at, DH:] = jnp.where(head_row, zero, val)
            fk2[at, 0:DH] = key
            fk2[at, DH:] = key

        def query_group(j):
            first = lax.rem(z + 4 - j, 4)

            arrived(2, h, j)
            for r in range(4):
                at = rows_of(4 * first + r)
                scaled = q[h, at, :].astype(F32) * c2
                high = scaled.astype(BF16)
                q2[at, 0:DH] = high
                q2[at, DH:] = (scaled - high.astype(F32)).astype(BF16)

        def windows(b):
            for r in range(4):
                window(4 * b + r)

        span(0, rows // 512, windows)
        lane = pl.ds(pl.multiple_of(h * DH, DH), DH)
        for win, w, o, kept in ((wink, wk, ck, ckh), (winv, wv, cv, cvh)):
            total = mm(win[0], w[h, 0:DH, :], NN)
            for r in range(1, RATE):
                total += mm(win[r], w[h, r * DH:(r + 1) * DH, :], NN)
            total = total.astype(BF16)
            kept[h] = total
            o[:, lane] = total
        ck2[:, 0:DH] = ckh[h]
        ck2[:, DH:] = ckh[h]
        cvt[...] = cvh[h].astype(F32).T.astype(BF16)

        for a in (vg, kg):
            a[...] = jnp.zeros_like(a)
        for a in (ptf, ptbuf, rcb, ubuf, tops):
            a[1] = jnp.zeros(a.shape[1:], a.dtype)
        lcb[1] = jnp.ones(lcb.shape[1:], F32)
        sums[1, 0] = jnp.ones(sums.shape[2:], F32)
        sums[1, 1] = jnp.zeros(sums.shape[2:], F32)

        @pl.when(seg < 7)
        def _():
            for n in range(2):
                memory(n, h).start()

        query_group(0)
        state = None
        for c in range(chunks):
            state = score_chunk(q2[block_rows(block_of(0)), :], c, state, 0)
        set_tops(state, 0)

        def two(j):
            @pl.when(j < count // 2 - 1)
            def _():
                query_group(j + 1)

            run(h, 2 * j, 0)
            run(h, 2 * j + 1, 1)

            @pl.when((h == 0) & (j == 1))
            def _():
                pass_pieces(1)
                pass_on(0, 1, (0, 1))

            @pl.when((h == 0) & (j == 2))
            def _():
                pass_on(0, 1, (2, 3))

            @pl.when((h == 0) & (j == 3))
            def _():
                pass_on(1, 1, (0, 1))

        span(0, count // 2, two)
        for f in grad_steps(h, count - 1, 1):
            f()

        kgb = (kg[...] * scale).astype(BF16)
        vgb = vg[...].astype(BF16)
        for r in range(RATE):
            part = slice(r * DH, (r + 1) * DH)
            grads[h, 0, part, :] = mm(wink[r], kgb, TN).astype(BF16)
            grads[h, 1, part, :] = mm(winv[r], vgb, TN).astype(BF16)

        @pl.when(seg > 0)
        def _():
            for n in range(2):
                memory(n, h).wait_recv()

        @pl.when(seg == 0)
        def _():
            mk[h] = jnp.zeros(mk.shape[1:], BF16)
            mv[h] = jnp.zeros(mv.shape[1:], BF16)

        mk2[:, 0:DH] = mk[h]
        mk2[:, DH:] = mk[h]
        span(1, 8, lambda d: scatter(h, d).start())

        @pl.when(h == heads - 1)
        def _():
            loss[...] = jnp.full(loss.shape, jnp.sum(lacc[...]), F32)
            lseg[seg] = loss[...]

        pairs = count // 2

        def step(t):
            i = lax.rem(t + 1 + jnp.minimum(me // 2, count - 1 - me // 2), pairs)

            @pl.when((h == heads - 1) & (t == 0))
            def _():
                span(1, 8, lambda d: tell(d).start())

            for n in range(pairs):
                pl.when(i == n)(functools.partial(attend_pair, h, n))
            for b in (2 * i, 2 * i + 1, 2 * (count - 1 - i), 2 * (count - 1 - i) + 1):
                @pl.when(b != me)
                def _():
                    give(h, b).start()

                @pl.when(b == me)
                def _():
                    keep(h).start()

            @pl.when((h == 0) & (t == 0))
            def _():
                pass_on(1, 1, (2, 3))

            @pl.when(t == pairs - 1 - h)
            def _():
                done(rs.at[h, pl.ds(0, 7)], grecv.at[h])
                acc = grads[h, :, share_of(seg), :].astype(F32)
                for d in range(1, 8):
                    acc += rs[h, peer(d)].astype(F32)
                red[h] = acc.astype(BF16)
                gk[h, share_of(seg), :] = red[h, 0].astype(F32)
                gv[h, share_of(seg), :] = red[h, 1].astype(F32)
                span(1, 8, lambda d: gather(h, d).start())

            @pl.when((h == heads - 1) & (t == pairs - 3))
            def _():
                done(lseg.at[pl.ds(0, 7)], lrecv.at[0])
                tally = lseg[0]
                for d in range(1, 8):
                    tally += lseg[d]
                lsum[...] = tally
                lseq[me] = tally
                span(1, 16, lambda d: spread(d).start())

        span(0, pairs, step)
        return carry

    lax.fori_loop(0, heads, one_head, 0)

    def finish(h, carry):
        done(ag.at[h, pl.ds(0, 7)], arecv.at[h])

        def collect(d):
            gk[h, share_of(peer(d)), :] = ag[h, peer(d), 0].astype(F32)
            gv[h, share_of(peer(d)), :] = ag[h, peer(d), 1].astype(F32)

        span(1, 8, collect)
        done(rs.at[h, pl.ds(0, 7)], gsend.at[h])
        done(ag.at[h, pl.ds(0, 7)], asend.at[h])
        for n in range(3):
            done(outs[n].at[h, pl.ds(0, 1920), :], out_sem.at[n, h])
        for n in range(2):
            done(stage.at[n, h, pl.ds(0, 15)], psend.at[n, h])

        @pl.when(seg < 7)
        def _():
            for n in range(2):
                done(outs[n].at[h], fsend.at[n, h])
                memory(n, h).wait_send()

        @pl.when(seg > 0)
        def _():
            for n in range(2):
                forward_piece(n, h).wait_send()

        done(obuf.at[h, pl.ds(0, 1920), :], osend.at[h])
        done(out.at[:, pl.ds(0, 1920)], orecv.at[h])
        keep(h).wait()
        return carry

    done(lseq.at[pl.ds(0, 15)], trecv.at[0])
    tally = lseq[0]
    for d in range(1, 16):
        tally += lseq[d]
    total_loss[0, 0] = jnp.max(tally) / (8 * rows)
    done(lseg.at[pl.ds(0, 7)], lsend.at[0])
    done(lseq.at[pl.ds(0, 15)], tsend.at[0])
    lax.fori_loop(0, heads, finish, 0)


def hand_out(*refs):
    count = len(refs) // 2
    for a, b in zip(refs[:count], refs[count:]):
        if a.shape == (1, 1):
            b[0, 0] = a[0, 0]
        else:
            b[...] = a[...]


def on_device(queries, keys, values, prior_keys, prior_values, conv_keys, conv_values, doc_starts):
    seq_count = lax.axis_size(SEQ)
    piece = queries.shape[0]
    rows = piece * seq_count
    heads = conv_keys.shape[0]
    width = heads * DH
    crows = rows // RATE
    share = RATE * DH // 8
    shape = jax.ShapeDtypeStruct
    dma = pltpu.SemaphoreType.DMA
    anyspec = pl.BlockSpec(memory_space=pl.ANY)
    vm = pl.BlockSpec(memory_space=pltpu.VMEM)
    sm = pl.BlockSpec(memory_space=pltpu.SMEM)

    def vmem(*dims, kind=BF16):
        return pltpu.VMEM(dims, kind)

    results = pl.pallas_call(
        layer_kernel,
        out_shape=(
            shape((piece, seq_count * width), BF16),
            shape((crows, width), BF16), shape((crows, width), BF16),
            shape((heads, RATE * DH, DH), F32), shape((heads, RATE * DH, DH), F32),
            shape((1, 1), F32),
        ),
        in_specs=[sm] + [anyspec] * 5 + [vm] * 2,
        out_specs=(anyspec, vm, vm, vm, vm, sm),
        scratch_shapes=[
            *[vmem(heads, rows, DH)] * 5,
            vmem(2, heads, seq_count, 16, DH),
            *[vmem(heads, crows, DH)] * 2,
            *[vmem(RATE, crows, DH)] * 2,
            *[vmem(rows, 2 * DH)] * 4,
            *[vmem(crows, 2 * DH)] * 2,
            *[vmem(heads, crows, DH)] * 2,
            vmem(DH, crows),
            vmem(2, BQ, rows, kind=F32), vmem(2, 2, BQ, 128, kind=F32),
            vmem(2, crows, BQ, kind=F32), vmem(2, crows, BQ),
            vmem(2, DH, BQ, kind=F32), vmem(2, 8, BQ, kind=F32),
            vmem(2, BQ, 2 * DH, kind=F32), vmem(2, 2, BQ, 128, kind=F32),
            vmem(crows, DH, kind=F32), vmem(crows, DH, kind=F32),
            vmem(DH, BQ, kind=F32),
            *[vmem(rows, DH, kind=F32)] * 3,
            vmem(heads, rows, DH),
            vmem(heads, 2, RATE * DH, DH),
            vmem(heads, 8, 2, share, DH), vmem(heads, 8, 2, share, DH),
            vmem(heads, 2, share, DH),
            vmem(8, 128, kind=F32), vmem(8, 8, 128, kind=F32), vmem(16, 8, 128, kind=F32), vmem(8, 128, kind=F32),
            dma((5, heads)), dma((3, heads)), dma((3, heads, 4)),
            dma((2, heads)), dma((2, heads)), dma((2, heads)), dma((2, heads)),
            dma((2, heads)), dma((2, heads)), dma((2, heads)),
            dma((2, heads)), dma((2, heads)),
            dma((heads,)), dma((heads,)), dma((heads,)), dma((heads,)),
            dma((1,)), dma((1,)), dma((1,)), dma((1,)),
            dma((heads,)), dma((heads,)), dma((heads,)),
        ],
        compiler_params=pltpu.CompilerParams(
            vmem_limit_bytes=60 << 20, collective_id=0, has_side_effects=True),
        name="layer",
    )(doc_starts, queries, keys, values, prior_keys, prior_values, conv_keys, conv_values)
    attended, ck, cv, gk, gv, total = pl.pallas_call(
        hand_out,
        out_shape=[shape(r.shape, r.dtype) for r in results],
        in_specs=[vm] * 5 + [sm],
        out_specs=[vm] * 5 + [sm],
        compiler_params=pltpu.CompilerParams(vmem_limit_bytes=67043328),
        name="hand_out",
    )(*results)
    return (attended, ck, cv, total[0, 0], gk, gv)


def solution(mesh):
    finer = Mesh(mesh.devices.reshape(4, 2, 4, 4), ("seg_0", "seg_1", "seq_0", "seq_1"))
    return jax.shard_map(
        on_device,
        mesh=finer,
        in_specs=(
            P(SEG_SEQ, None), P(SEG_SEQ, None), P(SEG_SEQ, None),
            P(SEQ, None), P(SEQ, None),
            P(SEQ, None, None), P(SEQ, None, None),
            P(),
        ),
        out_specs=(
            P(SEG_SEQ, None), P(SEG, SEQ), P(SEG, SEQ), P(),
            P(SEQ, None, None), P(SEQ, None, None),
        ),
        check_vma=False,
    )
```
